128 devices in a mesh: grp: 4 (over z_lo, core), mem: 32 (over z_hi, x, y).
Axes of the slice: x: 4, y: 4, z: 4 (z_hi: 2, z_lo: 2; z = z_hi * 2 + z_lo), core: 2. Of those that a mesh axis runs over, the one named last changes fastest.
Arguments:
- source_pts: float32 [64, 32768], P(None, ('grp', 'mem')), may hold values from -30 to 30
- target_pts: float32 [64, 32768], P(None, ('grp', 'mem')), may hold values from -30 to 30
- source_pot: float32 [32768], P(('grp', 'mem')), may hold values from -8 to 520
- target_pot: float32 [32768], P(('grp', 'mem')), may hold values from -8 to 520
- source_logw: float32 [32768], P(('grp', 'mem')), may hold values from -1 to 4
- target_logw: float32 [32768], P(('grp', 'mem')), may hold values from -1 to 4
Outputs:
- source_new: float32 [32768], P(('grp', 'mem'))
- target_new: float32 [32768], P(('grp', 'mem'))
The draws below stay inside these ranges and needn't reach their ends.
All inputs are finite; a program needn't handle non-finite values.
Results may differ from the reference program's by a relative error of at most 0.0001.
Values sent between devices are 32-bit elements; how exact they have to be, the bound alone decides.
No kernel may reach another device: no remote copies, remote signals or barrier semaphores. Data moves between devices by JAX's collectives and lax.ppermute only.
A program may use at most 64 MiB of HBM per device.

```python
import math
import jax
import jax.numpy as jnp
from jax import lax

FEAT = 64
POINTS = 32768


def cloud_draw(key, salt):
    first = jax.random.fold_in(key, salt)
    base = jnp.clip(jax.random.normal(first, (FEAT, POINTS), jnp.float32), -6.0, 6.0)
    return base


def potential_draw(key, salt):
    first = jax.random.fold_in(key, salt)
    base = jax.random.uniform(first, (POINTS,), jnp.float32, -8.0, 8.0)
    return base


def weight_draw(key, salt):
    first = jax.random.fold_in(key, salt)
    ramp = jnp.arange(POINTS).astype(jnp.float32) / POINTS
    noise = jax.random.uniform(first, (POINTS,), jnp.float32, -1.0, 1.0)
    return noise + jnp.log1p(2.0 * ramp)


def draw_source_pts(key, part):
    return cloud_draw(key, 11)


def draw_target_pts(key, part):
    return cloud_draw(key, 23)


def draw_source_pot(key, part):
    return potential_draw(key, 37)


def draw_target_pot(key, part):
    return potential_draw(key, 41)


def draw_source_logw(key, part):
    return weight_draw(key, 53)


def draw_target_logw(key, part):
    return weight_draw(key, 67)


def setup_inputs(seed: int = 0) -> dict:
    streams_of = jax.random.split(jax.random.key(seed), 7)
    source_pts = draw_source_pts(jax.random.fold_in(streams_of[6], 71), 0)
    target_pts = draw_target_pts(jax.random.fold_in(streams_of[6], 71), 0)
    source_pot = draw_source_pot(jax.random.fold_in(streams_of[6], 71), 0)
    target_pot = draw_target_pot(jax.random.fold_in(streams_of[6], 71), 0)
    source_logw = draw_source_logw(jax.random.fold_in(streams_of[6], 71), 0)
    target_logw = draw_target_logw(jax.random.fold_in(streams_of[6], 71), 0)
    return dict(source_pts=source_pts, target_pts=target_pts, source_pot=source_pot, target_pot=target_pot, source_logw=source_logw, target_logw=target_logw)


epsilon = 4.0
floor_value = -1e30


def log_total(values):
    peak = jnp.max(values)
    return peak + jnp.log(jnp.sum(jnp.exp(values - peak)))


def reference(source_pts, target_pts, source_pot, target_pot, source_logw, target_logw):
    src_log = source_logw - log_total(source_logw)
    tgt_log = target_logw - log_total(target_logw)
    src_sq = 0.5 * jnp.sum(source_pts * source_pts, 0)
    tgt_sq = 0.5 * jnp.sum(target_pts * target_pts, 0)
    row_term = src_log + source_pot / epsilon
    col_term = tgt_log + target_pot / epsilon
    width = math.gcd(POINTS, 512)
    count = POINTS // width
    xs = source_pts.reshape(FEAT, count, width).transpose(1, 0, 2)
    terms = row_term.reshape(count, width)
    squares = src_sq.reshape(count, width)

    def step(carry, item):
        col_max, col_sum = carry
        xblock, rblock, qblock = item
        cross = lax.dot_general(xblock, target_pts, (((0,), (0,)), ((), ())),
                                precision=lax.Precision.HIGHEST, preferred_element_type=jnp.float32)
        half = (qblock[:, None] + tgt_sq[None, :] - cross) / epsilon
        scores = col_term[None, :] - half
        peak = jnp.max(scores, 1)
        row_hat = -epsilon * (peak + jnp.log(jnp.sum(jnp.exp(scores - peak[:, None]), 1)))
        others = rblock[:, None] - half
        bmax = jnp.maximum(col_max, jnp.max(others, 0))
        col_sum = col_sum * jnp.exp(col_max - bmax) + jnp.sum(jnp.exp(others - bmax[None, :]), 0)
        return (bmax, col_sum), row_hat

    init = (jnp.full((POINTS,), floor_value, jnp.float32), jnp.zeros((POINTS,), jnp.float32))
    (col_max, col_sum), row_hat = lax.scan(step, init, (xs, terms, squares))
    col_hat = -epsilon * (col_max + jnp.log(col_sum))
    source_new = 0.5 * (source_pot + row_hat.reshape(POINTS))
    target_new = 0.5 * (target_pot + col_hat)
    return source_new, target_new
```

```python
import functools

import jax
import jax.numpy as jnp
from jax import lax
from jax.experimental import pallas as pl
from jax.experimental.pallas import tpu as pltpu
from jax.sharding import Mesh
from jax.sharding import PartitionSpec as P

epsilon = 4.0
LOG2E = 1.4426950408889634
LN2 = 0.6931471805599453
FEAT = 64
BLK = 256
LOW = 2.0 ** -90
HIGH = 2.0 ** 120
NORMS = 2.0 ** 15


def split(v):
    head = v.astype(jnp.bfloat16).astype(jnp.float32)
    return head, v - head


def bias_rows(bias, first):
    b1, rest = split(bias)
    b2, b3 = split(rest)
    row = lax.broadcasted_iota(jnp.int32, (16, BLK), 0)
    out = jnp.zeros((16, BLK), jnp.float32)
    for k, piece in enumerate((b1, b2, b3)):
        out = jnp.where(row == k + first, piece, out)
    return jnp.where((row >= 3 - first) & (row < 6 - first), 1.0, out)


def tile_kernel(nrow, ncol, M, *refs):
    row_refs = refs[:-9]
    col_ref, rowp, colp, xt, yk, rowacc, colacc, rmax, rsum = refs[-9:]
    views = []
    for r in row_refs:
        if len(r.shape) == 2:
            views.append(r)
        else:
            views.extend(r.at[k] for k in range(r.shape[0]))

    def terms(ref):
        pts = ref[:FEAT, :]
        sq = 0.5 * jnp.sum(pts * pts, 0, keepdims=True)
        return pts, sq, ref[FEAT:FEAT + 1, :]

    row_sq = jnp.zeros((1, BLK), jnp.float32)
    row_mass = jnp.zeros((1, BLK), jnp.float32)
    for k, ref in enumerate(views):
        pts, sq, term = terms(ref)
        row_sq = jnp.maximum(row_sq, sq)
        row_mass += jnp.exp(ref[FEAT + 1:FEAT + 2, :])
        x1, x2 = split(pts * (LOG2E / epsilon))
        bias = bias_rows((term - sq / epsilon) * LOG2E, 0)
        left = jnp.concatenate([x1, x2], 0)
        right = jnp.concatenate([x1, bias, jnp.zeros((48, BLK), jnp.float32)], 0)
        xt[k * BLK:(k + 1) * BLK, :128] = left.T.astype(jnp.bfloat16)
        xt[k * BLK:(k + 1) * BLK, 128:] = right.T.astype(jnp.bfloat16)

    def prep(j, state):
        col_sq, col_mass = state
        ref = col_ref.at[j]
        pts, sq, term = terms(ref)
        y1, y2 = split(pts)
        bias = bias_rows((term - sq / epsilon) * LOG2E, 3)
        at = pl.ds(pl.multiple_of(j * BLK, BLK), BLK)
        y1 = y1.astype(jnp.bfloat16)
        yk[0:64, at] = y1
        yk[64:128, at] = y1
        yk[128:192, at] = y2.astype(jnp.bfloat16)
        yk[192:208, at] = bias.astype(jnp.bfloat16)
        yk[208:256, at] = jnp.zeros((48, BLK), jnp.bfloat16)
        return jnp.maximum(col_sq, sq), col_mass + jnp.exp(ref[FEAT + 1:FEAT + 2, :])

    zero = jnp.zeros((1, BLK), jnp.float32)
    col_sq, col_mass = lax.fori_loop(0, ncol, prep, (zero, zero), unroll=4)
    rowacc[...] = jnp.zeros_like(rowacc)
    R = nrow * BLK

    def sweep(j, _):
        at = pl.ds(pl.multiple_of(j * BLK, BLK), BLK)
        right = yk[:, at]
        total = jnp.zeros((8, BLK), jnp.float32)
        for i in range(R // M):
            rows = slice(i * M, (i + 1) * M)
            e = jnp.exp2(jnp.dot(xt[rows, :], right, preferred_element_type=jnp.float32))
            rowacc[rows, :] += e[:, :128] + e[:, 128:]
            total += jnp.sum(e.reshape(M // 8, 8, BLK), 0)
        colacc[:, at] = total
        return 0

    lax.fori_loop(0, ncol, sweep, 0)
    rows = lax.dot_general(jnp.ones((8, 128), jnp.float32), rowacc[...], (((1,), (1,)), ((), ())),
                           precision=lax.Precision.HIGHEST, preferred_element_type=jnp.float32)[:1]
    cols = jnp.sum(colacc[...], 0, keepdims=True)
    low = jnp.minimum(jnp.min(rows), jnp.min(cols))
    high = jnp.maximum(jnp.max(rows), jnp.max(cols))
    fast = (low > LOW) & (high < HIGH) & (4.0 * jnp.max(row_sq) * jnp.max(col_sq) < NORMS)
    row_log, col_log = jnp.log(rows), jnp.log(cols)
    col_total = jnp.broadcast_to(jnp.sum(col_mass), (1, BLK))
    row_total = jnp.broadcast_to(jnp.sum(row_mass), (1, BLK))
    for k in range(nrow):
        rowp[k, 0:1, :] = row_log[:, k * BLK:(k + 1) * BLK]
        rowp[k, 1:2, :] = col_total
    for j in range(ncol):
        colp[j, 0:1, :] = col_log[:, j * BLK:(j + 1) * BLK]
        colp[j, 1:2, :] = row_total

    @pl.when(jnp.logical_not(fast))
    def _():
        rowacc[...] = jnp.zeros_like(rowacc)
        rmax[...] = jnp.full(rmax.shape, -1e30, jnp.float32)
        colacc[0:1, :] = jnp.full((1, ncol * BLK), -1e30, jnp.float32)
        colacc[1:2, :] = jnp.zeros((1, ncol * BLK), jnp.float32)
        rsum[...] = jnp.zeros_like(rsum)
        for k, ref in enumerate(views):
            flip = ref[...].T
            pts_t = flip[:, :FEAT]
            sq_t = 0.5 * jnp.sum(pts_t * pts_t, 1, keepdims=True)
            term_t = flip[:, FEAT:FEAT + 1]
            rmax[...] = jnp.full(rmax.shape, -1e30, jnp.float32)
            rsum[...] = jnp.zeros_like(rsum)

            def block(j, _):
                at = pl.ds(pl.multiple_of(j * BLK, BLK), BLK)
                pts, sq, term = terms(col_ref.at[j])
                cross = jnp.dot(pts_t, pts, precision=lax.Precision.HIGHEST,
                                preferred_element_type=jnp.float32)
                half = (sq_t + sq - cross) / epsilon
                scores = term - half
                old = rmax[...]
                new = jnp.maximum(old, jnp.broadcast_to(jnp.max(scores, 1, keepdims=True), old.shape))
                part = jnp.sum(jnp.exp(scores - new[:, :1]), 1, keepdims=True)
                rsum[...] = rsum[...] * jnp.exp(old - new) + part
                rmax[...] = new
                others = term_t - half
                cold = colacc[0:1, at]
                cnew = jnp.maximum(cold, jnp.max(others, 0, keepdims=True))
                colacc[1:2, at] = colacc[1:2, at] * jnp.exp(cold - cnew) + jnp.sum(
                    jnp.exp(others - cnew), 0, keepdims=True)
                colacc[0:1, at] = cnew
                return 0

            lax.fori_loop(0, ncol, block, 0)
            total = (rmax[...] + jnp.log(rsum[...])).T
            rowp[k, 0:1, :] = total[:1] + ref[FEAT:FEAT + 1, :]

        def finish(j, _):
            at = pl.ds(pl.multiple_of(j * BLK, BLK), BLK)
            colp[j, 0:1, :] = colacc[0:1, at] + jnp.log(colacc[1:2, at]) + col_ref[j, FEAT:FEAT + 1, :]
            return 0

        lax.fori_loop(0, ncol, finish, 0)


def tile(row_parts, cols, M=512):
    nrow = sum(1 if p.ndim == 2 else p.shape[0] for p in row_parts)
    ncol = cols.shape[0]
    vm = pl.BlockSpec(memory_space=pltpu.VMEM)
    return pl.pallas_call(
        functools.partial(tile_kernel, nrow, ncol, M),
        out_shape=(jax.ShapeDtypeStruct((nrow, 2, BLK), jnp.float32),
                   jax.ShapeDtypeStruct((ncol, 2, BLK), jnp.float32)),
        in_specs=[vm] * (len(row_parts) + 1),
        out_specs=(vm, vm),
        scratch_shapes=[
            pltpu.VMEM((nrow * BLK, 256), jnp.bfloat16),
            pltpu.VMEM((256, ncol * BLK), jnp.bfloat16),
            pltpu.VMEM((nrow * BLK, 128), jnp.float32),
            pltpu.VMEM((8, ncol * BLK), jnp.float32),
            pltpu.VMEM((BLK, 128), jnp.float32),
            pltpu.VMEM((BLK, 128), jnp.float32),
        ],
        compiler_params=pltpu.CompilerParams(vmem_limit_bytes=48 * 2 ** 20),
        cost_estimate=pl.CostEstimate(flops=2 * 256 * nrow * ncol * BLK * BLK, bytes_accessed=2 * 2 ** 20, transcendentals=nrow * ncol * BLK * BLK),
    )(*row_parts, cols)


GRP_MEM = ("grp_0", "grp_1", "mem_0", "mem_1", "mem_2")
PLANE = ("mem_1", "mem_2")
LINE = ("grp_0", "mem_0")
CORE = "grp_1"


def packed(pts, pot, logw):
    rest = jnp.zeros((6, pts.shape[1]), jnp.float32)
    return jnp.concatenate([pts, (logw + pot / epsilon)[None], logw[None], rest], 0)


def along(step):
    index = [(z % 2) * 2 + z // 2 for z in range(4)]
    return [(index[z], index[(z + step) % 4]) for z in range(4)]


def log_sum(pieces):
    logs, masses = pieces[:, 0], pieces[:, 1]
    peak = jnp.max(logs, 0)
    total = peak + jnp.log(jnp.sum(jnp.exp(logs - peak), 0))
    return total - jnp.log(jnp.sum(masses, 0))


def local(source_pts, target_pts, source_pot, target_pot, source_logw, target_logw):
    line = lax.axis_size(LINE)
    plane = lax.axis_size(PLANE)
    flip = [(0, 1), (1, 0)]
    rows = packed(source_pts, source_pot, source_logw)
    cols = packed(target_pts, target_pot, target_logw)
    mine = [rows]
    for k in range(1, line):
        mine.append(lax.ppermute(rows, LINE, along(-k)))
    others = lax.ppermute(jnp.stack(mine), CORE, flip)
    cols = lax.all_to_all(jnp.broadcast_to(cols, (plane, *cols.shape)), PLANE, 0, 0, tiled=True)
    rowp, colp = tile((*mine, others), cols)
    sibling = lax.ppermute(rowp[line:], CORE, flip)
    colp = lax.all_to_all(colp, PLANE, 0, 0, tiled=True)
    pairs = jnp.stack([rowp[:line], sibling], 1)
    got = [pairs[0]]
    for k in range(1, line):
        got.append(lax.ppermute(pairs[k], LINE, along(k)))
    row_total = log_sum(jnp.concatenate(got, 0)) - (source_logw + source_pot / epsilon)
    col_total = log_sum(colp) - (target_logw + target_pot / epsilon)
    return (0.5 * (source_pot - epsilon * row_total), 0.5 * (target_pot - epsilon * col_total))


def solution(mesh):
    finer = Mesh(mesh.devices.reshape(2, 2, 2, 4, 4), GRP_MEM)
    return jax.shard_map(
        local,
        mesh=finer,
        in_specs=(P(None, GRP_MEM), P(None, GRP_MEM), P(GRP_MEM), P(GRP_MEM), P(GRP_MEM), P(GRP_MEM)),
        out_specs=(P(GRP_MEM), P(GRP_MEM)),
        check_vma=False,
    )
```

```python
import functools

import jax
import jax.numpy as jnp
from jax import lax
from jax.experimental import pallas as pl
from jax.experimental.pallas import tpu as pltpu
from jax.sharding import Mesh
from jax.sharding import PartitionSpec as P

GRP_MEM = ("grp_0", "grp_1", "mem_0", "mem_1", "mem_2")
GROUP = ("grp_0", "grp_1", "mem_0")
PLANE = ("mem_1", "mem_2")
LINE = ("grp_0", "mem_0")
CORE = "grp_1"
SIDE = 4

epsilon = 4.0
LOG2E = 1.4426950408889634
FEAT = 64
BLK = 256
TALL = 136
floor_value = -1e30
LOW = 2.0**-90
HIGH = 2.0**120
NORMS = 2.0**15

VMEM = pl.BlockSpec(memory_space=pltpu.VMEM)


ANY = pl.BlockSpec(memory_space=pl.ANY)


def call(kernel, out, ins, scratch=(), cost=None, specs=None):
    return pl.pallas_call(
        kernel,
        out_shape=out,
        in_specs=[ANY if specs else VMEM] * ins,
        out_specs=specs or jax.tree.map(lambda _: VMEM, out),
        scratch_shapes=scratch,
        compiler_params=pltpu.CompilerParams(vmem_limit_bytes=40 * 2**20),
        cost_estimate=cost,
    )


def f32(*shape):
    return jax.ShapeDtypeStruct(shape, jnp.float32)


def pack_kernel(spts, tpts, spot, tpot, slogw, tlogw, rows, copies, cols, lines, sems, out_sems):
    loads = []
    for pts, block in ((spts, rows), (tpts, cols)):
        for half in range(2):
            loads.append((pts.at[:, 128 * half : 128 * (half + 1)], block.at[64 * half : 64 * (half + 1), :]))
    for k, ref in enumerate((slogw, spot, tlogw, tpot)):
        loads.append((ref, lines.at[k]))
    loads = [pltpu.make_async_copy(a, b, sems.at[k]) for k, (a, b) in enumerate(loads)]
    for load in loads:
        load.start()
    for k in range(4, 8):
        loads[k].wait()
    for block, logw, pot in ((rows, lines[0], lines[1]), (cols, lines[2], lines[3])):
        tail = (logw + pot / epsilon, logw, pot, jnp.zeros((2, 128), jnp.float32))
        block[128:136, :] = jnp.concatenate(tail, 0)
    loads[2].wait()
    loads[3].wait()
    stores = [pltpu.make_async_copy(cols, copies.at[k], out_sems.at[k]) for k in range(copies.shape[0])]
    for store in stores:
        store.start()
    loads[0].wait()
    loads[1].wait()
    for store in stores:
        store.wait()


def wide(block, line):
    return jnp.concatenate([block[line : line + 1, :], block[line + 1 : line + 2, :]], 1)


def unpacked(block):
    pts = jnp.concatenate([block[0:64, :], block[64:128, :]], 1)
    return pts, 0.5 * jnp.sum(pts * pts, 0, keepdims=True), wide(block, 128)


def split(v):
    head = v.astype(jnp.bfloat16).astype(jnp.float32)
    return head, v - head


def bias_lines(bias, first):
    b1, rest = split(bias)
    b2, b3 = split(rest)
    line = lax.broadcasted_iota(jnp.int32, (16, BLK), 0)
    out = jnp.zeros((16, BLK), jnp.float32)
    for k, piece in enumerate((b1, b2, b3)):
        out = jnp.where(line == k + first, piece, out)
    return jnp.where((line >= 3 - first) & (line < 6 - first), 1.0, out)


def blocks_of(refs):
    out = []
    for ref in refs:
        out.extend([ref] if len(ref.shape) == 2 else [ref.at[k] for k in range(ref.shape[0])])
    return out


def rows_kernel(*refs):
    blocks = blocks_of(refs[:-2])
    xt, stats = refs[-2:]
    most = jnp.zeros((1, BLK), jnp.float32)
    mass = jnp.zeros((1, BLK), jnp.float32)
    for k, block in enumerate(blocks):
        pts, sq, term = unpacked(block)
        most = jnp.maximum(most, sq)
        mass += jnp.exp(wide(block, 130))
        x1, x2 = split(pts * (LOG2E / epsilon))
        bias = bias_lines((term - sq / epsilon) * LOG2E, 0)
        left = jnp.concatenate([x1, x2], 0)
        right = jnp.concatenate([x1, bias, jnp.zeros((48, BLK), jnp.float32)], 0)
        xt[k * BLK : (k + 1) * BLK, :128] = left.T.astype(jnp.bfloat16)
        xt[k * BLK : (k + 1) * BLK, 128:] = right.T.astype(jnp.bfloat16)
    stats[0:1, :] = most
    stats[1:2, :] = mass


def tile_kernel(nrow, ncol, *refs):
    blocks = blocks_of(refs[:5])
    cols, xt, stats, out, own, yk, rowacc, colacc, rmax, rsum, rlog = refs[5:]
    high, core, mem_0 = (lax.axis_index(n) for n in GROUP)
    at_plane = lax.axis_index("mem_1") * SIDE + lax.axis_index("mem_2")
    at_group = (high * 2 + core) * 2 + mem_0
    z = mem_0 * 2 + high

    def owner(k):
        far = lax.rem(z + k % SIDE, SIDE)
        side = core if k < SIDE else 1 - core
        return ((lax.rem(far, 2) * 2 + side) * 2 + far // 2) * (SIDE * SIDE) + at_plane

    def prepare(j, state):
        most, mass = state
        block = cols.at[j]
        pts, sq, term = unpacked(block)
        y1, y2 = split(pts)
        bias = bias_lines((term - sq / epsilon) * LOG2E, 3)
        at = pl.ds(pl.multiple_of(j * BLK, BLK), BLK)
        y1 = y1.astype(jnp.bfloat16)
        yk[0:64, at] = y1
        yk[64:128, at] = y1
        yk[128:192, at] = y2.astype(jnp.bfloat16)
        yk[192:208, at] = bias.astype(jnp.bfloat16)
        yk[208:256, at] = jnp.zeros((48, BLK), jnp.bfloat16)
        return jnp.maximum(most, sq), mass + jnp.exp(wide(block, 130))

    zero = jnp.zeros((1, BLK), jnp.float32)
    most, mass = lax.fori_loop(0, ncol, prepare, (zero, zero), unroll=4)
    rowacc[...] = jnp.zeros_like(rowacc)
    step = 512

    def sweep(j, _):
        at = pl.ds(pl.multiple_of(j * BLK, BLK), BLK)
        right = yk[:, at]
        total = jnp.zeros((8, BLK), jnp.float32)
        for i in range(nrow * BLK // step):
            rows = slice(i * step, (i + 1) * step)
            e = jnp.exp2(jnp.dot(xt[rows, :], right, preferred_element_type=jnp.float32))
            rowacc[rows, :] += e[:, :128] + e[:, 128:]
            total += jnp.sum(e.reshape(step // 8, 8, BLK), 0)
        colacc[:, at] = total
        return 0

    lax.fori_loop(0, ncol, sweep, 0, unroll=8)
    s1, s2 = split(rowacc[...])
    parts = jnp.concatenate([s1, s2], 1).astype(jnp.bfloat16)
    rows = lax.dot_general(
        jnp.ones((16, 256), jnp.bfloat16), parts, (((1,), (1,)), ((), ())), preferred_element_type=jnp.float32
    )[:1]
    sums = jnp.sum(colacc[...], 0, keepdims=True)
    low = jnp.minimum(jnp.min(rows), jnp.min(sums))
    high = jnp.maximum(jnp.max(rows), jnp.max(sums))
    fast = (low > LOW) & (high < HIGH) & (4.0 * jnp.max(stats[0:1, :]) * jnp.max(most) < NORMS)
    rlog[...] = jnp.log(rows)
    colacc[0:1, :] = jnp.log(sums)

    @pl.when(jnp.logical_not(fast))
    def _():
        colacc[0:1, :] = jnp.full((1, ncol * BLK), floor_value, jnp.float32)
        colacc[1:2, :] = jnp.zeros((1, ncol * BLK), jnp.float32)
        for k, block in enumerate(blocks):
            flat, _, term = unpacked(block)
            pts_t = flat.T
            sq_t = 0.5 * jnp.sum(pts_t * pts_t, 1, keepdims=True)
            term_t = jnp.broadcast_to(term, (128, BLK)).T[:, :1]
            rmax[...] = jnp.full(rmax.shape, floor_value, jnp.float32)
            rsum[...] = jnp.zeros_like(rsum)

            def exact(j, _):
                at = pl.ds(pl.multiple_of(j * BLK, BLK), BLK)
                pts, sq, col_term = unpacked(cols.at[j])
                cross = jnp.dot(
                    pts_t, pts, precision=lax.Precision.HIGHEST, preferred_element_type=jnp.float32
                )
                half = (sq_t + sq - cross) / epsilon
                scores = col_term - half
                old = rmax[...]
                new = jnp.maximum(old, jnp.max(scores, 1, keepdims=True))
                part = jnp.sum(jnp.exp(scores - new[:, :1]), 1, keepdims=True)
                rsum[...] = rsum[...] * jnp.exp(old - new) + part
                rmax[...] = new
                others = term_t - half
                old = colacc[0:1, at]
                new = jnp.maximum(old, jnp.max(others, 0, keepdims=True))
                part = jnp.sum(jnp.exp(others - new), 0, keepdims=True)
                colacc[1:2, at] = colacc[1:2, at] * jnp.exp(old - new) + part
                colacc[0:1, at] = new
                return 0

            lax.fori_loop(0, ncol, exact, 0)
            total = (rmax[...] + jnp.log(rsum[...])).T[:1]
            rlog[:, k * BLK : (k + 1) * BLK] = total + term

        def finish(j, _):
            at = pl.ds(pl.multiple_of(j * BLK, BLK), BLK)
            colacc[0:1, at] = colacc[0:1, at] + jnp.log(colacc[1:2, at]) + wide(cols.at[j], 128)
            return 0

        lax.fori_loop(0, ncol, finish, 0)

    row_mass = jnp.broadcast_to(jnp.sum(stats[1:2, :], 1, keepdims=True), (1, BLK))
    col_mass = jnp.broadcast_to(jnp.sum(mass, 1, keepdims=True), (1, BLK))
    for j in range(ncol):
        to = at_group * ncol + j
        out[to, 0:1, :] = colacc[0:1, j * BLK : (j + 1) * BLK]
        out[to, 1:2, :] = row_mass
    mine = pl.ds(pl.multiple_of(at_plane * BLK, BLK), BLK)
    own[0:1, :] = colacc[0:1, mine]
    own[1:2, :] = row_mass
    for k in range(nrow):
        to = owner(k)
        out[to, 0:1, :] = rlog[:, k * BLK : (k + 1) * BLK]
        out[to, 1:2, :] = col_mass
    own[2:3, :] = wide(blocks[0], 128)
    own[3:4, :] = wide(blocks[0], 132)
    own[4:5, :] = wide(cols.at[at_plane], 128)
    own[5:6, :] = wide(cols.at[at_plane], 132)


def finish_kernel(nrow, ncol, got, own, source, target):
    at_plane = lax.axis_index("mem_1") * SIDE + lax.axis_index("mem_2")
    high, core, mem_0 = (lax.axis_index(n) for n in GROUP)
    at_group = (high * 2 + core) * 2 + mem_0

    def total(pieces):
        logs = jnp.concatenate([p[0:1, :] for p in pieces], 0)
        mass = sum(p[1:2, :] for p in pieces)
        peak = jnp.max(logs, 0, keepdims=True)
        return peak + jnp.log(jnp.sum(jnp.exp(logs - peak), 0, keepdims=True)) - jnp.log(mass)

    row_total = total([got[k * ncol + at_plane] for k in range(nrow)]) - own[2:3, :]
    local = own[0:2, :]
    from_cols = []
    for j in range(ncol):
        from_cols.append(jnp.where(at_plane == j, local, got[at_group * ncol + j]))
    col_total = total(from_cols) - own[4:5, :]
    source[...] = (0.5 * (own[3:4, :] - epsilon * row_total)).reshape(BLK)
    target[...] = (0.5 * (own[5:6, :] - epsilon * col_total)).reshape(BLK)


def along(step):
    index = [(z % 2) * 2 + z // 2 for z in range(SIDE)]
    return [(index[z], index[(z + step) % SIDE]) for z in range(SIDE)]


def local(source_pts, target_pts, source_pot, target_pot, source_logw, target_logw):
    nrow, ncol = lax.axis_size(GROUP), lax.axis_size(PLANE)
    lines = [v.reshape(2, 128) for v in (source_pot, target_pot, source_logw, target_logw)]
    rows, copies = call(
        pack_kernel,
        (f32(TALL, 128), f32(ncol, TALL, 128)),
        6,
        scratch=[
            pltpu.VMEM((TALL, 128), jnp.float32),
            pltpu.VMEM((4, 2, 128), jnp.float32),
            pltpu.SemaphoreType.DMA((8,)),
            pltpu.SemaphoreType.DMA((ncol,)),
        ],
        specs=(VMEM, ANY),
    )(source_pts, target_pts, *lines)
    mine = [rows]
    for k in range(1, SIDE):
        mine.append(lax.ppermute(rows, LINE, along(-k)))
    others = lax.ppermute(jnp.stack(mine), CORE, [(0, 1), (1, 0)])
    cols = lax.all_to_all(copies, PLANE, 0, 0, tiled=True)
    size = nrow * ncol * BLK * BLK
    xt, stats = call(
        rows_kernel,
        (jax.ShapeDtypeStruct((nrow * BLK, 256), jnp.bfloat16), f32(2, BLK)),
        5,
        cost=pl.CostEstimate(flops=10**6, bytes_accessed=10**6, transcendentals=0),
    )(*mine, others)
    out, own = call(
        functools.partial(tile_kernel, nrow, ncol),
        (f32(nrow * ncol, 2, BLK), f32(8, BLK)),
        8,
        scratch=[
            pltpu.VMEM((256, ncol * BLK), jnp.bfloat16),
            pltpu.VMEM((nrow * BLK, 128), jnp.float32),
            pltpu.VMEM((8, ncol * BLK), jnp.float32),
            pltpu.VMEM((BLK, 128), jnp.float32),
            pltpu.VMEM((BLK, 128), jnp.float32),
            pltpu.VMEM((1, nrow * BLK), jnp.float32),
        ],
        cost=pl.CostEstimate(flops=512 * size, bytes_accessed=4 * 2**20, transcendentals=size),
    )(*mine, others, cols, xt, stats)
    got = lax.all_to_all(out, GRP_MEM, 0, 0, tiled=True)
    return call(functools.partial(finish_kernel, nrow, ncol), (f32(BLK), f32(BLK)), 2)(got, own)


def solution(mesh):
    finer = Mesh(mesh.devices.reshape(2, 2, 2, 4, 4), GRP_MEM)
    return jax.shard_map(
        local,
        mesh=finer,
        in_specs=(P(None, GRP_MEM), P(None, GRP_MEM), P(GRP_MEM), P(GRP_MEM), P(GRP_MEM), P(GRP_MEM)),
        out_specs=(P(GRP_MEM), P(GRP_MEM)),
        check_vma=False,
    )
```

```python
import functools

import jax
import jax.numpy as jnp
from jax import lax
from jax.experimental import pallas as pl
from jax.experimental.pallas import tpu as pltpu
from jax.sharding import Mesh
from jax.sharding import PartitionSpec as P

GRP_MEM = ("grp_0", "grp_1", "mem_0", "mem_1", "mem_2")
GROUP = ("grp_0", "grp_1", "mem_0")
PLANE = ("mem_1", "mem_2")
LINE = ("grp_0", "mem_0")
CORE = "grp_1"
SIDE = 4

epsilon = 4.0
LOG2E = 1.4426950408889634
FEAT = 64
BLK = 256
TALL = 136
floor_value = -1e30
LOW = 2.0**-90
HIGH = 2.0**120
NORMS = 2.0**15

VMEM = pl.BlockSpec(memory_space=pltpu.VMEM)


HBM = pl.BlockSpec(memory_space=pltpu.HBM)


def call(kernel, out, ins, scratch=(), cost=None, specs=None):
    return pl.pallas_call(
        kernel,
        out_shape=out,
        in_specs=[HBM if specs else VMEM] * ins,
        out_specs=specs or jax.tree.map(lambda _: VMEM, out),
        scratch_shapes=scratch,
        compiler_params=pltpu.CompilerParams(vmem_limit_bytes=40 * 2**20),
        cost_estimate=cost,
    )


def f32(*shape):
    return jax.ShapeDtypeStruct(shape, jnp.float32)


def pack_kernel(spts, tpts, spot, tpot, slogw, tlogw, rows, copies, cols, lines, sems, out_sems):
    loads = []
    for pts, block in ((spts, rows), (tpts, cols)):
        for half in range(2):
            loads.append((pts.at[:, 128 * half : 128 * (half + 1)], block.at[64 * half : 64 * (half + 1), :]))
    for k, ref in enumerate((slogw, spot, tlogw, tpot)):
        loads.append((ref, lines.at[k]))
    loads = [pltpu.make_async_copy(a, b, sems.at[k]) for k, (a, b) in enumerate(loads)]
    for load in loads:
        load.start()
    for k in range(4, 8):
        loads[k].wait()
    for block, logw, pot, other in ((rows, lines[0], lines[1], lines[2]), (cols, lines[2], lines[3], lines[0])):
        tail = (logw + pot / epsilon, logw, pot, other)
        block[128:136, :] = jnp.concatenate(tail, 0)
    loads[2].wait()
    loads[3].wait()
    stores = [pltpu.make_async_copy(cols, copies.at[k], out_sems.at[k]) for k in range(copies.shape[0])]
    for store in stores:
        store.start()
    loads[0].wait()
    loads[1].wait()
    for store in stores:
        store.wait()


def wide(block, line):
    return jnp.concatenate([block[line : line + 1, :], block[line + 1 : line + 2, :]], 1)


def unpacked(block):
    pts = jnp.concatenate([block[0:64, :], block[64:128, :]], 1)
    return pts, 0.5 * jnp.sum(pts * pts, 0, keepdims=True), wide(block, 128)


def split(v):
    head = v.astype(jnp.bfloat16).astype(jnp.float32)
    return head, v - head


def bias_lines(bias, first):
    b1, rest = split(bias)
    b2, b3 = split(rest)
    line = lax.broadcasted_iota(jnp.int32, (16, BLK), 0)
    out = jnp.zeros((16, BLK), jnp.float32)
    for k, piece in enumerate((b1, b2, b3)):
        out = jnp.where(line == k + first, piece, out)
    return jnp.where((line >= 3 - first) & (line < 6 - first), 1.0, out)


def blocks_of(refs):
    out = []
    for ref in refs:
        out.extend([ref] if len(ref.shape) == 2 else [ref.at[k] for k in range(ref.shape[0])])
    return out


def rows_kernel(*refs):
    blocks = blocks_of(refs[:-2])
    xt, stats = refs[-2:]
    most = jnp.zeros((1, BLK), jnp.float32)
    for k, block in enumerate(blocks):
        pts, sq, term = unpacked(block)
        most = jnp.maximum(most, sq)
        x1, x2 = split(pts * (LOG2E / epsilon))
        bias = bias_lines((term - sq / epsilon) * LOG2E, 0)
        left = jnp.concatenate([x1, x2], 0)
        right = jnp.concatenate([x1, bias, jnp.zeros((48, BLK), jnp.float32)], 0)
        xt[k * BLK : (k + 1) * BLK, :128] = left.T.astype(jnp.bfloat16)
        xt[k * BLK : (k + 1) * BLK, 128:] = right.T.astype(jnp.bfloat16)
    stats[...] = most


def tile_kernel(nrow, ncol, *refs):
    blocks = blocks_of(refs[:5])
    cols, xt, stats, out, own, yk, rowacc, colacc, rmax, rsum, rlog = refs[5:]
    high, core, mem_0 = (lax.axis_index(n) for n in GROUP)
    at_plane = lax.axis_index("mem_1") * SIDE + lax.axis_index("mem_2")
    at_group = (high * 2 + core) * 2 + mem_0
    z = mem_0 * 2 + high

    def owner(k):
        far = lax.rem(z + k % SIDE, SIDE)
        side = core if k < SIDE else 1 - core
        return ((lax.rem(far, 2) * 2 + side) * 2 + far // 2) * (SIDE * SIDE) + at_plane

    def prepare(j, state):
        most, masses = state
        block = cols.at[j]
        pts, sq, term = unpacked(block)
        y1, y2 = split(pts)
        bias = bias_lines((term - sq / epsilon) * LOG2E, 3)
        at = pl.ds(pl.multiple_of(j * BLK, BLK), BLK)
        y1 = y1.astype(jnp.bfloat16)
        yk[0:64, at] = y1
        yk[64:128, at] = y1
        yk[128:192, at] = y2.astype(jnp.bfloat16)
        yk[192:208, at] = bias.astype(jnp.bfloat16)
        yk[208:256, at] = jnp.zeros((48, BLK), jnp.bfloat16)
        return jnp.maximum(most, sq), masses + jnp.exp(block[128:136, :])

    most, masses = lax.fori_loop(
        0, ncol, prepare, (jnp.zeros((1, BLK), jnp.float32), jnp.zeros((8, 128), jnp.float32)), unroll=4
    )
    rowacc[...] = jnp.zeros_like(rowacc)
    step = 512

    def sweep(j, _):
        at = pl.ds(pl.multiple_of(j * BLK, BLK), BLK)
        right = yk[:, at]
        total = jnp.zeros((8, BLK), jnp.float32)
        for i in range(nrow * BLK // step):
            rows = slice(i * step, (i + 1) * step)
            e = jnp.exp2(jnp.dot(xt[rows, :], right, preferred_element_type=jnp.float32))
            rowacc[rows, :] += e[:, :128] + e[:, 128:]
            total += jnp.sum(e.reshape(step // 8, 8, BLK), 0)
        colacc[:, at] = total
        return 0

    lax.fori_loop(0, ncol, sweep, 0, unroll=8)
    s1, s2 = split(rowacc[...])
    parts = jnp.concatenate([s1, s2], 1).astype(jnp.bfloat16)
    rows = lax.dot_general(
        jnp.ones((16, 256), jnp.bfloat16), parts, (((1,), (1,)), ((), ())), preferred_element_type=jnp.float32
    )[:1]
    sums = jnp.sum(colacc[...], 0, keepdims=True)
    low = jnp.minimum(jnp.min(rows), jnp.min(sums))
    high = jnp.maximum(jnp.max(rows), jnp.max(sums))
    fast = (low > LOW) & (high < HIGH) & (4.0 * jnp.max(stats[...]) * jnp.max(most) < NORMS)
    rlog[...] = jnp.log(rows)
    colacc[0:1, :] = jnp.log(sums)

    @pl.when(jnp.logical_not(fast))
    def _():
        colacc[0:1, :] = jnp.full((1, ncol * BLK), floor_value, jnp.float32)
        colacc[1:2, :] = jnp.zeros((1, ncol * BLK), jnp.float32)
        for k, block in enumerate(blocks):
            flat, _, term = unpacked(block)
            pts_t = flat.T
            sq_t = 0.5 * jnp.sum(pts_t * pts_t, 1, keepdims=True)
            term_t = jnp.broadcast_to(term, (128, BLK)).T[:, :1]
            rmax[...] = jnp.full(rmax.shape, floor_value, jnp.float32)
            rsum[...] = jnp.zeros_like(rsum)

            def exact(j, _):
                at = pl.ds(pl.multiple_of(j * BLK, BLK), BLK)
                pts, sq, col_term = unpacked(cols.at[j])
                cross = jnp.dot(
                    pts_t, pts, precision=lax.Precision.HIGHEST, preferred_element_type=jnp.float32
                )
                half = (sq_t + sq - cross) / epsilon
                scores = col_term - half
                old = rmax[...]
                new = jnp.maximum(old, jnp.max(scores, 1, keepdims=True))
                part = jnp.sum(jnp.exp(scores - new[:, :1]), 1, keepdims=True)
                rsum[...] = rsum[...] * jnp.exp(old - new) + part
                rmax[...] = new
                others = term_t - half
                old = colacc[0:1, at]
                new = jnp.maximum(old, jnp.max(others, 0, keepdims=True))
                part = jnp.sum(jnp.exp(others - new), 0, keepdims=True)
                colacc[1:2, at] = colacc[1:2, at] * jnp.exp(old - new) + part
                colacc[0:1, at] = new
                return 0

            lax.fori_loop(0, ncol, exact, 0)
            total = (rmax[...] + jnp.log(rsum[...])).T[:1]
            rlog[:, k * BLK : (k + 1) * BLK] = total + term

        def finish(j, _):
            at = pl.ds(pl.multiple_of(j * BLK, BLK), BLK)
            colacc[0:1, at] = colacc[0:1, at] + jnp.log(colacc[1:2, at]) + wide(cols.at[j], 128)
            return 0

        lax.fori_loop(0, ncol, finish, 0)

    target_mass = jnp.sum(masses[2:4, :], keepdims=True)
    source_mass = jnp.sum(masses[6:8, :], keepdims=True)
    mass = jnp.concatenate(
        [jnp.broadcast_to(source_mass, (1, 128)), jnp.broadcast_to(target_mass, (1, 128))], 1
    )
    before = lax.rem(at_plane + ncol - 1, ncol)
    for k in range(nrow):
        out[k * ncol + before] = mass
    for j in range(ncol):
        out[at_group * ncol + j] = colacc[0:1, j * BLK : (j + 1) * BLK]
    for k in range(nrow):
        out[owner(k)] = rlog[:, k * BLK : (k + 1) * BLK]
    own[0:1, :] = colacc[0:1, pl.ds(pl.multiple_of(at_plane * BLK, BLK), BLK)]
    own[1:2, :] = mass
    own[2:3, :] = wide(blocks[0], 128)
    own[3:4, :] = wide(blocks[0], 132)
    own[4:5, :] = wide(cols.at[at_plane], 128)
    own[5:6, :] = wide(cols.at[at_plane], 132)


def finish_kernel(nrow, ncol, got, own, source, target):
    at_plane = lax.axis_index("mem_1") * SIDE + lax.axis_index("mem_2")
    high, core, mem_0 = (lax.axis_index(n) for n in GROUP)
    at_group = (high * 2 + core) * 2 + mem_0
    after = lax.rem(at_plane + 1, ncol)

    def total(pieces):
        logs = jnp.concatenate(pieces, 0)
        peak = jnp.max(logs, 0, keepdims=True)
        return peak + jnp.log(jnp.sum(jnp.exp(logs - peak), 0, keepdims=True))

    mass = own[1:2, :]
    for k in range(nrow):
        mass = mass + jnp.where(at_group == k, 0.0, got[k * ncol + after])
    mass = jnp.log(mass)
    row_total = total([got[k * ncol + at_plane] for k in range(nrow)]) - own[2:3, :] - wide_of(mass, 1)
    pieces = [jnp.where(at_plane == j, own[0:1, :], got[at_group * ncol + j]) for j in range(ncol)]
    col_total = total(pieces) - own[4:5, :] - wide_of(mass, 0)
    source[...] = (0.5 * (own[3:4, :] - epsilon * row_total)).reshape(BLK)
    target[...] = (0.5 * (own[5:6, :] - epsilon * col_total)).reshape(BLK)


def wide_of(mass, half):
    line = mass[:, 128 * half : 128 * (half + 1)]
    return jnp.concatenate([line, line], 1)


def along(step):
    index = [(z % 2) * 2 + z // 2 for z in range(SIDE)]
    return [(index[z], index[(z + step) % SIDE]) for z in range(SIDE)]


def local(source_pts, target_pts, source_pot, target_pot, source_logw, target_logw):
    nrow, ncol = lax.axis_size(GROUP), lax.axis_size(PLANE)
    lines = [v.reshape(2, 128) for v in (source_pot, target_pot, source_logw, target_logw)]
    rows, copies = call(
        pack_kernel,
        (f32(TALL, 128), f32(ncol, TALL, 128)),
        6,
        scratch=[
            pltpu.VMEM((TALL, 128), jnp.float32),
            pltpu.VMEM((4, 2, 128), jnp.float32),
            pltpu.SemaphoreType.DMA((8,)),
            pltpu.SemaphoreType.DMA((ncol,)),
        ],
        specs=(VMEM, HBM),
    )(*(pltpu.with_memory_space_constraint(v, pltpu.HBM) for v in (source_pts, target_pts, *lines)))
    mine = [rows]
    for k in range(1, SIDE):
        mine.append(lax.ppermute(rows, LINE, along(-k)))
    others = lax.ppermute(jnp.stack(mine), CORE, [(0, 1), (1, 0)])
    cols = lax.all_to_all(copies, PLANE, 0, 0, tiled=True)
    size = nrow * ncol * BLK * BLK
    xt, stats = call(
        rows_kernel,
        (jax.ShapeDtypeStruct((nrow * BLK, 256), jnp.bfloat16), f32(1, BLK)),
        5,
        cost=pl.CostEstimate(flops=10**6, bytes_accessed=10**6, transcendentals=0),
    )(*mine, others)
    out, own = call(
        functools.partial(tile_kernel, nrow, ncol),
        (f32(nrow * ncol, 1, BLK), f32(8, BLK)),
        8,
        scratch=[
            pltpu.VMEM((256, ncol * BLK), jnp.bfloat16),
            pltpu.VMEM((nrow * BLK, 128), jnp.float32),
            pltpu.VMEM((8, ncol * BLK), jnp.float32),
            pltpu.VMEM((BLK, 128), jnp.float32),
            pltpu.VMEM((BLK, 128), jnp.float32),
            pltpu.VMEM((1, nrow * BLK), jnp.float32),
        ],
        cost=pl.CostEstimate(flops=512 * size, bytes_accessed=4 * 2**20, transcendentals=size),
    )(*mine, others, cols, xt, stats)
    got = lax.all_to_all(out, GRP_MEM, 0, 0, tiled=True)
    return call(functools.partial(finish_kernel, nrow, ncol), (f32(BLK), f32(BLK)), 2)(got, own)


def solution(mesh):
    finer = Mesh(mesh.devices.reshape(2, 2, 2, 4, 4), GRP_MEM)
    return jax.shard_map(
        local,
        mesh=finer,
        in_specs=(P(None, GRP_MEM), P(None, GRP_MEM), P(GRP_MEM), P(GRP_MEM), P(GRP_MEM), P(GRP_MEM)),
        out_specs=(P(GRP_MEM), P(GRP_MEM)),
        check_vma=False,
    )
```

```python
import functools

import jax
import jax.numpy as jnp
from jax import lax
from jax.experimental import pallas as pl
from jax.experimental.pallas import tpu as pltpu
from jax.sharding import Mesh
from jax.sharding import PartitionSpec as P

GRP_MEM = ("grp_0", "grp_1", "mem_0", "mem_1", "mem_2")
GROUP = ("grp_0", "grp_1", "mem_0")
PLANE = ("mem_1", "mem_2")
LINE = ("grp_0", "mem_0")
CORE = "grp_1"
SIDE = 4

epsilon = 4.0
LOG2E = 1.4426950408889634
FEAT = 64
BLK = 256
TALL = 136
floor_value = -1e30
LOW = 2.0**-90
HIGH = 2.0**120
NORMS = 2.0**15

VMEM = pl.BlockSpec(memory_space=pltpu.VMEM)


HBM = pl.BlockSpec(memory_space=pltpu.HBM)


def call(kernel, out, ins, scratch=(), cost=None, specs=None):
    return pl.pallas_call(
        kernel,
        out_shape=out,
        in_specs=[HBM if specs else VMEM] * ins,
        out_specs=specs or jax.tree.map(lambda _: VMEM, out),
        scratch_shapes=scratch,
        compiler_params=pltpu.CompilerParams(vmem_limit_bytes=40 * 2**20),
        cost_estimate=cost,
    )


def f32(*shape):
    return jax.ShapeDtypeStruct(shape, jnp.float32)


def pack_kernel(spts, tpts, spot, tpot, slogw, tlogw, rows, copies, cols, lines, sems, out_sems):
    loads = []
    for pts, block in ((spts, rows), (tpts, cols)):
        for half in range(2):
            loads.append((pts.at[:, 128 * half : 128 * (half + 1)], block.at[64 * half : 64 * (half + 1), :]))
    for k, ref in enumerate((slogw, spot, tlogw, tpot)):
        loads.append((ref, lines.at[k]))
    loads = [pltpu.make_async_copy(a, b, sems.at[k]) for k, (a, b) in enumerate(loads)]
    for load in loads:
        load.start()
    for k in range(4, 8):
        loads[k].wait()
    for block, logw, pot, other in ((rows, lines[0], lines[1], lines[2]), (cols, lines[2], lines[3], lines[0])):
        tail = (logw + pot / epsilon, logw, pot, other)
        block[128:136, :] = jnp.concatenate(tail, 0)
    loads[2].wait()
    loads[3].wait()
    stores = [pltpu.make_async_copy(cols, copies.at[k], out_sems.at[k]) for k in range(copies.shape[0])]
    for store in stores:
        store.start()
    loads[0].wait()
    loads[1].wait()
    for store in stores:
        store.wait()


def wide(block, line):
    return jnp.concatenate([block[line : line + 1, :], block[line + 1 : line + 2, :]], 1)


def unpacked(block):
    pts = jnp.concatenate([block[0:64, :], block[64:128, :]], 1)
    return pts, 0.5 * jnp.sum(pts * pts, 0, keepdims=True), wide(block, 128)


def split(v):
    head = v.astype(jnp.bfloat16).astype(jnp.float32)
    return head, v - head


def bias_lines(bias, first):
    b1, rest = split(bias)
    b2, b3 = split(rest)
    line = lax.broadcasted_iota(jnp.int32, (16, BLK), 0)
    out = jnp.zeros((16, BLK), jnp.float32)
    for k, piece in enumerate((b1, b2, b3)):
        out = jnp.where(line == k + first, piece, out)
    return jnp.where((line >= 3 - first) & (line < 6 - first), 1.0, out)


def blocks_of(refs):
    out = []
    for ref in refs:
        out.extend([ref] if len(ref.shape) == 2 else [ref.at[k] for k in range(ref.shape[0])])
    return out


def rows_kernel(*refs):
    blocks = blocks_of(refs[:-2])
    xt, stats = refs[-2:]
    most = jnp.zeros((1, BLK), jnp.float32)
    for k, block in enumerate(blocks):
        pts, sq, term = unpacked(block)
        most = jnp.maximum(most, sq)
        x1, x2 = split(pts * (LOG2E / epsilon))
        bias = bias_lines((term - sq / epsilon) * LOG2E, 0)
        left = jnp.concatenate([x1, x2], 0)
        right = jnp.concatenate([x1, bias, jnp.zeros((48, BLK), jnp.float32)], 0)
        xt[k * BLK : (k + 1) * BLK, :128] = left.T.astype(jnp.bfloat16)
        xt[k * BLK : (k + 1) * BLK, 128:] = right.T.astype(jnp.bfloat16)
    stats[...] = most


def half_kernel(nrow, ncol, last, *refs):
    blocks = blocks_of(refs[:nrow_refs(last)])
    refs = refs[nrow_refs(last) :]
    if last:
        cols, xt, stats, yk, former, lines, out, own, rowacc, colacc, rmax, rsum, rlog = refs
        most = former[1:2, 0:BLK]
    else:
        cols, xt, stats, yk, former, lines, rowacc, colacc, rmax, rsum, rlog = refs

        def prepare(j, state):
            most, masses = state
            block = cols.at[j]
            pts, sq, term = unpacked(block)
            y1, y2 = split(pts)
            bias = bias_lines((term - sq / epsilon) * LOG2E, 3)
            at = pl.ds(pl.multiple_of(j * BLK, BLK), BLK)
            y1 = y1.astype(jnp.bfloat16)
            yk[0:64, at] = y1
            yk[64:128, at] = y1
            yk[128:192, at] = y2.astype(jnp.bfloat16)
            yk[192:208, at] = bias.astype(jnp.bfloat16)
            yk[208:256, at] = jnp.zeros((48, BLK), jnp.bfloat16)
            return jnp.maximum(most, sq), masses + jnp.exp(block[128:136, :])

        most, masses = lax.fori_loop(
            0, ncol, prepare, (jnp.zeros((1, BLK), jnp.float32), jnp.zeros((8, 128), jnp.float32)), unroll=4
        )
    rowacc[...] = jnp.zeros_like(rowacc)
    step = 512
    first = 0 if last else nrow * BLK

    def sweep(j, _):
        at = pl.ds(pl.multiple_of(j * BLK, BLK), BLK)
        right = yk[:, at]
        total = jnp.zeros((8, BLK), jnp.float32)
        for i in range(nrow * BLK // step):
            rows = slice(i * step, (i + 1) * step)
            held = slice(first + i * step, first + (i + 1) * step)
            e = jnp.exp2(jnp.dot(xt[held, :], right, preferred_element_type=jnp.float32))
            rowacc[rows, :] += e[:, :128] + e[:, 128:]
            total += jnp.sum(e.reshape(step // 8, 8, BLK), 0)
        colacc[:, at] = total
        return 0

    lax.fori_loop(0, ncol, sweep, 0, unroll=True)
    s1, s2 = split(rowacc[...])
    parts = jnp.concatenate([s1, s2], 1).astype(jnp.bfloat16)
    rows = lax.dot_general(
        jnp.ones((16, 256), jnp.bfloat16), parts, (((1,), (1,)), ((), ())), preferred_element_type=jnp.float32
    )[:1]
    sums = jnp.sum(colacc[...], 0, keepdims=True)
    low = jnp.minimum(jnp.min(rows), jnp.min(sums))
    high = jnp.maximum(jnp.max(rows), jnp.max(sums))
    fast = (low > LOW) & (high < HIGH) & (4.0 * jnp.max(stats[...]) * jnp.max(most) < NORMS)
    rlog[...] = jnp.log(rows)
    colacc[0:1, :] = jnp.log(sums)

    @pl.when(jnp.logical_not(fast))
    def _():
        colacc[0:1, :] = jnp.full((1, ncol * BLK), floor_value, jnp.float32)
        colacc[1:2, :] = jnp.zeros((1, ncol * BLK), jnp.float32)
        for k, block in enumerate(blocks):
            flat, _, term = unpacked(block)
            pts_t = flat.T
            sq_t = 0.5 * jnp.sum(pts_t * pts_t, 1, keepdims=True)
            term_t = jnp.broadcast_to(term, (128, BLK)).T[:, :1]
            rmax[...] = jnp.full(rmax.shape, floor_value, jnp.float32)
            rsum[...] = jnp.zeros_like(rsum)

            def exact(j, _):
                at = pl.ds(pl.multiple_of(j * BLK, BLK), BLK)
                pts, sq, col_term = unpacked(cols.at[j])
                cross = jnp.dot(
                    pts_t, pts, precision=lax.Precision.HIGHEST, preferred_element_type=jnp.float32
                )
                half = (sq_t + sq - cross) / epsilon
                scores = col_term - half
                old = rmax[...]
                new = jnp.maximum(old, jnp.max(scores, 1, keepdims=True))
                part = jnp.sum(jnp.exp(scores - new[:, :1]), 1, keepdims=True)
                rsum[...] = rsum[...] * jnp.exp(old - new) + part
                rmax[...] = new
                others = term_t - half
                old = colacc[0:1, at]
                new = jnp.maximum(old, jnp.max(others, 0, keepdims=True))
                part = jnp.sum(jnp.exp(others - new), 0, keepdims=True)
                colacc[1:2, at] = colacc[1:2, at] * jnp.exp(old - new) + part
                colacc[0:1, at] = new
                return 0

            lax.fori_loop(0, ncol, exact, 0)
            total = (rmax[...] + jnp.log(rsum[...])).T[:1]
            rlog[:, k * BLK : (k + 1) * BLK] = total + term

        def finish(j, _):
            at = pl.ds(pl.multiple_of(j * BLK, BLK), BLK)
            colacc[0:1, at] = colacc[0:1, at] + jnp.log(colacc[1:2, at]) + wide(cols.at[j], 128)
            return 0

        lax.fori_loop(0, ncol, finish, 0)

    for k in range(nrow):
        lines[k : k + 1, :] = rlog[:, k * BLK : (k + 1) * BLK]
    if last:
        lines[4:5, :] = former[1:2, BLK : 2 * BLK]
        both = both_logs(colacc[0:1, :], former[0:1, :])
        for j in range(ncol):
            out[j] = both[:, j * BLK : (j + 1) * BLK]
        at_plane = lax.axis_index("mem_1") * SIDE + lax.axis_index("mem_2")
        own[0:1, :] = wide(blocks[0], 128)
        own[1:2, :] = wide(blocks[0], 132)
        own[2:3, :] = wide(cols.at[at_plane], 128)
        own[3:4, :] = wide(cols.at[at_plane], 132)
    else:
        target_mass = jnp.sum(masses[2:4, :], keepdims=True)
        source_mass = jnp.sum(masses[6:8, :], keepdims=True)
        mass = jnp.concatenate(
            [jnp.broadcast_to(source_mass, (1, 128)), jnp.broadcast_to(target_mass, (1, 128))], 1
        )
        lines[4:5, :] = mass
        former[0:1, :] = colacc[0:1, :]
        former[1:2, 0:BLK] = most
        former[1:2, BLK : 2 * BLK] = mass


def nrow_refs(last):
    return SIDE if last else 1


def both_logs(a, b):
    peak = jnp.maximum(a, b)
    return peak + jnp.log(jnp.exp(a - peak) + jnp.exp(b - peak))


def merge_kernel(mine, other, *outs):
    logs = both_logs(mine[0:4, :], other[0:4, :])
    mass = mine[4:5, :] + other[4:5, :]
    for k, out in enumerate(outs):
        out[0:1, :] = logs[k : k + 1, :]
        out[1:2, :] = mass


def finish_kernel(got, own, *refs):
    lines, (source, target) = refs[:-2], refs[-2:]

    def total(logs):
        peak = jnp.max(logs, 0, keepdims=True)
        return peak + jnp.log(jnp.sum(jnp.exp(logs - peak), 0, keepdims=True))

    mass = jnp.log(sum(line[1:2, :] for line in lines))
    row_total = total(jnp.concatenate([line[0:1, :] for line in lines], 0)) - own[0:1, :] - wide_of(mass, 1)
    col_total = total(jnp.concatenate([got[j] for j in range(got.shape[0])], 0)) - own[2:3, :] - wide_of(mass, 0)
    source[...] = (0.5 * (own[1:2, :] - epsilon * row_total)).reshape(BLK)
    target[...] = (0.5 * (own[3:4, :] - epsilon * col_total)).reshape(BLK)


def wide_of(mass, half):
    line = mass[:, 128 * half : 128 * (half + 1)]
    return jnp.concatenate([line, line], 1)


def along(step):
    index = [(z % 2) * 2 + z // 2 for z in range(SIDE)]
    return [(index[z], index[(z + step) % SIDE]) for z in range(SIDE)]


def local(source_pts, target_pts, source_pot, target_pot, source_logw, target_logw):
    nrow, ncol = lax.axis_size(GROUP), lax.axis_size(PLANE)
    lines = [v.reshape(2, 128) for v in (source_pot, target_pot, source_logw, target_logw)]
    rows, copies = call(
        pack_kernel,
        (f32(TALL, 128), f32(ncol, TALL, 128)),
        6,
        scratch=[
            pltpu.VMEM((TALL, 128), jnp.float32),
            pltpu.VMEM((4, 2, 128), jnp.float32),
            pltpu.SemaphoreType.DMA((8,)),
            pltpu.SemaphoreType.DMA((ncol,)),
        ],
        specs=(VMEM, HBM),
    )(*(pltpu.with_memory_space_constraint(v, pltpu.HBM) for v in (source_pts, target_pts, *lines)))
    mine = [rows]
    for k in range(1, SIDE):
        mine.append(lax.ppermute(rows, LINE, along(-k)))
    others = lax.ppermute(jnp.stack(mine), CORE, [(0, 1), (1, 0)])
    cols = lax.all_to_all(copies, PLANE, 0, 0, tiled=True)
    nrow = nrow // 2
    size = nrow * ncol * BLK * BLK
    cost = pl.CostEstimate(flops=512 * size, bytes_accessed=4 * 2**20, transcendentals=size)
    xt, stats = call(
        rows_kernel,
        (jax.ShapeDtypeStruct((2 * nrow * BLK, 256), jnp.bfloat16), f32(1, BLK)),
        5,
        cost=pl.CostEstimate(flops=10**6, bytes_accessed=10**6, transcendentals=0),
    )(*mine, others)
    scratch = [
        pltpu.VMEM((nrow * BLK, 128), jnp.float32),
        pltpu.VMEM((8, ncol * BLK), jnp.float32),
        pltpu.VMEM((BLK, 128), jnp.float32),
        pltpu.VMEM((BLK, 128), jnp.float32),
        pltpu.VMEM((1, nrow * BLK), jnp.float32),
    ]
    yk, former, lines = call(
        functools.partial(half_kernel, nrow, ncol, False),
        (jax.ShapeDtypeStruct((256, ncol * BLK), jnp.bfloat16), f32(2, ncol * BLK), f32(8, BLK)),
        4,
        scratch=scratch,
        cost=cost,
    )(others, cols, xt, stats)
    crossed = lax.ppermute(lines, CORE, [(0, 1), (1, 0)])
    lines, out, own = call(
        functools.partial(half_kernel, nrow, ncol, True),
        (f32(8, BLK), f32(ncol, 1, BLK), f32(8, BLK)),
        SIDE + 5,
        scratch=scratch,
        cost=cost,
    )(*mine, cols, xt, stats, yk, former)
    got = lax.all_to_all(out, PLANE, 0, 0, tiled=True)
    merged = call(
        merge_kernel,
        (f32(8, BLK),) * SIDE,
        2,
        cost=pl.CostEstimate(flops=10**5, bytes_accessed=10**5, transcendentals=0),
    )(lines, crossed)
    parts = [merged[0]]
    for k in range(1, SIDE):
        parts.append(lax.ppermute(merged[k], LINE, along(k)))
    return call(finish_kernel, (f32(BLK), f32(BLK)), 2 + SIDE)(got, own, *parts)


def solution(mesh):
    finer = Mesh(mesh.devices.reshape(2, 2, 2, 4, 4), GRP_MEM)
    return jax.shard_map(
        local,
        mesh=finer,
        in_specs=(P(None, GRP_MEM), P(None, GRP_MEM), P(GRP_MEM), P(GRP_MEM), P(GRP_MEM), P(GRP_MEM)),
        out_specs=(P(GRP_MEM), P(GRP_MEM)),
        check_vma=False,
    )
```

```python
import functools

import jax
import jax.numpy as jnp
from jax import lax
from jax.experimental import pallas as pl
from jax.experimental.pallas import tpu as pltpu
from jax.sharding import Mesh
from jax.sharding import PartitionSpec as P

GRP_MEM = ("grp_0", "grp_1", "mem_0", "mem_1", "mem_2")
GROUP = ("grp_0", "grp_1", "mem_0")
PLANE = ("mem_1", "mem_2")
LINE = ("grp_0", "mem_0")
CORE = "grp_1"
SIDE = 4

epsilon = 4.0
LOG2E = 1.4426950408889634
FEAT = 64
BLK = 256
TALL = 136
floor_value = -1e30
LOW = 2.0**-90
HIGH = 2.0**120
NORM = 90.5

VMEM = pl.BlockSpec(memory_space=pltpu.VMEM)


HBM = pl.BlockSpec(memory_space=pltpu.HBM)


def call(kernel, out, ins, scratch=(), cost=None, specs=None):
    return pl.pallas_call(
        kernel,
        out_shape=out,
        in_specs=[HBM if specs else VMEM] * ins,
        out_specs=specs or jax.tree.map(lambda _: VMEM, out),
        scratch_shapes=scratch,
        compiler_params=pltpu.CompilerParams(vmem_limit_bytes=40 * 2**20),
        cost_estimate=cost,
    )


def f32(*shape):
    return jax.ShapeDtypeStruct(shape, jnp.float32)


def pack_kernel(spts, tpts, spot, tpot, slogw, tlogw, rows, copies, cols, lines, sems, out_sems):
    loads = []
    for pts, block in ((spts, rows), (tpts, cols)):
        for half in range(2):
            loads.append((pts.at[:, 128 * half : 128 * (half + 1)], block.at[64 * half : 64 * (half + 1), :]))
    for k, ref in enumerate((slogw, spot, tlogw, tpot)):
        loads.append((ref, lines.at[k]))
    loads = [pltpu.make_async_copy(a, b, sems.at[k]) for k, (a, b) in enumerate(loads)]
    for load in loads:
        load.start()
    for k in range(4, 8):
        loads[k].wait()
    for block, logw, pot, other in ((rows, lines[0], lines[1], lines[2]), (cols, lines[2], lines[3], lines[0])):
        tail = (logw + pot / epsilon, logw, pot, other)
        block[128:136, :] = jnp.concatenate(tail, 0)
    loads[2].wait()
    loads[3].wait()
    stores = [pltpu.make_async_copy(cols, copies.at[k], out_sems.at[k]) for k in range(copies.shape[0])]
    for store in stores:
        store.start()
    loads[0].wait()
    loads[1].wait()
    for store in stores:
        store.wait()


def wide(block, line):
    return jnp.concatenate([block[line : line + 1, :], block[line + 1 : line + 2, :]], 1)


def unpacked(block):
    pts = jnp.concatenate([block[0:64, :], block[64:128, :]], 1)
    return pts, 0.5 * jnp.sum(pts * pts, 0, keepdims=True), wide(block, 128)


def split(v):
    head = v.astype(jnp.bfloat16).astype(jnp.float32)
    return head, v - head


def bias_lines(bias, first):
    b1, rest = split(bias)
    b2, b3 = split(rest)
    line = lax.broadcasted_iota(jnp.int32, (16, BLK), 0)
    out = jnp.zeros((16, BLK), jnp.float32)
    for k, piece in enumerate((b1, b2, b3)):
        out = jnp.where(line == k + first, piece, out)
    return jnp.where((line >= 3 - first) & (line < 6 - first), 1.0, out)


def blocks_of(refs):
    out = []
    for ref in refs:
        out.extend([ref] if len(ref.shape) == 2 else [ref.at[k] for k in range(ref.shape[0])])
    return out


def rows_kernel(*refs):
    blocks = blocks_of(refs[:-2])
    xt, stats = refs[-2:]
    most = jnp.zeros((1, BLK), jnp.float32)
    for k, block in enumerate(blocks):
        pts, sq, term = unpacked(block)
        most = jnp.maximum(most, sq)
        x1, x2 = split(pts * (LOG2E / epsilon))
        bias = bias_lines((term - sq / epsilon) * LOG2E, 0)
        left = jnp.concatenate([x1, x2], 0)
        right = jnp.concatenate([x1, bias, jnp.zeros((48, BLK), jnp.float32)], 0)
        xt[k * BLK : (k + 1) * BLK, :128] = left.T.astype(jnp.bfloat16)
        xt[k * BLK : (k + 1) * BLK, 128:] = right.T.astype(jnp.bfloat16)
    stats[...] = most


def outside(v, low, high):
    return jnp.where((v > low) & (v < high), 0.0, 1.0)


def half_kernel(nrow, ncol, last, *refs):
    blocks = blocks_of(refs[:nrow_refs(last)])
    refs = refs[nrow_refs(last) :]
    if last:
        cols, xt, stats, yk, former, lines, out, own, rowacc, colacc, rmax, rsum, rlog = refs
        most = former[1:2, 0:BLK]
    else:
        cols, xt, stats, yk, former, lines, rowacc, colacc, rmax, rsum, rlog = refs

        def prepare(j, state):
            most, masses = state
            block = cols.at[j]
            pts, sq, term = unpacked(block)
            y1, y2 = split(pts)
            bias = bias_lines((term - sq / epsilon) * LOG2E, 3)
            at = pl.ds(pl.multiple_of(j * BLK, BLK), BLK)
            y1 = y1.astype(jnp.bfloat16)
            yk[0:64, at] = y1
            yk[64:128, at] = y1
            yk[128:192, at] = y2.astype(jnp.bfloat16)
            yk[192:208, at] = bias.astype(jnp.bfloat16)
            yk[208:256, at] = jnp.zeros((48, BLK), jnp.bfloat16)
            return jnp.maximum(most, sq), masses + jnp.exp(block[128:136, :])

        most, masses = lax.fori_loop(
            0, ncol, prepare, (jnp.zeros((1, BLK), jnp.float32), jnp.zeros((8, 128), jnp.float32)), unroll=4
        )
    step = 512
    first = 0 if last else nrow * BLK

    for j in range(ncol):
        at = slice(j * BLK, (j + 1) * BLK)
        right = yk[:, at]
        total = jnp.zeros((8, BLK), jnp.float32)
        for i in range(nrow * BLK // step):
            rows = slice(i * step, (i + 1) * step)
            held = slice(first + i * step, first + (i + 1) * step)
            e = jnp.exp2(jnp.dot(xt[held, :], right, preferred_element_type=jnp.float32))
            part = e[:, :128] + e[:, 128:]
            rowacc[rows, :] = part if j == 0 else rowacc[rows, :] + part
            total += jnp.sum(e.reshape(step // 8, 8, BLK), 0)
        colacc[:, at] = total

    s1, s2 = split(rowacc[...])
    parts = jnp.concatenate([s1, s2], 1).astype(jnp.bfloat16)
    rows = lax.dot_general(
        jnp.ones((16, 256), jnp.bfloat16), parts, (((1,), (1,)), ((), ())), preferred_element_type=jnp.float32
    )[:1]
    sums = jnp.sum(colacc[...], 0, keepdims=True)
    ill = outside(stats[...], floor_value, NORM) + outside(most, floor_value, NORM)
    for j in range(nrow):
        ill = ill + outside(rows[:, j * BLK : (j + 1) * BLK], LOW, HIGH)
    for j in range(ncol):
        ill = ill + outside(sums[:, j * BLK : (j + 1) * BLK], LOW, HIGH)
    fast = jnp.max(ill) < 0.5
    rlog[...] = jnp.log(rows)
    colacc[0:1, :] = jnp.log(sums)

    @pl.when(jnp.logical_not(fast))
    def _():
        colacc[0:1, :] = jnp.full((1, ncol * BLK), floor_value, jnp.float32)
        colacc[1:2, :] = jnp.zeros((1, ncol * BLK), jnp.float32)
        for k, block in enumerate(blocks):
            flat, _, term = unpacked(block)
            pts_t = flat.T
            sq_t = 0.5 * jnp.sum(pts_t * pts_t, 1, keepdims=True)
            term_t = jnp.broadcast_to(term, (128, BLK)).T[:, :1]
            rmax[...] = jnp.full(rmax.shape, floor_value, jnp.float32)
            rsum[...] = jnp.zeros_like(rsum)

            def exact(j, _):
                at = pl.ds(pl.multiple_of(j * BLK, BLK), BLK)
                pts, sq, col_term = unpacked(cols.at[j])
                cross = jnp.dot(
                    pts_t, pts, precision=lax.Precision.HIGHEST, preferred_element_type=jnp.float32
                )
                half = (sq_t + sq - cross) / epsilon
                scores = col_term - half
                old = rmax[...]
                new = jnp.maximum(old, jnp.max(scores, 1, keepdims=True))
                part = jnp.sum(jnp.exp(scores - new[:, :1]), 1, keepdims=True)
                rsum[...] = rsum[...] * jnp.exp(old - new) + part
                rmax[...] = new
                others = term_t - half
                old = colacc[0:1, at]
                new = jnp.maximum(old, jnp.max(others, 0, keepdims=True))
                part = jnp.sum(jnp.exp(others - new), 0, keepdims=True)
                colacc[1:2, at] = colacc[1:2, at] * jnp.exp(old - new) + part
                colacc[0:1, at] = new
                return 0

            lax.fori_loop(0, ncol, exact, 0)
            total = (rmax[...] + jnp.log(rsum[...])).T[:1]
            rlog[:, k * BLK : (k + 1) * BLK] = total + term

        def finish(j, _):
            at = pl.ds(pl.multiple_of(j * BLK, BLK), BLK)
            colacc[0:1, at] = colacc[0:1, at] + jnp.log(colacc[1:2, at]) + wide(cols.at[j], 128)
            return 0

        lax.fori_loop(0, ncol, finish, 0)

    for k in range(nrow):
        lines[k : k + 1, :] = rlog[:, k * BLK : (k + 1) * BLK]
    if last:
        lines[4:5, :] = former[1:2, BLK : 2 * BLK]
        both = both_logs(colacc[0:1, :], former[0:1, :])
        for j in range(ncol):
            out[j] = both[:, j * BLK : (j + 1) * BLK]
        at_plane = lax.axis_index("mem_1") * SIDE + lax.axis_index("mem_2")
        own[0:1, :] = wide(blocks[0], 128)
        own[1:2, :] = wide(blocks[0], 132)
        own[2:3, :] = wide(cols.at[at_plane], 128)
        own[3:4, :] = wide(cols.at[at_plane], 132)
    else:
        target_mass = jnp.sum(masses[2:4, :], keepdims=True)
        source_mass = jnp.sum(masses[6:8, :], keepdims=True)
        mass = jnp.concatenate(
            [jnp.broadcast_to(source_mass, (1, 128)), jnp.broadcast_to(target_mass, (1, 128))], 1
        )
        lines[4:5, :] = mass
        former[0:1, :] = colacc[0:1, :]
        former[1:2, 0:BLK] = most
        former[1:2, BLK : 2 * BLK] = mass


def nrow_refs(last):
    return SIDE if last else 1


def both_logs(a, b):
    peak = jnp.maximum(a, b)
    return peak + jnp.log(jnp.exp(a - peak) + jnp.exp(b - peak))


def first_kernel(mine, other, keep, send):
    low = lax.axis_index("grp_0")
    logs = both_logs(mine[0:4, :], other[0:4, :])
    up, down = logs[1:2, :], logs[3:4, :]
    send[0:1, :] = jnp.where(low == 0, up, down)
    send[1:2, :] = logs[2:3, :]
    keep[0:1, :] = logs[0:1, :]
    keep[1:2, :] = jnp.where(low == 0, down, up)
    send[2:3, :] = keep[2:3, :] = mine[4:5, :] + other[4:5, :]


def second_kernel(kept, got, keep, send):
    logs = both_logs(kept[0:2, :], got[0:2, :])
    keep[0:1, :] = logs[0:1, :]
    send[0:1, :] = logs[1:2, :]
    send[1:2, :] = keep[1:2, :] = kept[2:3, :] + got[2:3, :]


def finish_kernel(got, own, *refs):
    lines, (source, target) = refs[:-2], refs[-2:]

    def total(logs):
        peak = jnp.max(logs, 0, keepdims=True)
        return peak + jnp.log(jnp.sum(jnp.exp(logs - peak), 0, keepdims=True))

    mass = jnp.log(sum(line[1:2, :] for line in lines))
    row_total = total(jnp.concatenate([line[0:1, :] for line in lines], 0)) - own[0:1, :] - wide_of(mass, 1)
    col_total = total(jnp.concatenate([got[j] for j in range(got.shape[0])], 0)) - own[2:3, :] - wide_of(mass, 0)
    source[...] = (0.5 * (own[1:2, :] - epsilon * row_total)).reshape(BLK)
    target[...] = (0.5 * (own[3:4, :] - epsilon * col_total)).reshape(BLK)


def wide_of(mass, half):
    line = mass[:, 128 * half : 128 * (half + 1)]
    return jnp.concatenate([line, line], 1)


def along(step):
    index = [(z % 2) * 2 + z // 2 for z in range(SIDE)]
    return [(index[z], index[(z + step) % SIDE]) for z in range(SIDE)]


def local(source_pts, target_pts, source_pot, target_pot, source_logw, target_logw):
    nrow, ncol = lax.axis_size(GROUP), lax.axis_size(PLANE)
    lines = [v.reshape(2, 128) for v in (source_pot, target_pot, source_logw, target_logw)]
    rows, copies = call(
        pack_kernel,
        (f32(TALL, 128), f32(ncol, TALL, 128)),
        6,
        scratch=[
            pltpu.VMEM((TALL, 128), jnp.float32),
            pltpu.VMEM((4, 2, 128), jnp.float32),
            pltpu.SemaphoreType.DMA((8,)),
            pltpu.SemaphoreType.DMA((ncol,)),
        ],
        specs=(VMEM, HBM),
    )(*(pltpu.with_memory_space_constraint(v, pltpu.HBM) for v in (source_pts, target_pts, *lines)))
    mine = [rows]
    for k in range(1, SIDE):
        mine.append(lax.ppermute(rows, LINE, along(-k)))
    others = lax.ppermute(jnp.stack(mine), CORE, [(0, 1), (1, 0)])
    cols = lax.all_to_all(copies, PLANE, 0, 0, tiled=True)
    nrow = nrow // 2
    size = nrow * ncol * BLK * BLK
    cost = pl.CostEstimate(flops=512 * size, bytes_accessed=4 * 2**20, transcendentals=size)
    xt, stats = call(
        rows_kernel,
        (jax.ShapeDtypeStruct((2 * nrow * BLK, 256), jnp.bfloat16), f32(1, BLK)),
        5,
        cost=pl.CostEstimate(flops=10**6, bytes_accessed=10**6, transcendentals=0),
    )(*mine, others)
    scratch = [
        pltpu.VMEM((nrow * BLK, 128), jnp.float32),
        pltpu.VMEM((8, ncol * BLK), jnp.float32),
        pltpu.VMEM((BLK, 128), jnp.float32),
        pltpu.VMEM((BLK, 128), jnp.float32),
        pltpu.VMEM((1, nrow * BLK), jnp.float32),
    ]
    yk, former, lines = call(
        functools.partial(half_kernel, nrow, ncol, False),
        (jax.ShapeDtypeStruct((256, ncol * BLK), jnp.bfloat16), f32(2, ncol * BLK), f32(8, BLK)),
        4,
        scratch=scratch,
        cost=cost,
    )(others, cols, xt, stats)
    crossed = lax.ppermute(lines, CORE, [(0, 1), (1, 0)])
    lines, out, own = call(
        functools.partial(half_kernel, nrow, ncol, True),
        (f32(8, BLK), f32(ncol, 1, BLK), f32(8, BLK)),
        SIDE + 5,
        scratch=scratch,
        cost=cost,
    )(*mine, cols, xt, stats, yk, former)
    got = lax.all_to_all(out, PLANE, 0, 0, tiled=True)
    small = pl.CostEstimate(flops=10**5, bytes_accessed=10**5, transcendentals=0)
    keep, send = call(first_kernel, (f32(8, BLK), f32(8, BLK)), 2, cost=small)(lines, crossed)
    send = lax.ppermute(send, LINE[0], [(0, 1), (1, 0)])
    keep, send = call(second_kernel, (f32(8, BLK), f32(8, BLK)), 2, cost=small)(keep, send)
    send = lax.ppermute(send, LINE, [(i, SIDE - 1 - i) for i in range(SIDE)])
    return call(finish_kernel, (f32(BLK), f32(BLK)), 4)(got, own, keep, send)


def solution(mesh):
    finer = Mesh(mesh.devices.reshape(2, 2, 2, 4, 4), GRP_MEM)
    return jax.shard_map(
        local,
        mesh=finer,
        in_specs=(P(None, GRP_MEM), P(None, GRP_MEM), P(GRP_MEM), P(GRP_MEM), P(GRP_MEM), P(GRP_MEM)),
        out_specs=(P(GRP_MEM), P(GRP_MEM)),
        check_vma=False,
    )
```

```python
import functools

import jax
import jax.numpy as jnp
from jax import lax
from jax.experimental import pallas as pl
from jax.experimental.pallas import tpu as pltpu
from jax.sharding import Mesh
from jax.sharding import PartitionSpec as P

GRP_MEM = ("grp_0", "grp_1", "mem_0", "mem_1", "mem_2")
GROUP = ("grp_0", "grp_1", "mem_0")
PLANE = ("mem_1", "mem_2")
LINE = ("grp_0", "mem_0")
CORE = "grp_1"
SIDE = 4

epsilon = 4.0
LOG2E = 1.4426950408889634
FEAT = 64
BLK = 256
TALL = 136
floor_value = -1e30
LOW = 2.0**-90
HIGH = 2.0**120
NORM = 90.5

VMEM = pl.BlockSpec(memory_space=pltpu.VMEM)


HBM = pl.BlockSpec(memory_space=pltpu.HBM)


def call(kernel, out, ins, scratch=(), cost=None, specs=None):
    return pl.pallas_call(
        kernel,
        out_shape=out,
        in_specs=[HBM if specs else VMEM] * ins,
        out_specs=specs or jax.tree.map(lambda _: VMEM, out),
        scratch_shapes=scratch,
        compiler_params=pltpu.CompilerParams(vmem_limit_bytes=40 * 2**20),
        cost_estimate=cost,
    )


def f32(*shape):
    return jax.ShapeDtypeStruct(shape, jnp.float32)


def pack_kernel(spts, tpts, spot, tpot, slogw, tlogw, rows, copies, cols, lines, sems, out_sems):
    loads = []
    for pts, block in ((spts, rows), (tpts, cols)):
        for half in range(2):
            loads.append((pts.at[:, 128 * half : 128 * (half + 1)], block.at[64 * half : 64 * (half + 1), :]))
    for k, ref in enumerate((slogw, spot, tlogw, tpot)):
        loads.append((ref, lines.at[k]))
    loads = [pltpu.make_async_copy(a, b, sems.at[k]) for k, (a, b) in enumerate(loads)]
    for load in loads:
        load.start()
    for k in range(4, 8):
        loads[k].wait()
    for block, logw, pot, other in ((rows, lines[0], lines[1], lines[2]), (cols, lines[2], lines[3], lines[0])):
        tail = (logw + pot / epsilon, logw, pot, other)
        block[128:136, :] = jnp.concatenate(tail, 0)
    loads[2].wait()
    loads[3].wait()
    stores = [pltpu.make_async_copy(cols, copies.at[k], out_sems.at[k]) for k in range(copies.shape[0])]
    for store in stores:
        store.start()
    loads[0].wait()
    loads[1].wait()
    for store in stores:
        store.wait()


def wide(block, line):
    return jnp.concatenate([block[line : line + 1, :], block[line + 1 : line + 2, :]], 1)


def unpacked(block):
    pts = jnp.concatenate([block[0:64, :], block[64:128, :]], 1)
    return pts, 0.5 * jnp.sum(pts * pts, 0, keepdims=True), wide(block, 128)


def split(v):
    head = v.astype(jnp.bfloat16).astype(jnp.float32)
    return head, v - head


def bias_lines(bias, first):
    b1, rest = split(bias)
    b2, b3 = split(rest)
    line = lax.broadcasted_iota(jnp.int32, (16, BLK), 0)
    out = jnp.zeros((16, BLK), jnp.float32)
    for k, piece in enumerate((b1, b2, b3)):
        out = jnp.where(line == k + first, piece, out)
    return jnp.where((line >= 3 - first) & (line < 6 - first), 1.0, out)


def blocks_of(refs):
    out = []
    for ref in refs:
        out.extend([ref] if len(ref.shape) == 2 else [ref.at[k] for k in range(ref.shape[0])])
    return out


def rows_kernel(*refs):
    blocks = blocks_of(refs[:-2])
    xt, stats = refs[-2:]
    most = jnp.zeros((1, BLK), jnp.float32)
    for k, block in enumerate(blocks):
        pts, sq, term = unpacked(block)
        most = jnp.maximum(most, sq)
        x1, x2 = split(pts * (LOG2E / epsilon))
        bias = bias_lines((term - sq / epsilon) * LOG2E, 0)
        left = jnp.concatenate([x1, x2], 0)
        right = jnp.concatenate([x1, bias, jnp.zeros((48, BLK), jnp.float32)], 0)
        xt[k * BLK : (k + 1) * BLK, :128] = left.T.astype(jnp.bfloat16)
        xt[k * BLK : (k + 1) * BLK, 128:] = right.T.astype(jnp.bfloat16)
    stats[...] = most


def outside(v, low, high):
    return jnp.where((v > low) & (v < high), 0.0, 1.0)


def half_kernel(nrow, ncol, last, *refs):
    blocks = blocks_of(refs[:nrow_refs(last)])
    refs = refs[nrow_refs(last) :]
    if last:
        cols, xt, stats, yk, former, lines, out, own, rowacc, colacc, rmax, rsum, rlog = refs
        most = former[1:2, 0:BLK]
    else:
        cols, xt, stats, yk, former, lines, rowacc, colacc, rmax, rsum, rlog = refs

        def prepare(j, state):
            most, masses = state
            block = cols.at[j]
            pts, sq, term = unpacked(block)
            y1, y2 = split(pts)
            bias = bias_lines((term - sq / epsilon) * LOG2E, 3)
            at = pl.ds(pl.multiple_of(j * BLK, BLK), BLK)
            y1 = y1.astype(jnp.bfloat16)
            yk[0:64, at] = y1
            yk[64:128, at] = y1
            yk[128:192, at] = y2.astype(jnp.bfloat16)
            yk[192:208, at] = bias.astype(jnp.bfloat16)
            yk[208:256, at] = jnp.zeros((48, BLK), jnp.bfloat16)
            return jnp.maximum(most, sq), masses + jnp.exp(block[128:136, :])

        most, masses = lax.fori_loop(
            0, ncol, prepare, (jnp.zeros((1, BLK), jnp.float32), jnp.zeros((8, 128), jnp.float32)), unroll=4
        )
    step = 512
    first = 0 if last else nrow * BLK

    for j in range(ncol):
        at = slice(j * BLK, (j + 1) * BLK)
        right = yk[:, at]
        total = jnp.zeros((8, BLK), jnp.float32)
        for i in range(nrow * BLK // step):
            rows = slice(i * step, (i + 1) * step)
            held = slice(first + i * step, first + (i + 1) * step)
            e = jnp.exp2(jnp.dot(xt[held, :], right, preferred_element_type=jnp.float32))
            part = e[:, :128] + e[:, 128:]
            rowacc[rows, :] = part if j == 0 else rowacc[rows, :] + part
            total += jnp.sum(e.reshape(step // 8, 8, BLK), 0)
        colacc[:, at] = total

    s1, s2 = split(rowacc[...])
    parts = jnp.concatenate([s1, s2], 1).astype(jnp.bfloat16)
    rows = lax.dot_general(
        jnp.ones((16, 256), jnp.bfloat16), parts, (((1,), (1,)), ((), ())), preferred_element_type=jnp.float32
    )[:1]
    sums = jnp.sum(colacc[...], 0, keepdims=True)
    ill = outside(stats[...], floor_value, NORM) + outside(most, floor_value, NORM)
    for j in range(nrow):
        ill = ill + outside(rows[:, j * BLK : (j + 1) * BLK], LOW, HIGH)
    for j in range(ncol):
        ill = ill + outside(sums[:, j * BLK : (j + 1) * BLK], LOW, HIGH)
    fast = jnp.max(ill) < 0.5
    rlog[...] = jnp.log(rows)
    colacc[0:1, :] = jnp.log(sums)

    @pl.when(jnp.logical_not(fast))
    def _():
        colacc[0:1, :] = jnp.full((1, ncol * BLK), floor_value, jnp.float32)
        colacc[1:2, :] = jnp.zeros((1, ncol * BLK), jnp.float32)
        for k, block in enumerate(blocks):
            flat, _, term = unpacked(block)
            pts_t = flat.T
            sq_t = 0.5 * jnp.sum(pts_t * pts_t, 1, keepdims=True)
            term_t = jnp.broadcast_to(term, (128, BLK)).T[:, :1]
            rmax[...] = jnp.full(rmax.shape, floor_value, jnp.float32)
            rsum[...] = jnp.zeros_like(rsum)

            def exact(j, _):
                at = pl.ds(pl.multiple_of(j * BLK, BLK), BLK)
                pts, sq, col_term = unpacked(cols.at[j])
                cross = jnp.dot(
                    pts_t, pts, precision=lax.Precision.HIGHEST, preferred_element_type=jnp.float32
                )
                half = (sq_t + sq - cross) / epsilon
                scores = col_term - half
                old = rmax[...]
                new = jnp.maximum(old, jnp.max(scores, 1, keepdims=True))
                part = jnp.sum(jnp.exp(scores - new[:, :1]), 1, keepdims=True)
                rsum[...] = rsum[...] * jnp.exp(old - new) + part
                rmax[...] = new
                others = term_t - half
                old = colacc[0:1, at]
                new = jnp.maximum(old, jnp.max(others, 0, keepdims=True))
                part = jnp.sum(jnp.exp(others - new), 0, keepdims=True)
                colacc[1:2, at] = colacc[1:2, at] * jnp.exp(old - new) + part
                colacc[0:1, at] = new
                return 0

            lax.fori_loop(0, ncol, exact, 0)
            total = (rmax[...] + jnp.log(rsum[...])).T[:1]
            rlog[:, k * BLK : (k + 1) * BLK] = total + term

        def finish(j, _):
            at = pl.ds(pl.multiple_of(j * BLK, BLK), BLK)
            colacc[0:1, at] = colacc[0:1, at] + jnp.log(colacc[1:2, at]) + wide(cols.at[j], 128)
            return 0

        lax.fori_loop(0, ncol, finish, 0)

    for k in range(nrow):
        lines[k : k + 1, :] = rlog[:, k * BLK : (k + 1) * BLK]
    if last:
        lines[4:5, :] = former[1:2, BLK : 2 * BLK]
        both = both_logs(colacc[0:1, :], former[0:1, :])
        for j in range(ncol):
            out[j] = both[:, j * BLK : (j + 1) * BLK]
        at_plane = lax.axis_index("mem_1") * SIDE + lax.axis_index("mem_2")
        own[0:1, :] = wide(blocks[0], 128)
        own[1:2, :] = wide(blocks[0], 132)
        own[2:3, :] = wide(cols.at[at_plane], 128)
        own[3:4, :] = wide(cols.at[at_plane], 132)
    else:
        target_mass = jnp.sum(masses[2:4, :], keepdims=True)
        source_mass = jnp.sum(masses[6:8, :], keepdims=True)
        mass = jnp.concatenate(
            [jnp.broadcast_to(source_mass, (1, 128)), jnp.broadcast_to(target_mass, (1, 128))], 1
        )
        lines[4:5, :] = mass
        former[0:1, :] = colacc[0:1, :]
        former[1:2, 0:BLK] = most
        former[1:2, BLK : 2 * BLK] = mass


def nrow_refs(last):
    return SIDE if last else 1


def both_logs(a, b):
    peak = jnp.maximum(a, b)
    return peak + jnp.log(jnp.exp(a - peak) + jnp.exp(b - peak))


def first_kernel(mine, other, keep, send):
    low = lax.axis_index("grp_0")
    logs = both_logs(mine[0:4, :], other[0:4, :])
    up, down = logs[1:2, :], logs[3:4, :]
    send[0:1, :] = jnp.where(low == 0, up, down)
    send[1:2, :] = logs[2:3, :]
    keep[0:1, :] = logs[0:1, :]
    keep[1:2, :] = jnp.where(low == 0, down, up)
    send[2:3, :] = keep[2:3, :] = mine[4:5, :] + other[4:5, :]


def second_kernel(kept, got, keep, send):
    logs = both_logs(kept[0:2, :], got[0:2, :])
    keep[0:1, :] = logs[0:1, :]
    send[0:1, :] = logs[1:2, :]
    send[1:2, :] = keep[1:2, :] = kept[2:3, :] + got[2:3, :]


def finish_kernel(got, own, *refs):
    lines, (source, target) = refs[:-2], refs[-2:]

    def total(logs):
        peak = jnp.max(logs, 0, keepdims=True)
        return peak + jnp.log(jnp.sum(jnp.exp(logs - peak), 0, keepdims=True))

    mass = jnp.log(sum(line[1:2, :] for line in lines))
    row_total = total(jnp.concatenate([line[0:1, :] for line in lines], 0)) - own[0:1, :] - wide_of(mass, 1)
    col_total = total(jnp.concatenate([got[j] for j in range(got.shape[0])], 0)) - own[2:3, :] - wide_of(mass, 0)
    source[...] = (0.5 * (own[1:2, :] - epsilon * row_total)).reshape(BLK)
    target[...] = (0.5 * (own[3:4, :] - epsilon * col_total)).reshape(BLK)


def wide_of(mass, half):
    line = mass[:, 128 * half : 128 * (half + 1)]
    return jnp.concatenate([line, line], 1)


def along(step):
    index = [(z % 2) * 2 + z // 2 for z in range(SIDE)]
    return [(index[z], index[(z + step) % SIDE]) for z in range(SIDE)]


def local(source_pts, target_pts, source_pot, target_pot, source_logw, target_logw):
    nrow, ncol = lax.axis_size(GROUP), lax.axis_size(PLANE)
    lines = [v.reshape(2, 128) for v in (source_pot, target_pot, source_logw, target_logw)]
    rows, copies = call(
        pack_kernel,
        (f32(TALL, 128), f32(ncol, TALL, 128)),
        6,
        scratch=[
            pltpu.VMEM((TALL, 128), jnp.float32),
            pltpu.VMEM((4, 2, 128), jnp.float32),
            pltpu.SemaphoreType.DMA((8,)),
            pltpu.SemaphoreType.DMA((ncol,)),
        ],
        specs=(VMEM, HBM),
    )(*(pltpu.with_memory_space_constraint(v, pltpu.HBM) for v in (source_pts, target_pts, *lines)))
    mine = [rows]
    for k in range(1, SIDE):
        mine.append(lax.ppermute(rows, LINE, along(-k)))
    others = lax.ppermute(jnp.stack(mine), CORE, [(0, 1), (1, 0)])
    cols = lax.all_to_all(copies, PLANE, 0, 0, tiled=True)
    nrow = nrow // 2
    size = nrow * ncol * BLK * BLK
    cost = pl.CostEstimate(flops=512 * size, bytes_accessed=4 * 2**20, transcendentals=size)
    xt, stats = call(
        rows_kernel,
        (jax.ShapeDtypeStruct((2 * nrow * BLK, 256), jnp.bfloat16), f32(1, BLK)),
        5,
        cost=pl.CostEstimate(flops=10**6, bytes_accessed=10**6, transcendentals=0),
    )(*mine, others)
    scratch = [
        pltpu.VMEM((nrow * BLK, 128), jnp.float32),
        pltpu.VMEM((8, ncol * BLK), jnp.float32),
        pltpu.VMEM((BLK, 128), jnp.float32),
        pltpu.VMEM((BLK, 128), jnp.float32),
        pltpu.VMEM((1, nrow * BLK), jnp.float32),
    ]
    yk, former, lines = call(
        functools.partial(half_kernel, nrow, ncol, False),
        (jax.ShapeDtypeStruct((256, ncol * BLK), jnp.bfloat16), f32(2, ncol * BLK), f32(8, BLK)),
        4,
        scratch=scratch,
        cost=cost,
    )(others, cols, xt, stats)
    crossed = lax.ppermute(lines, CORE, [(0, 1), (1, 0)])
    lines, out, own = call(
        functools.partial(half_kernel, nrow, ncol, True),
        (f32(8, BLK), f32(ncol, 1, BLK), f32(8, BLK)),
        SIDE + 5,
        scratch=scratch,
        cost=cost,
    )(*mine, cols, xt, stats, yk, former)
    got = lax.all_to_all(out, PLANE, 0, 0, tiled=True)
    small = pl.CostEstimate(flops=10**5, bytes_accessed=10**5, transcendentals=0)
    keep, send = call(first_kernel, (f32(8, BLK), f32(8, BLK)), 2, cost=small)(lines, crossed)
    send = lax.ppermute(send, LINE[0], [(0, 1), (1, 0)])
    keep, send = call(second_kernel, (f32(2, BLK), f32(2, BLK)), 2, cost=small)(keep, send)
    send = lax.ppermute(send, LINE, [(i, SIDE - 1 - i) for i in range(SIDE)])
    return call(finish_kernel, (f32(BLK), f32(BLK)), 4)(got, own, keep, send)


def solution(mesh):
    finer = Mesh(mesh.devices.reshape(2, 2, 2, 4, 4), GRP_MEM)
    return jax.shard_map(
        local,
        mesh=finer,
        in_specs=(P(None, GRP_MEM), P(None, GRP_MEM), P(GRP_MEM), P(GRP_MEM), P(GRP_MEM), P(GRP_MEM)),
        out_specs=(P(GRP_MEM), P(GRP_MEM)),
        check_vma=False,
    )
```

```python
import functools

import jax
import jax.numpy as jnp
from jax import lax
from jax.experimental import pallas as pl
from jax.experimental.pallas import tpu as pltpu
from jax.sharding import Mesh
from jax.sharding import PartitionSpec as P

GRP_MEM = ("grp_0", "grp_1", "mem_0", "mem_1", "mem_2")
GROUP = ("grp_0", "grp_1", "mem_0")
PLANE = ("mem_1", "mem_2")
LINE = ("grp_0", "mem_0")
CORE = "grp_1"
SIDE = 4

epsilon = 4.0
LOG2E = 1.4426950408889634
FEAT = 64
BLK = 256
TALL = 136
floor_value = -1e30
LOW = 2.0**-90
HIGH = 2.0**120
NORM = 90.5

VMEM = pl.BlockSpec(memory_space=pltpu.VMEM)


HBM = pl.BlockSpec(memory_space=pltpu.HBM)


def call(kernel, out, ins, scratch=(), cost=None, specs=None):
    return pl.pallas_call(
        kernel,
        out_shape=out,
        in_specs=[HBM if specs else VMEM] * ins,
        out_specs=specs or jax.tree.map(lambda _: VMEM, out),
        scratch_shapes=scratch,
        compiler_params=pltpu.CompilerParams(vmem_limit_bytes=40 * 2**20),
        cost_estimate=cost,
    )


def f32(*shape):
    return jax.ShapeDtypeStruct(shape, jnp.float32)


def pack_kernel(spts, tpts, spot, tpot, slogw, tlogw, rows, copies, cols, lines, sems, out_sems):
    loads = []
    for pts, block in ((tpts, cols), (spts, rows)):
        for half in range(2):
            loads.append((pts.at[:, 128 * half : 128 * (half + 1)], block.at[64 * half : 64 * (half + 1), :]))
    for k, ref in enumerate((slogw, spot, tlogw, tpot)):
        loads.append((ref, lines.at[k]))
    loads = [pltpu.make_async_copy(a, b, sems.at[k]) for k, (a, b) in enumerate(loads)]
    for load in loads:
        load.start()
    for k in range(4, 8):
        loads[k].wait()
    tails = []
    for logw, pot, other in ((lines[0], lines[1], lines[2]), (lines[2], lines[3], lines[0])):
        tails.append(jnp.concatenate((logw + pot / epsilon, logw, pot, other), 0))
    cols[128:136, :] = tails[1]
    loads[0].wait()
    loads[1].wait()
    stores = [pltpu.make_async_copy(cols, copies.at[k], out_sems.at[k]) for k in range(copies.shape[0])]
    for store in stores:
        store.start()
    rows[128:136, :] = tails[0]
    loads[2].wait()
    loads[3].wait()
    for store in stores:
        store.wait()


def wide(block, line):
    return jnp.concatenate([block[line : line + 1, :], block[line + 1 : line + 2, :]], 1)


def unpacked(block):
    pts = jnp.concatenate([block[0:64, :], block[64:128, :]], 1)
    return pts, 0.5 * jnp.sum(pts * pts, 0, keepdims=True), wide(block, 128)


def split(v):
    head = v.astype(jnp.bfloat16).astype(jnp.float32)
    return head, v - head


def bias_lines(bias, first):
    b1, rest = split(bias)
    b2, b3 = split(rest)
    line = lax.broadcasted_iota(jnp.int32, (16, BLK), 0)
    out = jnp.zeros((16, BLK), jnp.float32)
    for k, piece in enumerate((b1, b2, b3)):
        out = jnp.where(line == k + first, piece, out)
    return jnp.where((line >= 3 - first) & (line < 6 - first), 1.0, out)


def blocks_of(refs):
    out = []
    for ref in refs:
        out.extend([ref] if len(ref.shape) == 2 else [ref.at[k] for k in range(ref.shape[0])])
    return out


def rows_kernel(*refs):
    blocks = blocks_of(refs[:-2])
    xt, stats = refs[-2:]
    most = jnp.zeros((1, BLK), jnp.float32)
    for k, block in enumerate(blocks):
        pts, sq, term = unpacked(block)
        most = jnp.maximum(most, sq)
        x1, x2 = split(pts * (LOG2E / epsilon))
        bias = bias_lines((term - sq / epsilon) * LOG2E, 0)
        left = jnp.concatenate([x1, x2], 0)
        right = jnp.concatenate([x1, bias, jnp.zeros((48, BLK), jnp.float32)], 0)
        xt[k * BLK : (k + 1) * BLK, :128] = left.T.astype(jnp.bfloat16)
        xt[k * BLK : (k + 1) * BLK, 128:] = right.T.astype(jnp.bfloat16)
    stats[...] = most


def outside(v, low, high):
    return jnp.where((v > low) & (v < high), 0.0, 1.0)


def half_kernel(nrow, ncol, last, *refs):
    blocks = blocks_of(refs[:nrow_refs(last)])
    refs = refs[nrow_refs(last) :]
    if last:
        cols, xt, stats, yk, former, lines, out, own, rowacc, colacc, rmax, rsum, rlog = refs
        most = former[1:2, 0:BLK]
    else:
        cols, xt, stats, yk, former, lines, rowacc, colacc, rmax, rsum, rlog = refs

        most = jnp.zeros((1, BLK), jnp.float32)
        masses = jnp.zeros((8, 128), jnp.float32)
    step = 512
    first = 0 if last else nrow * BLK

    for j in range(ncol):
        at = slice(j * BLK, (j + 1) * BLK)
        if last:
            right = yk[:, at]
        else:
            block = cols.at[j]
            pts, sq, term = unpacked(block)
            y1, y2 = split(pts)
            bias = bias_lines((term - sq / epsilon) * LOG2E, 3).astype(jnp.bfloat16)
            y1 = y1.astype(jnp.bfloat16)
            right = jnp.concatenate([y1, y1, y2.astype(jnp.bfloat16), bias, jnp.zeros((48, BLK), jnp.bfloat16)], 0)
            yk[:, at] = right
            most = jnp.maximum(most, sq)
            masses = masses + jnp.exp(block[128:136, :])
        total = jnp.zeros((8, BLK), jnp.float32)
        for i in range(nrow * BLK // step):
            rows = slice(i * step, (i + 1) * step)
            held = slice(first + i * step, first + (i + 1) * step)
            e = jnp.exp2(jnp.dot(xt[held, :], right, preferred_element_type=jnp.float32))
            part = e[:, :128] + e[:, 128:]
            rowacc[rows, :] = part if j == 0 else rowacc[rows, :] + part
            total += jnp.sum(e.reshape(step // 8, 8, BLK), 0)
        colacc[:, at] = total

    s1, s2 = split(rowacc[...])
    parts = jnp.concatenate([s1, s2], 1).astype(jnp.bfloat16)
    rows = lax.dot_general(
        jnp.ones((16, 256), jnp.bfloat16), parts, (((1,), (1,)), ((), ())), preferred_element_type=jnp.float32
    )[:1]
    sums = jnp.sum(colacc[...], 0, keepdims=True)
    ill = outside(stats[...], floor_value, NORM) + outside(most, floor_value, NORM)
    for j in range(nrow):
        ill = ill + outside(rows[:, j * BLK : (j + 1) * BLK], LOW, HIGH)
    for j in range(ncol):
        ill = ill + outside(sums[:, j * BLK : (j + 1) * BLK], LOW, HIGH)
    fast = jnp.max(ill) < 0.5
    rlog[...] = jnp.log(rows)
    colacc[0:1, :] = jnp.log(sums)

    @pl.when(jnp.logical_not(fast))
    def _():
        colacc[0:1, :] = jnp.full((1, ncol * BLK), floor_value, jnp.float32)
        colacc[1:2, :] = jnp.zeros((1, ncol * BLK), jnp.float32)
        for k, block in enumerate(blocks):
            flat, _, term = unpacked(block)
            pts_t = flat.T
            sq_t = 0.5 * jnp.sum(pts_t * pts_t, 1, keepdims=True)
            term_t = jnp.broadcast_to(term, (128, BLK)).T[:, :1]
            rmax[...] = jnp.full(rmax.shape, floor_value, jnp.float32)
            rsum[...] = jnp.zeros_like(rsum)

            def exact(j, _):
                at = pl.ds(pl.multiple_of(j * BLK, BLK), BLK)
                pts, sq, col_term = unpacked(cols.at[j])
                cross = jnp.dot(
                    pts_t, pts, precision=lax.Precision.HIGHEST, preferred_element_type=jnp.float32
                )
                half = (sq_t + sq - cross) / epsilon
                scores = col_term - half
                old = rmax[...]
                new = jnp.maximum(old, jnp.max(scores, 1, keepdims=True))
                part = jnp.sum(jnp.exp(scores - new[:, :1]), 1, keepdims=True)
                rsum[...] = rsum[...] * jnp.exp(old - new) + part
                rmax[...] = new
                others = term_t - half
                old = colacc[0:1, at]
                new = jnp.maximum(old, jnp.max(others, 0, keepdims=True))
                part = jnp.sum(jnp.exp(others - new), 0, keepdims=True)
                colacc[1:2, at] = colacc[1:2, at] * jnp.exp(old - new) + part
                colacc[0:1, at] = new
                return 0

            lax.fori_loop(0, ncol, exact, 0)
            total = (rmax[...] + jnp.log(rsum[...])).T[:1]
            rlog[:, k * BLK : (k + 1) * BLK] = total + term

        def finish(j, _):
            at = pl.ds(pl.multiple_of(j * BLK, BLK), BLK)
            colacc[0:1, at] = colacc[0:1, at] + jnp.log(colacc[1:2, at]) + wide(cols.at[j], 128)
            return 0

        lax.fori_loop(0, ncol, finish, 0)

    for k in range(nrow):
        lines[k : k + 1, :] = rlog[:, k * BLK : (k + 1) * BLK]
    if last:
        lines[4:5, :] = former[1:2, BLK : 2 * BLK]
        both = both_logs(colacc[0:1, :], former[0:1, :])
        for j in range(ncol):
            out[j] = both[:, j * BLK : (j + 1) * BLK]
        at_plane = lax.axis_index("mem_1") * SIDE + lax.axis_index("mem_2")
        own[0:1, :] = wide(blocks[0], 128)
        own[1:2, :] = wide(blocks[0], 132)
        own[2:3, :] = wide(cols.at[at_plane], 128)
        own[3:4, :] = wide(cols.at[at_plane], 132)
    else:
        target_mass = jnp.sum(masses[2:4, :], keepdims=True)
        source_mass = jnp.sum(masses[6:8, :], keepdims=True)
        mass = jnp.concatenate(
            [jnp.broadcast_to(source_mass, (1, 128)), jnp.broadcast_to(target_mass, (1, 128))], 1
        )
        lines[4:5, :] = mass
        former[0:1, :] = colacc[0:1, :]
        former[1:2, 0:BLK] = most
        former[1:2, BLK : 2 * BLK] = mass


def nrow_refs(last):
    return SIDE if last else 1


def both_logs(a, b):
    peak = jnp.maximum(a, b)
    return peak + jnp.log(jnp.exp(a - peak) + jnp.exp(b - peak))


def first_kernel(mine, other, keep, send):
    low = lax.axis_index("grp_0")
    logs = both_logs(mine[0:4, :], other[0:4, :])
    up, down = logs[1:2, :], logs[3:4, :]
    send[0:1, :] = jnp.where(low == 0, up, down)
    send[1:2, :] = logs[2:3, :]
    keep[0:1, :] = logs[0:1, :]
    keep[1:2, :] = jnp.where(low == 0, down, up)
    send[2:3, :] = keep[2:3, :] = mine[4:5, :] + other[4:5, :]


def second_kernel(kept, got, keep, send):
    logs = both_logs(kept[0:2, :], got[0:2, :])
    keep[0:1, :] = logs[0:1, :]
    send[0:1, :] = logs[1:2, :]
    send[1:2, :] = keep[1:2, :] = kept[2:3, :] + got[2:3, :]


def finish_kernel(got, own, *refs):
    lines, (source, target) = refs[:-2], refs[-2:]

    def total(logs):
        peak = jnp.max(logs, 0, keepdims=True)
        return peak + jnp.log(jnp.sum(jnp.exp(logs - peak), 0, keepdims=True))

    mass = jnp.log(sum(line[1:2, :] for line in lines))
    row_total = total(jnp.concatenate([line[0:1, :] for line in lines], 0)) - own[0:1, :] - wide_of(mass, 1)
    col_total = total(jnp.concatenate([got[j] for j in range(got.shape[0])], 0)) - own[2:3, :] - wide_of(mass, 0)
    source[...] = (0.5 * (own[1:2, :] - epsilon * row_total)).reshape(BLK)
    target[...] = (0.5 * (own[3:4, :] - epsilon * col_total)).reshape(BLK)


def wide_of(mass, half):
    line = mass[:, 128 * half : 128 * (half + 1)]
    return jnp.concatenate([line, line], 1)


def along(step):
    index = [(z % 2) * 2 + z // 2 for z in range(SIDE)]
    return [(index[z], index[(z + step) % SIDE]) for z in range(SIDE)]


def local(source_pts, target_pts, source_pot, target_pot, source_logw, target_logw):
    nrow, ncol = lax.axis_size(GROUP), lax.axis_size(PLANE)
    lines = [v.reshape(2, 128) for v in (source_pot, target_pot, source_logw, target_logw)]
    rows, copies = call(
        pack_kernel,
        (f32(TALL, 128), f32(ncol, TALL, 128)),
        6,
        scratch=[
            pltpu.VMEM((TALL, 128), jnp.float32),
            pltpu.VMEM((4, 2, 128), jnp.float32),
            pltpu.SemaphoreType.DMA((8,)),
            pltpu.SemaphoreType.DMA((ncol,)),
        ],
        specs=(VMEM, HBM),
    )(*(pltpu.with_memory_space_constraint(v, pltpu.HBM) for v in (source_pts, target_pts, *lines)))
    mine = [rows]
    for k in range(1, SIDE):
        mine.append(lax.ppermute(rows, LINE, along(-k)))
    others = lax.ppermute(jnp.stack(mine), CORE, [(0, 1), (1, 0)])
    cols = lax.all_to_all(copies, PLANE, 0, 0, tiled=True)
    nrow = nrow // 2
    size = nrow * ncol * BLK * BLK
    cost = pl.CostEstimate(flops=512 * size, bytes_accessed=4 * 2**20, transcendentals=size)
    xt, stats = call(
        rows_kernel,
        (jax.ShapeDtypeStruct((2 * nrow * BLK, 256), jnp.bfloat16), f32(1, BLK)),
        5,
        cost=pl.CostEstimate(flops=10**6, bytes_accessed=10**6, transcendentals=0),
    )(*mine, others)
    scratch = [
        pltpu.VMEM((nrow * BLK, 128), jnp.float32),
        pltpu.VMEM((8, ncol * BLK), jnp.float32),
        pltpu.VMEM((BLK, 128), jnp.float32),
        pltpu.VMEM((BLK, 128), jnp.float32),
        pltpu.VMEM((1, nrow * BLK), jnp.float32),
    ]
    yk, former, lines = call(
        functools.partial(half_kernel, nrow, ncol, False),
        (jax.ShapeDtypeStruct((256, ncol * BLK), jnp.bfloat16), f32(2, ncol * BLK), f32(8, BLK)),
        4,
        scratch=scratch,
        cost=cost,
    )(others, cols, xt, stats)
    crossed = lax.ppermute(lines, CORE, [(0, 1), (1, 0)])
    lines, out, own = call(
        functools.partial(half_kernel, nrow, ncol, True),
        (f32(8, BLK), f32(ncol, 1, BLK), f32(8, BLK)),
        SIDE + 5,
        scratch=scratch,
        cost=cost,
    )(*mine, cols, xt, stats, yk, former)
    got = lax.all_to_all(out, PLANE, 0, 0, tiled=True)
    small = pl.CostEstimate(flops=10**5, bytes_accessed=10**5, transcendentals=0)
    keep, send = call(first_kernel, (f32(8, BLK), f32(8, BLK)), 2, cost=small)(lines, crossed)
    send = lax.ppermute(send, LINE[0], [(0, 1), (1, 0)])
    keep, send = call(second_kernel, (f32(2, BLK), f32(2, BLK)), 2, cost=small)(keep, send)
    send = lax.ppermute(send, LINE, [(i, SIDE - 1 - i) for i in range(SIDE)])
    return call(finish_kernel, (f32(BLK), f32(BLK)), 4)(got, own, keep, send)


def solution(mesh):
    finer = Mesh(mesh.devices.reshape(2, 2, 2, 4, 4), GRP_MEM)
    return jax.shard_map(
        local,
        mesh=finer,
        in_specs=(P(None, GRP_MEM), P(None, GRP_MEM), P(GRP_MEM), P(GRP_MEM), P(GRP_MEM), P(GRP_MEM)),
        out_specs=(P(GRP_MEM), P(GRP_MEM)),
        check_vma=False,
    )
```

```python
import functools

import jax
import jax.numpy as jnp
from jax import lax
from jax.experimental import pallas as pl
from jax.experimental.pallas import tpu as pltpu
from jax.sharding import Mesh
from jax.sharding import PartitionSpec as P

GRP_MEM = ("grp_0", "grp_1", "mem_0", "mem_1", "mem_2", "mem_3")
COLS = ("grp_1", "mem_1", "mem_3")
LINE = ("grp_0", "mem_0")
FACE = ("mem_2", "mem_3")
SIDE = 4

epsilon = 4.0
LOG2E = 1.4426950408889634
FEAT = 64
BLK = 256
TALL = 136
floor_value = -1e30
LOW = 2.0**-90
HIGH = 2.0**120
NORM = 90.5

VMEM = pl.BlockSpec(memory_space=pltpu.VMEM)


HBM = pl.BlockSpec(memory_space=pltpu.HBM)


def call(kernel, out, ins, scratch=(), cost=None, specs=None):
    return pl.pallas_call(
        kernel,
        out_shape=out,
        in_specs=[HBM if specs else VMEM] * ins,
        out_specs=specs or jax.tree.map(lambda _: VMEM, out),
        scratch_shapes=scratch,
        compiler_params=pltpu.CompilerParams(vmem_limit_bytes=40 * 2**20),
        cost_estimate=cost,
    )


def f32(*shape):
    return jax.ShapeDtypeStruct(shape, jnp.float32)


def pack_kernel(spts, tpts, spot, tpot, slogw, tlogw, rows, copies, cols, lines, sems, out_sems):
    loads = []
    for pts, block in ((tpts, cols), (spts, rows)):
        for half in range(2):
            loads.append((pts.at[:, 128 * half : 128 * (half + 1)], block.at[64 * half : 64 * (half + 1), :]))
    for k, ref in enumerate((slogw, spot, tlogw, tpot)):
        loads.append((ref, lines.at[k]))
    loads = [pltpu.make_async_copy(a, b, sems.at[k]) for k, (a, b) in enumerate(loads)]
    for load in loads:
        load.start()
    for k in range(4, 8):
        loads[k].wait()
    tails = []
    for logw, pot, other in ((lines[0], lines[1], lines[2]), (lines[2], lines[3], lines[0])):
        tails.append(jnp.concatenate((logw + pot / epsilon, logw, pot, other), 0))
    cols[128:136, :] = tails[1]
    loads[0].wait()
    loads[1].wait()
    stores = [pltpu.make_async_copy(cols, copies.at[k], out_sems.at[k]) for k in range(copies.shape[0])]
    for store in stores:
        store.start()
    rows[128:136, :] = tails[0]
    loads[2].wait()
    loads[3].wait()
    for store in stores:
        store.wait()


def wide(block, line):
    return jnp.concatenate([block[line : line + 1, :], block[line + 1 : line + 2, :]], 1)


def unpacked(block):
    pts = jnp.concatenate([block[0:64, :], block[64:128, :]], 1)
    return pts, 0.5 * jnp.sum(pts * pts, 0, keepdims=True), wide(block, 128)


def split(v):
    head = v.astype(jnp.bfloat16).astype(jnp.float32)
    return head, v - head


def bias_lines(bias, first):
    b1, rest = split(bias)
    b2, b3 = split(rest)
    line = lax.broadcasted_iota(jnp.int32, (16, BLK), 0)
    out = jnp.zeros((16, BLK), jnp.float32)
    for k, piece in enumerate((b1, b2, b3)):
        out = jnp.where(line == k + first, piece, out)
    return jnp.where((line >= 3 - first) & (line < 6 - first), 1.0, out)


def blocks_of(refs):
    out = []
    for ref in refs:
        out.extend([ref] if len(ref.shape) == 2 else [ref.at[k] for k in range(ref.shape[0])])
    return out


def rows_kernel(*refs):
    blocks = blocks_of(refs[:-2])
    blocks = blocks[0::2] + blocks[1::2]
    xt, stats = refs[-2:]
    most = jnp.zeros((1, BLK), jnp.float32)
    for k, block in enumerate(blocks):
        pts, sq, term = unpacked(block)
        most = jnp.maximum(most, sq)
        x1, x2 = split(pts * (LOG2E / epsilon))
        bias = bias_lines((term - sq / epsilon) * LOG2E, 0)
        left = jnp.concatenate([x1, x2], 0)
        right = jnp.concatenate([x1, bias, jnp.zeros((48, BLK), jnp.float32)], 0)
        xt[k * BLK : (k + 1) * BLK, :128] = left.T.astype(jnp.bfloat16)
        xt[k * BLK : (k + 1) * BLK, 128:] = right.T.astype(jnp.bfloat16)
    stats[...] = most


def outside(v, low, high):
    return jnp.where((v > low) & (v < high), 0.0, 1.0)


def half_kernel(nrow, ncol, last, *refs):
    blocks = blocks_of(refs[:SIDE])[0 if last else 1 :: 2]
    refs = refs[SIDE:]
    if last:
        cols, xt, stats, yk, former, lines, out, own, rowacc, colacc, rmax, rsum, rlog = refs
        most = former[1:2, 0:BLK]
    else:
        cols, xt, stats, yk, former, lines, rowacc, colacc, rmax, rsum, rlog = refs

        most = jnp.zeros((1, BLK), jnp.float32)
        masses = jnp.zeros((8, 128), jnp.float32)
    step = 512
    first = 0 if last else nrow * BLK

    for j in range(ncol):
        at = slice(j * BLK, (j + 1) * BLK)
        if last:
            right = yk[:, at]
        else:
            block = cols.at[j]
            pts, sq, term = unpacked(block)
            y1, y2 = split(pts)
            bias = bias_lines((term - sq / epsilon) * LOG2E, 3).astype(jnp.bfloat16)
            y1 = y1.astype(jnp.bfloat16)
            right = jnp.concatenate([y1, y1, y2.astype(jnp.bfloat16), bias, jnp.zeros((48, BLK), jnp.bfloat16)], 0)
            yk[:, at] = right
            most = jnp.maximum(most, sq)
            masses = masses + jnp.exp(block[128:136, :])
        total = jnp.zeros((8, BLK), jnp.float32)
        for i in range(nrow * BLK // step):
            rows = slice(i * step, (i + 1) * step)
            held = slice(first + i * step, first + (i + 1) * step)
            e = jnp.exp2(jnp.dot(xt[held, :], right, preferred_element_type=jnp.float32))
            part = e[:, :128] + e[:, 128:]
            rowacc[rows, :] = part if j == 0 else rowacc[rows, :] + part
            total += jnp.sum(e.reshape(step // 8, 8, BLK), 0)
        colacc[:, at] = total

    s1, s2 = split(rowacc[...])
    parts = jnp.concatenate([s1, s2], 1).astype(jnp.bfloat16)
    rows = lax.dot_general(
        jnp.ones((16, 256), jnp.bfloat16), parts, (((1,), (1,)), ((), ())), preferred_element_type=jnp.float32
    )[:1]
    sums = jnp.sum(colacc[...], 0, keepdims=True)
    ill = outside(stats[...], floor_value, NORM) + outside(most, floor_value, NORM)
    for j in range(nrow):
        ill = ill + outside(rows[:, j * BLK : (j + 1) * BLK], LOW, HIGH)
    for j in range(ncol):
        ill = ill + outside(sums[:, j * BLK : (j + 1) * BLK], LOW, HIGH)
    fast = jnp.max(ill) < 0.5
    rlog[...] = jnp.log(rows)
    colacc[0:1, :] = jnp.log(sums)

    @pl.when(jnp.logical_not(fast))
    def _():
        colacc[0:1, :] = jnp.full((1, ncol * BLK), floor_value, jnp.float32)
        colacc[1:2, :] = jnp.zeros((1, ncol * BLK), jnp.float32)
        for k, block in enumerate(blocks):
            flat, _, term = unpacked(block)
            pts_t = flat.T
            sq_t = 0.5 * jnp.sum(pts_t * pts_t, 1, keepdims=True)
            term_t = jnp.broadcast_to(term, (128, BLK)).T[:, :1]
            rmax[...] = jnp.full(rmax.shape, floor_value, jnp.float32)
            rsum[...] = jnp.zeros_like(rsum)

            def exact(j, _):
                at = pl.ds(pl.multiple_of(j * BLK, BLK), BLK)
                pts, sq, col_term = unpacked(cols.at[j])
                cross = jnp.dot(
                    pts_t, pts, precision=lax.Precision.HIGHEST, preferred_element_type=jnp.float32
                )
                half = (sq_t + sq - cross) / epsilon
                scores = col_term - half
                old = rmax[...]
                new = jnp.maximum(old, jnp.max(scores, 1, keepdims=True))
                part = jnp.sum(jnp.exp(scores - new[:, :1]), 1, keepdims=True)
                rsum[...] = rsum[...] * jnp.exp(old - new) + part
                rmax[...] = new
                others = term_t - half
                old = colacc[0:1, at]
                new = jnp.maximum(old, jnp.max(others, 0, keepdims=True))
                part = jnp.sum(jnp.exp(others - new), 0, keepdims=True)
                colacc[1:2, at] = colacc[1:2, at] * jnp.exp(old - new) + part
                colacc[0:1, at] = new
                return 0

            lax.fori_loop(0, ncol, exact, 0)
            total = (rmax[...] + jnp.log(rsum[...])).T[:1]
            rlog[:, k * BLK : (k + 1) * BLK] = total + term

        def finish(j, _):
            at = pl.ds(pl.multiple_of(j * BLK, BLK), BLK)
            colacc[0:1, at] = colacc[0:1, at] + jnp.log(colacc[1:2, at]) + wide(cols.at[j], 128)
            return 0

        lax.fori_loop(0, ncol, finish, 0)

    for k in range(nrow):
        lines[k : k + 1, :] = rlog[:, k * BLK : (k + 1) * BLK]
    if last:
        lines[4:5, :] = former[1:2, BLK : 2 * BLK]
        both = both_logs(colacc[0:1, :], former[0:1, :])
        for j in range(ncol):
            out[j] = both[:, j * BLK : (j + 1) * BLK]
        core, x, low = (lax.axis_index(n) for n in COLS)
        here = (core * SIDE + x) * 2 + low
        own[0:1, :] = wide(blocks[0], 128)
        own[1:2, :] = wide(blocks[0], 132)
        own[2:3, :] = wide(cols.at[here], 128)
        own[3:4, :] = wide(cols.at[here], 132)
    else:
        target_mass = jnp.sum(masses[2:4, :], keepdims=True)
        source_mass = jnp.sum(masses[6:8, :], keepdims=True)
        mass = jnp.concatenate(
            [jnp.broadcast_to(source_mass, (1, 128)), jnp.broadcast_to(target_mass, (1, 128))], 1
        )
        lines[4:5, :] = mass
        former[0:1, :] = colacc[0:1, :]
        former[1:2, 0:BLK] = most
        former[1:2, BLK : 2 * BLK] = mass


def both_logs(a, b):
    peak = jnp.maximum(a, b)
    return peak + jnp.log(jnp.exp(a - peak) + jnp.exp(b - peak))


def first_kernel(mine, other, keep, send):
    low = lax.axis_index("grp_0")
    logs = both_logs(mine[0:4, :], other[0:4, :])
    up, down = logs[1:2, :], logs[3:4, :]
    send[0:1, :] = jnp.where(low == 0, up, down)
    send[1:2, :] = logs[2:3, :]
    keep[0:1, :] = logs[0:1, :]
    keep[1:2, :] = jnp.where(low == 0, down, up)
    send[2:3, :] = keep[2:3, :] = mine[4:5, :] + other[4:5, :]


def second_kernel(kept, got, keep, send):
    logs = both_logs(kept[0:2, :], got[0:2, :])
    keep[0:1, :] = logs[0:1, :]
    send[0:1, :] = logs[1:2, :]
    send[1:2, :] = keep[1:2, :] = kept[2:3, :] + got[2:3, :]


def finish_kernel(got, own, *refs):
    lines, (source, target) = refs[:-2], refs[-2:]

    def total(logs):
        peak = jnp.max(logs, 0, keepdims=True)
        return peak + jnp.log(jnp.sum(jnp.exp(logs - peak), 0, keepdims=True))

    mass = jnp.log(sum(line[1:2, :] for line in lines))
    row_total = total(jnp.concatenate([line[0:1, :] for line in lines], 0)) - own[0:1, :] - wide_of(mass, 1)
    col_total = total(jnp.concatenate([got[j] for j in range(got.shape[0])], 0)) - own[2:3, :] - wide_of(mass, 0)
    source[...] = (0.5 * (own[1:2, :] - epsilon * row_total)).reshape(BLK)
    target[...] = (0.5 * (own[3:4, :] - epsilon * col_total)).reshape(BLK)


def wide_of(mass, half):
    line = mass[:, 128 * half : 128 * (half + 1)]
    return jnp.concatenate([line, line], 1)


def along(step):
    index = [(z % 2) * 2 + z // 2 for z in range(SIDE)]
    return [(index[z], index[(z + step) % SIDE]) for z in range(SIDE)]


def local(source_pts, target_pts, source_pot, target_pot, source_logw, target_logw):
    nrow, ncol = SIDE, lax.axis_size(COLS)
    lines = [v.reshape(2, 128) for v in (source_pot, target_pot, source_logw, target_logw)]
    rows, copies = call(
        pack_kernel,
        (f32(TALL, 128), f32(ncol, TALL, 128)),
        6,
        scratch=[
            pltpu.VMEM((TALL, 128), jnp.float32),
            pltpu.VMEM((4, 2, 128), jnp.float32),
            pltpu.SemaphoreType.DMA((8,)),
            pltpu.SemaphoreType.DMA((ncol,)),
        ],
        specs=(VMEM, HBM),
    )(*(pltpu.with_memory_space_constraint(v, pltpu.HBM) for v in (source_pts, target_pts, *lines)))
    turned = [(i, SIDE - 1 - i) for i in range(SIDE)]
    pair = jnp.stack([rows, lax.ppermute(rows, FACE, turned)])
    mine = [pair]
    for k in range(1, SIDE):
        mine.append(lax.ppermute(pair, LINE, along(-k)))
    cols = lax.all_to_all(copies, COLS, 0, 0, tiled=True)
    size = nrow * ncol * BLK * BLK
    cost = pl.CostEstimate(flops=512 * size, bytes_accessed=4 * 2**20, transcendentals=size)
    xt, stats = call(
        rows_kernel,
        (jax.ShapeDtypeStruct((2 * nrow * BLK, 256), jnp.bfloat16), f32(1, BLK)),
        SIDE,
        cost=pl.CostEstimate(flops=10**6, bytes_accessed=10**6, transcendentals=0),
    )(*mine)
    scratch = [
        pltpu.VMEM((nrow * BLK, 128), jnp.float32),
        pltpu.VMEM((8, ncol * BLK), jnp.float32),
        pltpu.VMEM((BLK, 128), jnp.float32),
        pltpu.VMEM((BLK, 128), jnp.float32),
        pltpu.VMEM((1, nrow * BLK), jnp.float32),
    ]
    yk, former, lines = call(
        functools.partial(half_kernel, nrow, ncol, False),
        (jax.ShapeDtypeStruct((256, ncol * BLK), jnp.bfloat16), f32(2, ncol * BLK), f32(8, BLK)),
        SIDE + 3,
        scratch=scratch,
        cost=cost,
    )(*mine, cols, xt, stats)
    crossed = lax.ppermute(lines, FACE, turned)
    lines, out, own = call(
        functools.partial(half_kernel, nrow, ncol, True),
        (f32(8, BLK), f32(ncol, 1, BLK), f32(8, BLK)),
        SIDE + 5,
        scratch=scratch,
        cost=cost,
    )(*mine, cols, xt, stats, yk, former)
    got = lax.all_to_all(out, COLS, 0, 0, tiled=True)
    small = pl.CostEstimate(flops=10**5, bytes_accessed=10**5, transcendentals=0)
    keep, send = call(first_kernel, (f32(8, BLK), f32(8, BLK)), 2, cost=small)(lines, crossed)
    send = lax.ppermute(send, LINE[0], [(0, 1), (1, 0)])
    keep, send = call(second_kernel, (f32(2, BLK), f32(2, BLK)), 2, cost=small)(keep, send)
    send = lax.ppermute(send, LINE, turned)
    return call(finish_kernel, (f32(BLK), f32(BLK)), 4)(got, own, keep, send)


def solution(mesh):
    finer = Mesh(mesh.devices.reshape(2, 2, 2, 4, 2, 2), GRP_MEM)
    return jax.shard_map(
        local,
        mesh=finer,
        in_specs=(P(None, GRP_MEM), P(None, GRP_MEM), P(GRP_MEM), P(GRP_MEM), P(GRP_MEM), P(GRP_MEM)),
        out_specs=(P(GRP_MEM), P(GRP_MEM)),
        check_vma=False,
    )
```

```python
import functools

import jax
import jax.numpy as jnp
from jax import lax
from jax.experimental import pallas as pl
from jax.experimental.pallas import tpu as pltpu
from jax.sharding import Mesh
from jax.sharding import PartitionSpec as P

GRP_MEM = ("grp_0", "grp_1", "mem_0", "mem_1", "mem_2")
GROUP = ("grp_0", "grp_1", "mem_0")
PLANE = ("mem_1", "mem_2")
LINE = ("grp_0", "mem_0")
CORE = "grp_1"
SIDE = 4
LINES = 8

epsilon = 4.0
LOG2E = 1.4426950408889634
FEAT = 64
BLK = 256
TALL = 136
floor_value = -1e30
LOW = 2.0**-90
HIGH = 2.0**120
NORM = 90.5

VMEM = pl.BlockSpec(memory_space=pltpu.VMEM)


HBM = pl.BlockSpec(memory_space=pltpu.HBM)


def call(kernel, out, ins, scratch=(), cost=None, specs=None):
    return pl.pallas_call(
        kernel,
        out_shape=out,
        in_specs=[HBM if specs else VMEM] * ins,
        out_specs=specs or jax.tree.map(lambda _: VMEM, out),
        scratch_shapes=scratch,
        compiler_params=pltpu.CompilerParams(vmem_limit_bytes=40 * 2**20),
        cost_estimate=cost,
    )


def f32(*shape):
    return jax.ShapeDtypeStruct(shape, jnp.float32)


def pack_kernel(spts, tpts, spot, tpot, slogw, tlogw, rows, copies, cols, lines, sems, out_sems):
    loads = []
    for pts, block in ((tpts, cols), (spts, rows)):
        for half in range(2):
            loads.append((pts.at[:, 128 * half : 128 * (half + 1)], block.at[64 * half : 64 * (half + 1), :]))
    for k, ref in enumerate((slogw, spot, tlogw, tpot)):
        loads.append((ref, lines.at[k]))
    loads = [pltpu.make_async_copy(a, b, sems.at[k]) for k, (a, b) in enumerate(loads)]
    for load in loads:
        load.start()
    for k in range(4, 8):
        loads[k].wait()
    tails = []
    for logw, pot, other in ((lines[0], lines[1], lines[2]), (lines[2], lines[3], lines[0])):
        tails.append(jnp.concatenate((logw + pot / epsilon, logw, pot, other), 0))
    cols[128:136, :] = tails[1]
    loads[0].wait()
    loads[1].wait()
    stores = [pltpu.make_async_copy(cols, copies.at[k], out_sems.at[k]) for k in range(copies.shape[0])]
    for store in stores:
        store.start()
    rows[128:136, :] = tails[0]
    loads[2].wait()
    loads[3].wait()
    for store in stores:
        store.wait()


def wide(block, line):
    return jnp.concatenate([block[line : line + 1, :], block[line + 1 : line + 2, :]], 1)


def unpacked(block):
    pts = jnp.concatenate([block[0:64, :], block[64:128, :]], 1)
    return pts, 0.5 * jnp.sum(pts * pts, 0, keepdims=True), wide(block, 128)


def split(v):
    head = v.astype(jnp.bfloat16).astype(jnp.float32)
    return head, v - head


def bias_lines(bias, first):
    b1, rest = split(bias)
    b2, b3 = split(rest)
    line = lax.broadcasted_iota(jnp.int32, (16, BLK), 0)
    out = jnp.zeros((16, BLK), jnp.float32)
    for k, piece in enumerate((b1, b2, b3)):
        out = jnp.where(line == k + first, piece, out)
    return jnp.where((line >= 3 - first) & (line < 6 - first), 1.0, out)


def blocks_of(refs):
    out = []
    for ref in refs:
        out.extend([ref] if len(ref.shape) == 2 else [ref.at[k] for k in range(ref.shape[0])])
    return out


def rows_kernel(*refs):
    blocks = blocks_of(refs[:-2])
    xt, stats = refs[-2:]
    most = jnp.zeros((1, BLK), jnp.float32)
    for k, block in enumerate(blocks):
        pts, sq, term = unpacked(block)
        most = jnp.maximum(most, sq)
        x1, x2 = split(pts * (LOG2E / epsilon))
        bias = bias_lines((term - sq / epsilon) * LOG2E, 0)
        left = jnp.concatenate([x1, x2], 0)
        right = jnp.concatenate([x1, bias, jnp.zeros((48, BLK), jnp.float32)], 0)
        xt[k * BLK : (k + 1) * BLK, :128] = left.T.astype(jnp.bfloat16)
        xt[k * BLK : (k + 1) * BLK, 128:] = right.T.astype(jnp.bfloat16)
    stats[...] = most


def outside(v, low, high):
    return jnp.where((v > low) & (v < high), 0.0, 1.0)


def tile_kernel(nrow, ncol, *refs):
    blocks = blocks_of(refs[: SIDE + 1])
    cols, xt, stats, lines, cross, out, own, rowacc, colacc, rmax, rsum, rlog = refs[SIDE + 1 :]
    most = jnp.zeros((1, BLK), jnp.float32)
    masses = jnp.zeros((8, 128), jnp.float32)
    step = 512

    for j in range(ncol):
        at = slice(j * BLK, (j + 1) * BLK)
        block = cols.at[j]
        pts, sq, term = unpacked(block)
        y1, y2 = split(pts)
        bias = bias_lines((term - sq / epsilon) * LOG2E, 3).astype(jnp.bfloat16)
        y1 = y1.astype(jnp.bfloat16)
        right = jnp.concatenate([y1, y1, y2.astype(jnp.bfloat16), bias, jnp.zeros((48, BLK), jnp.bfloat16)], 0)
        most = jnp.maximum(most, sq)
        masses = masses + jnp.exp(block[128:136, :])
        total = jnp.zeros((8, BLK), jnp.float32)
        for i in range(nrow * BLK // step):
            rows = slice(i * step, (i + 1) * step)
            e = jnp.exp2(jnp.dot(xt[rows, :], right, preferred_element_type=jnp.float32))
            part = e[:, :128] + e[:, 128:]
            rowacc[rows, :] = part if j == 0 else rowacc[rows, :] + part
            total += jnp.sum(e.reshape(step // 8, 8, BLK), 0)
        colacc[:, at] = total

    s1, s2 = split(rowacc[...])
    parts = jnp.concatenate([s1, s2], 1).astype(jnp.bfloat16)
    rows = lax.dot_general(
        jnp.ones((16, 256), jnp.bfloat16), parts, (((1,), (1,)), ((), ())), preferred_element_type=jnp.float32
    )[:1]
    sums = jnp.sum(colacc[...], 0, keepdims=True)
    ill = outside(stats[...], floor_value, NORM) + outside(most, floor_value, NORM)
    for j in range(nrow):
        ill = ill + outside(rows[:, j * BLK : (j + 1) * BLK], LOW, HIGH)
    for j in range(ncol):
        ill = ill + outside(sums[:, j * BLK : (j + 1) * BLK], LOW, HIGH)
    fast = jnp.max(ill) < 0.5
    rlog[...] = jnp.log(rows)
    colacc[0:1, :] = jnp.log(sums)

    @pl.when(jnp.logical_not(fast))
    def _():
        colacc[0:1, :] = jnp.full((1, ncol * BLK), floor_value, jnp.float32)
        colacc[1:2, :] = jnp.zeros((1, ncol * BLK), jnp.float32)
        for k, block in enumerate(blocks):
            flat, _, term = unpacked(block)
            pts_t = flat.T
            sq_t = 0.5 * jnp.sum(pts_t * pts_t, 1, keepdims=True)
            term_t = jnp.broadcast_to(term, (128, BLK)).T[:, :1]
            rmax[...] = jnp.full(rmax.shape, floor_value, jnp.float32)
            rsum[...] = jnp.zeros_like(rsum)

            def exact(j, _):
                at = pl.ds(pl.multiple_of(j * BLK, BLK), BLK)
                pts, sq, col_term = unpacked(cols.at[j])
                cross = jnp.dot(
                    pts_t, pts, precision=lax.Precision.HIGHEST, preferred_element_type=jnp.float32
                )
                half = (sq_t + sq - cross) / epsilon
                scores = col_term - half
                old = rmax[...]
                new = jnp.maximum(old, jnp.max(scores, 1, keepdims=True))
                part = jnp.sum(jnp.exp(scores - new[:, :1]), 1, keepdims=True)
                rsum[...] = rsum[...] * jnp.exp(old - new) + part
                rmax[...] = new
                others = term_t - half
                old = colacc[0:1, at]
                new = jnp.maximum(old, jnp.max(others, 0, keepdims=True))
                part = jnp.sum(jnp.exp(others - new), 0, keepdims=True)
                colacc[1:2, at] = colacc[1:2, at] * jnp.exp(old - new) + part
                colacc[0:1, at] = new
                return 0

            lax.fori_loop(0, ncol, exact, 0)
            total = (rmax[...] + jnp.log(rsum[...])).T[:1]
            rlog[:, k * BLK : (k + 1) * BLK] = total + term

        def finish(j, _):
            at = pl.ds(pl.multiple_of(j * BLK, BLK), BLK)
            colacc[0:1, at] = colacc[0:1, at] + jnp.log(colacc[1:2, at]) + wide(cols.at[j], 128)
            return 0

        lax.fori_loop(0, ncol, finish, 0)

    target_mass = jnp.sum(masses[2:4, :], keepdims=True)
    source_mass = jnp.sum(masses[6:8, :], keepdims=True)
    mass = jnp.concatenate(
        [jnp.broadcast_to(source_mass, (1, 128)), jnp.broadcast_to(target_mass, (1, 128))], 1
    )
    for to, base in ((lines, 0), (cross, SIDE)):
        for k in range(SIDE):
            to[k : k + 1, :] = rlog[:, (base + k) * BLK : (base + k + 1) * BLK]
        to[4:5, :] = mass
    for j in range(ncol):
        out[j] = colacc[0:1, j * BLK : (j + 1) * BLK]
    at_plane = lax.axis_index("mem_1") * SIDE + lax.axis_index("mem_2")
    own[0:1, :] = wide(blocks[0], 128)
    own[1:2, :] = wide(blocks[0], 132)
    own[2:3, :] = wide(cols.at[at_plane], 128)
    own[3:4, :] = wide(cols.at[at_plane], 132)


def both_logs(a, b):
    peak = jnp.maximum(a, b)
    return peak + jnp.log(jnp.exp(a - peak) + jnp.exp(b - peak))


def first_kernel(mine, other, keep, send):
    low = lax.axis_index("grp_0")
    logs = both_logs(mine[0:4, :], other[0:4, :])
    up, down = logs[1:2, :], logs[3:4, :]
    send[0:1, :] = jnp.where(low == 0, up, down)
    send[1:2, :] = logs[2:3, :]
    keep[0:1, :] = logs[0:1, :]
    keep[1:2, :] = jnp.where(low == 0, down, up)
    send[2:3, :] = keep[2:3, :] = mine[4:5, :] + other[4:5, :]


def second_kernel(kept, got, keep, send):
    logs = both_logs(kept[0:2, :], got[0:2, :])
    keep[0:1, :] = logs[0:1, :]
    send[0:1, :] = logs[1:2, :]
    send[1:2, :] = keep[1:2, :] = kept[2:3, :] + got[2:3, :]


def finish_kernel(got, own, *refs):
    lines, (source, target) = refs[:-2], refs[-2:]

    def total(logs):
        peak = jnp.max(logs, 0, keepdims=True)
        return peak + jnp.log(jnp.sum(jnp.exp(logs - peak), 0, keepdims=True))

    mass = jnp.log(sum(line[1:2, :] for line in lines))
    row_total = total(jnp.concatenate([line[0:1, :] for line in lines], 0)) - own[0:1, :] - wide_of(mass, 1)
    col_total = total(jnp.concatenate([got[j] for j in range(got.shape[0])], 0)) - own[2:3, :] - wide_of(mass, 0)
    source[...] = (0.5 * (own[1:2, :] - epsilon * row_total)).reshape(BLK)
    target[...] = (0.5 * (own[3:4, :] - epsilon * col_total)).reshape(BLK)


def wide_of(mass, half):
    line = mass[:, 128 * half : 128 * (half + 1)]
    return jnp.concatenate([line, line], 1)


def along(step):
    index = [(z % 2) * 2 + z // 2 for z in range(SIDE)]
    return [(index[z], index[(z + step) % SIDE]) for z in range(SIDE)]


def local(source_pts, target_pts, source_pot, target_pot, source_logw, target_logw):
    nrow, ncol = lax.axis_size(GROUP), lax.axis_size(PLANE)
    lines = [v.reshape(2, 128) for v in (source_pot, target_pot, source_logw, target_logw)]
    rows, copies = call(
        pack_kernel,
        (f32(TALL, 128), f32(ncol, TALL, 128)),
        6,
        scratch=[
            pltpu.VMEM((TALL, 128), jnp.float32),
            pltpu.VMEM((4, 2, 128), jnp.float32),
            pltpu.SemaphoreType.DMA((8,)),
            pltpu.SemaphoreType.DMA((ncol,)),
        ],
        specs=(VMEM, HBM),
    )(*(pltpu.with_memory_space_constraint(v, pltpu.HBM) for v in (source_pts, target_pts, *lines)))
    mine = [rows]
    for k in range(1, SIDE):
        mine.append(lax.ppermute(rows, LINE, along(-k)))
    others = lax.ppermute(jnp.stack(mine), CORE, [(0, 1), (1, 0)])
    cols = lax.all_to_all(copies, PLANE, 0, 0, tiled=True)
    size = nrow * ncol * BLK * BLK
    cost = pl.CostEstimate(flops=512 * size, bytes_accessed=4 * 2**20, transcendentals=size)
    xt, stats = call(
        rows_kernel,
        (jax.ShapeDtypeStruct((nrow * BLK, 256), jnp.bfloat16), f32(1, BLK)),
        5,
        cost=pl.CostEstimate(flops=10**6, bytes_accessed=10**6, transcendentals=0),
    )(*mine, others)
    scratch = [
        pltpu.VMEM((nrow * BLK, 128), jnp.float32),
        pltpu.VMEM((8, ncol * BLK), jnp.float32),
        pltpu.VMEM((BLK, 128), jnp.float32),
        pltpu.VMEM((BLK, 128), jnp.float32),
        pltpu.VMEM((1, nrow * BLK), jnp.float32),
    ]
    lines, cross, out, own = call(
        functools.partial(tile_kernel, nrow, ncol),
        (f32(LINES, BLK), f32(LINES, BLK), f32(ncol, 1, BLK), f32(8, BLK)),
        SIDE + 4,
        scratch=scratch,
        cost=cost,
    )(*mine, others, cols, xt, stats)
    crossed = lax.ppermute(cross, CORE, [(0, 1), (1, 0)])
    got = lax.all_to_all(out, PLANE, 0, 0, tiled=True)
    small = pl.CostEstimate(flops=10**5, bytes_accessed=10**5, transcendentals=0)
    keep, send = call(first_kernel, (f32(8, BLK), f32(8, BLK)), 2, cost=small)(lines, crossed)
    send = lax.ppermute(send, LINE[0], [(0, 1), (1, 0)])
    keep, send = call(second_kernel, (f32(2, BLK), f32(2, BLK)), 2, cost=small)(keep, send)
    send = lax.ppermute(send, LINE, [(i, SIDE - 1 - i) for i in range(SIDE)])
    return call(finish_kernel, (f32(BLK), f32(BLK)), 4)(got, own, keep, send)


def solution(mesh):
    finer = Mesh(mesh.devices.reshape(2, 2, 2, 4, 4), GRP_MEM)
    return jax.shard_map(
        local,
        mesh=finer,
        in_specs=(P(None, GRP_MEM), P(None, GRP_MEM), P(GRP_MEM), P(GRP_MEM), P(GRP_MEM), P(GRP_MEM)),
        out_specs=(P(GRP_MEM), P(GRP_MEM)),
        check_vma=False,
    )
```

```python
import functools

import jax
import jax.numpy as jnp
from jax import lax
from jax.experimental import pallas as pl
from jax.experimental.pallas import tpu as pltpu
from jax.sharding import Mesh
from jax.sharding import PartitionSpec as P

GRP_MEM = ("grp_0", "grp_1", "mem_0", "mem_1", "mem_2")
GROUP = ("grp_0", "grp_1", "mem_0")
PLANE = ("mem_1", "mem_2")
LINE = ("grp_0", "mem_0")
CORE = "grp_1"
SIDE = 4
LINES = 8
SENT = 8

epsilon = 4.0
LOG2E = 1.4426950408889634
FEAT = 64
BLK = 256
TALL = 136
floor_value = -1e30
LOW = 2.0**-90
HIGH = 2.0**120
NORM = 90.5

VMEM = pl.BlockSpec(memory_space=pltpu.VMEM)


HBM = pl.BlockSpec(memory_space=pltpu.HBM)


def call(kernel, out, ins, scratch=(), cost=None, specs=None):
    return pl.pallas_call(
        kernel,
        out_shape=out,
        in_specs=[HBM if specs else VMEM] * ins,
        out_specs=specs or jax.tree.map(lambda _: VMEM, out),
        scratch_shapes=scratch,
        compiler_params=pltpu.CompilerParams(vmem_limit_bytes=40 * 2**20),
        cost_estimate=cost,
    )


def f32(*shape):
    return jax.ShapeDtypeStruct(shape, jnp.float32)


def pack_kernel(spts, tpts, spot, tpot, slogw, tlogw, rows, copies, cols, lines, sems, out_sems):
    loads = []
    for pts, block in ((tpts, cols), (spts, rows)):
        for half in range(2):
            loads.append((pts.at[:, 128 * half : 128 * (half + 1)], block.at[64 * half : 64 * (half + 1), :]))
    for k, ref in enumerate((slogw, spot, tlogw, tpot)):
        loads.append((ref, lines.at[k]))
    loads = [pltpu.make_async_copy(a, b, sems.at[k]) for k, (a, b) in enumerate(loads)]
    for load in loads:
        load.start()
    for k in range(4, 8):
        loads[k].wait()
    tails = []
    for logw, pot, other in ((lines[0], lines[1], lines[2]), (lines[2], lines[3], lines[0])):
        tails.append(jnp.concatenate((logw + pot / epsilon, logw, pot, other), 0))
    cols[128:136, :] = tails[1]
    loads[0].wait()
    loads[1].wait()
    stores = [pltpu.make_async_copy(cols, copies.at[k], out_sems.at[k]) for k in range(copies.shape[0])]
    for store in stores:
        store.start()
    rows[128:136, :] = tails[0]
    loads[2].wait()
    loads[3].wait()
    for store in stores:
        store.wait()


def wide(block, line):
    return jnp.concatenate([block[line : line + 1, :], block[line + 1 : line + 2, :]], 1)


def unpacked(block):
    pts = jnp.concatenate([block[0:64, :], block[64:128, :]], 1)
    return pts, 0.5 * jnp.sum(pts * pts, 0, keepdims=True), wide(block, 128)


def split(v):
    head = v.astype(jnp.bfloat16).astype(jnp.float32)
    return head, v - head


def bias_lines(bias, first):
    b1, rest = split(bias)
    b2, b3 = split(rest)
    line = lax.broadcasted_iota(jnp.int32, (16, BLK), 0)
    out = jnp.zeros((16, BLK), jnp.float32)
    for k, piece in enumerate((b1, b2, b3)):
        out = jnp.where(line == k + first, piece, out)
    return jnp.where((line >= 3 - first) & (line < 6 - first), 1.0, out)


def blocks_of(refs):
    out = []
    for ref in refs:
        out.extend([ref] if len(ref.shape) == 2 else [ref.at[k] for k in range(ref.shape[0])])
    return out


def rows_kernel(*refs):
    blocks = blocks_of(refs[:-2])
    xt, stats = refs[-2:]
    most = jnp.zeros((1, BLK), jnp.float32)
    for k, block in enumerate(blocks):
        pts, sq, term = unpacked(block)
        most = jnp.maximum(most, sq)
        x1, x2 = split(pts * (LOG2E / epsilon))
        bias = bias_lines((term - sq / epsilon) * LOG2E, 0)
        left = jnp.concatenate([x1, x2], 0)
        right = jnp.concatenate([x1, bias, jnp.zeros((48, BLK), jnp.float32)], 0)
        xt[k * BLK : (k + 1) * BLK, :128] = left.T.astype(jnp.bfloat16)
        xt[k * BLK : (k + 1) * BLK, 128:] = right.T.astype(jnp.bfloat16)
    stats[...] = most


def outside(v, low, high):
    return jnp.where((v > low) & (v < high), 0.0, 1.0)


def tile_kernel(nrow, ncol, *refs):
    blocks = blocks_of(refs[: SIDE + 1])
    cols, xt, stats, lines, cross, out, own, rowacc, colacc, rmax, rsum, rlog = refs[SIDE + 1 :]
    most = jnp.zeros((1, BLK), jnp.float32)
    masses = jnp.zeros((8, 128), jnp.float32)
    step = 2048

    for j in range(ncol):
        at = slice(j * BLK, (j + 1) * BLK)
        block = cols.at[j]
        pts, sq, term = unpacked(block)
        y1, y2 = split(pts)
        bias = bias_lines((term - sq / epsilon) * LOG2E, 3).astype(jnp.bfloat16)
        y1 = y1.astype(jnp.bfloat16)
        right = jnp.concatenate([y1, y1, y2.astype(jnp.bfloat16), bias, jnp.zeros((48, BLK), jnp.bfloat16)], 0)
        most = jnp.maximum(most, sq)
        masses = masses + jnp.exp(block[128:136, :])
        total = jnp.zeros((8, BLK), jnp.float32)
        for i in range(nrow * BLK // step):
            rows = slice(i * step, (i + 1) * step)
            e = jnp.exp2(jnp.dot(xt[rows, :], right, preferred_element_type=jnp.float32))
            part = e[:, :128] + e[:, 128:]
            rowacc[rows, :] = part if j == 0 else rowacc[rows, :] + part
            total += jnp.sum(e.reshape(step // 8, 8, BLK), 0)
        colacc[:, at] = total

    s1, s2 = split(rowacc[...])
    parts = jnp.concatenate([s1, s2], 1).astype(jnp.bfloat16)
    rows = lax.dot_general(
        jnp.ones((16, 256), jnp.bfloat16), parts, (((1,), (1,)), ((), ())), preferred_element_type=jnp.float32
    )[:1]
    sums = jnp.sum(colacc[...], 0, keepdims=True)
    ill = outside(stats[...], floor_value, NORM) + outside(most, floor_value, NORM)
    for j in range(nrow):
        ill = ill + outside(rows[:, j * BLK : (j + 1) * BLK], LOW, HIGH)
    for j in range(ncol):
        ill = ill + outside(sums[:, j * BLK : (j + 1) * BLK], LOW, HIGH)
    fast = jnp.max(ill) < 0.5
    rlog[...] = jnp.log(rows)
    colacc[0:1, :] = jnp.log(sums)

    @pl.when(jnp.logical_not(fast))
    def _():
        colacc[0:1, :] = jnp.full((1, ncol * BLK), floor_value, jnp.float32)
        colacc[1:2, :] = jnp.zeros((1, ncol * BLK), jnp.float32)
        for k, block in enumerate(blocks):
            flat, _, term = unpacked(block)
            pts_t = flat.T
            sq_t = 0.5 * jnp.sum(pts_t * pts_t, 1, keepdims=True)
            term_t = jnp.broadcast_to(term, (128, BLK)).T[:, :1]
            rmax[...] = jnp.full(rmax.shape, floor_value, jnp.float32)
            rsum[...] = jnp.zeros_like(rsum)

            def exact(j, _):
                at = pl.ds(pl.multiple_of(j * BLK, BLK), BLK)
                pts, sq, col_term = unpacked(cols.at[j])
                cross = jnp.dot(
                    pts_t, pts, precision=lax.Precision.HIGHEST, preferred_element_type=jnp.float32
                )
                half = (sq_t + sq - cross) / epsilon
                scores = col_term - half
                old = rmax[...]
                new = jnp.maximum(old, jnp.max(scores, 1, keepdims=True))
                part = jnp.sum(jnp.exp(scores - new[:, :1]), 1, keepdims=True)
                rsum[...] = rsum[...] * jnp.exp(old - new) + part
                rmax[...] = new
                others = term_t - half
                old = colacc[0:1, at]
                new = jnp.maximum(old, jnp.max(others, 0, keepdims=True))
                part = jnp.sum(jnp.exp(others - new), 0, keepdims=True)
                colacc[1:2, at] = colacc[1:2, at] * jnp.exp(old - new) + part
                colacc[0:1, at] = new
                return 0

            lax.fori_loop(0, ncol, exact, 0)
            total = (rmax[...] + jnp.log(rsum[...])).T[:1]
            rlog[:, k * BLK : (k + 1) * BLK] = total + term

        def finish(j, _):
            at = pl.ds(pl.multiple_of(j * BLK, BLK), BLK)
            colacc[0:1, at] = colacc[0:1, at] + jnp.log(colacc[1:2, at]) + wide(cols.at[j], 128)
            return 0

        lax.fori_loop(0, ncol, finish, 0)

    target_mass = jnp.sum(masses[2:4, :], keepdims=True)
    source_mass = jnp.sum(masses[6:8, :], keepdims=True)
    mass = jnp.concatenate(
        [jnp.broadcast_to(source_mass, (1, 128)), jnp.broadcast_to(target_mass, (1, 128))], 1
    )
    for to, base in ((lines, 0), (cross, SIDE)):
        for k in range(SIDE):
            to[k : k + 1, :] = rlog[:, (base + k) * BLK : (base + k + 1) * BLK]
        to[4:5, :] = mass
    for j in range(ncol):
        out[j] = colacc[0:1, j * BLK : (j + 1) * BLK]
    at_plane = lax.axis_index("mem_1") * SIDE + lax.axis_index("mem_2")
    own[0:1, :] = wide(blocks[0], 128)
    own[1:2, :] = wide(blocks[0], 132)
    own[2:3, :] = wide(cols.at[at_plane], 128)
    own[3:4, :] = wide(cols.at[at_plane], 132)


def both_logs(a, b):
    peak = jnp.maximum(a, b)
    return peak + jnp.log(jnp.exp(a - peak) + jnp.exp(b - peak))


def merge_kernel(mine, other, *outs):
    logs = both_logs(mine[0:4, :], other[0:4, :])
    mass = mine[4:5, :] + other[4:5, :]
    for k, out in enumerate(outs):
        out[0:1, :] = logs[k : k + 1, :]
        out[1:2, :] = mass


def finish_kernel(got, own, *refs):
    lines, (source, target) = refs[:-2], refs[-2:]

    def total(logs):
        peak = jnp.max(logs, 0, keepdims=True)
        return peak + jnp.log(jnp.sum(jnp.exp(logs - peak), 0, keepdims=True))

    mass = jnp.log(sum(line[1:2, :] for line in lines))
    row_total = total(jnp.concatenate([line[0:1, :] for line in lines], 0)) - own[0:1, :] - wide_of(mass, 1)
    col_total = total(jnp.concatenate([got[j] for j in range(got.shape[0])], 0)) - own[2:3, :] - wide_of(mass, 0)
    source[...] = (0.5 * (own[1:2, :] - epsilon * row_total)).reshape(BLK)
    target[...] = (0.5 * (own[3:4, :] - epsilon * col_total)).reshape(BLK)


def wide_of(mass, half):
    line = mass[:, 128 * half : 128 * (half + 1)]
    return jnp.concatenate([line, line], 1)


def along(step):
    index = [(z % 2) * 2 + z // 2 for z in range(SIDE)]
    return [(index[z], index[(z + step) % SIDE]) for z in range(SIDE)]


def local(source_pts, target_pts, source_pot, target_pot, source_logw, target_logw):
    nrow, ncol = lax.axis_size(GROUP), lax.axis_size(PLANE)
    lines = [v.reshape(2, 128) for v in (source_pot, target_pot, source_logw, target_logw)]
    rows, copies = call(
        pack_kernel,
        (f32(TALL, 128), f32(ncol, TALL, 128)),
        6,
        scratch=[
            pltpu.VMEM((TALL, 128), jnp.float32),
            pltpu.VMEM((4, 2, 128), jnp.float32),
            pltpu.SemaphoreType.DMA((8,)),
            pltpu.SemaphoreType.DMA((ncol,)),
        ],
        specs=(VMEM, HBM),
    )(*(pltpu.with_memory_space_constraint(v, pltpu.HBM) for v in (source_pts, target_pts, *lines)))
    mine = [rows]
    for k in range(1, SIDE):
        mine.append(lax.ppermute(rows, LINE, along(-k)))
    others = lax.ppermute(jnp.stack(mine), CORE, [(0, 1), (1, 0)])
    cols = lax.all_to_all(copies, PLANE, 0, 0, tiled=True)
    size = nrow * ncol * BLK * BLK
    cost = pl.CostEstimate(flops=512 * size, bytes_accessed=4 * 2**20, transcendentals=size)
    xt, stats = call(
        rows_kernel,
        (jax.ShapeDtypeStruct((nrow * BLK, 256), jnp.bfloat16), f32(1, BLK)),
        5,
        cost=pl.CostEstimate(flops=10**6, bytes_accessed=10**6, transcendentals=0),
    )(*mine, others)
    scratch = [
        pltpu.VMEM((nrow * BLK, 128), jnp.float32),
        pltpu.VMEM((8, ncol * BLK), jnp.float32),
        pltpu.VMEM((BLK, 128), jnp.float32),
        pltpu.VMEM((BLK, 128), jnp.float32),
        pltpu.VMEM((1, nrow * BLK), jnp.float32),
    ]
    lines, cross, out, own = call(
        functools.partial(tile_kernel, nrow, ncol),
        (f32(LINES, BLK), f32(LINES, BLK), f32(ncol, 1, BLK), f32(8, BLK)),
        SIDE + 4,
        scratch=scratch,
        cost=cost,
    )(*mine, others, cols, xt, stats)
    crossed = lax.ppermute(cross, CORE, [(0, 1), (1, 0)])
    got = lax.all_to_all(out, PLANE, 0, 0, tiled=True)
    small = pl.CostEstimate(flops=10**5, bytes_accessed=10**5, transcendentals=0)
    parts = list(call(merge_kernel, (f32(SENT, BLK),) * SIDE, 2, cost=small)(lines, crossed))
    for k in range(1, SIDE):
        parts[k] = lax.ppermute(parts[k], LINE, along(k))
    return call(finish_kernel, (f32(BLK), f32(BLK)), 2 + SIDE)(got, own, *parts)


def solution(mesh):
    finer = Mesh(mesh.devices.reshape(2, 2, 2, 4, 4), GRP_MEM)
    return jax.shard_map(
        local,
        mesh=finer,
        in_specs=(P(None, GRP_MEM), P(None, GRP_MEM), P(GRP_MEM), P(GRP_MEM), P(GRP_MEM), P(GRP_MEM)),
        out_specs=(P(GRP_MEM), P(GRP_MEM)),
        check_vma=False,
    )
```

```python
import functools

import jax
import jax.numpy as jnp
from jax import lax
from jax.experimental import pallas as pl
from jax.experimental.pallas import tpu as pltpu
from jax.sharding import Mesh
from jax.sharding import PartitionSpec as P

GRP_MEM = ("grp_0", "grp_1", "mem_0", "mem_1", "mem_2")
GROUP = ("grp_0", "grp_1", "mem_0")
PLANE = ("mem_1", "mem_2")
LINE = ("grp_0", "mem_0")
CORE = "grp_1"
SIDE = 4
LINES = 8
SENT = 2

epsilon = 4.0
LOG2E = 1.4426950408889634
FEAT = 64
BLK = 256
TALL = 136
floor_value = -1e30
LOW = 2.0**-90
HIGH = 2.0**120
NORM = 90.5

VMEM = pl.BlockSpec(memory_space=pltpu.VMEM)


HBM = pl.BlockSpec(memory_space=pltpu.HBM)


def call(kernel, out, ins, scratch=(), cost=None, specs=None):
    return pl.pallas_call(
        kernel,
        out_shape=out,
        in_specs=[HBM if specs else VMEM] * ins,
        out_specs=specs or jax.tree.map(lambda _: VMEM, out),
        scratch_shapes=scratch,
        compiler_params=pltpu.CompilerParams(vmem_limit_bytes=40 * 2**20),
        cost_estimate=cost,
    )


def f32(*shape):
    return jax.ShapeDtypeStruct(shape, jnp.float32)


def pack_kernel(spts, tpts, spot, tpot, slogw, tlogw, rows, copies, cols, lines, sems, out_sems):
    loads = []
    for pts, block in ((tpts, cols), (spts, rows)):
        for half in range(2):
            loads.append((pts.at[:, 128 * half : 128 * (half + 1)], block.at[64 * half : 64 * (half + 1), :]))
    for k, ref in enumerate((slogw, spot, tlogw, tpot)):
        loads.append((ref, lines.at[k]))
    loads = [pltpu.make_async_copy(a, b, sems.at[k]) for k, (a, b) in enumerate(loads)]
    for load in loads:
        load.start()
    for k in range(4, 8):
        loads[k].wait()
    tails = []
    for logw, pot, other in ((lines[0], lines[1], lines[2]), (lines[2], lines[3], lines[0])):
        tails.append(jnp.concatenate((logw + pot / epsilon, logw, pot, other), 0))
    cols[128:136, :] = tails[1]
    loads[0].wait()
    loads[1].wait()
    stores = [pltpu.make_async_copy(cols, copies.at[k], out_sems.at[k]) for k in range(copies.shape[0])]
    for store in stores:
        store.start()
    rows[128:136, :] = tails[0]
    loads[2].wait()
    loads[3].wait()
    for store in stores:
        store.wait()


def wide(block, line):
    return jnp.concatenate([block[line : line + 1, :], block[line + 1 : line + 2, :]], 1)


def unpacked(block):
    pts = jnp.concatenate([block[0:64, :], block[64:128, :]], 1)
    return pts, 0.5 * jnp.sum(pts * pts, 0, keepdims=True), wide(block, 128)


def split(v):
    head = v.astype(jnp.bfloat16).astype(jnp.float32)
    return head, v - head


def bias_lines(bias, first):
    b1, rest = split(bias)
    b2, b3 = split(rest)
    line = lax.broadcasted_iota(jnp.int32, (16, BLK), 0)
    out = jnp.zeros((16, BLK), jnp.float32)
    for k, piece in enumerate((b1, b2, b3)):
        out = jnp.where(line == k + first, piece, out)
    return jnp.where((line >= 3 - first) & (line < 6 - first), 1.0, out)


def blocks_of(refs):
    out = []
    for ref in refs:
        out.extend([ref] if len(ref.shape) == 2 else [ref.at[k] for k in range(ref.shape[0])])
    return out


def rows_kernel(*refs):
    blocks = blocks_of(refs[:-2])
    xt, stats = refs[-2:]
    most = jnp.zeros((1, BLK), jnp.float32)
    for k, block in enumerate(blocks):
        pts, sq, term = unpacked(block)
        most = jnp.maximum(most, sq)
        x1, x2 = split(pts * (LOG2E / epsilon))
        bias = bias_lines((term - sq / epsilon) * LOG2E, 0)
        left = jnp.concatenate([x1, x2], 0)
        right = jnp.concatenate([x1, bias, jnp.zeros((48, BLK), jnp.float32)], 0)
        xt[k * BLK : (k + 1) * BLK, :128] = left.T.astype(jnp.bfloat16)
        xt[k * BLK : (k + 1) * BLK, 128:] = right.T.astype(jnp.bfloat16)
    stats[...] = most


def outside(v, low, high):
    return jnp.where((v > low) & (v < high), 0.0, 1.0)


def tile_kernel(nrow, ncol, *refs):
    blocks = blocks_of(refs[: SIDE + 1])
    cols, xt, stats, lines, cross, out, own, rowacc, colacc, rmax, rsum, rlog = refs[SIDE + 1 :]
    most = jnp.zeros((1, BLK), jnp.float32)
    masses = jnp.zeros((8, 128), jnp.float32)
    step = 2048

    for j in range(ncol):
        at = slice(j * BLK, (j + 1) * BLK)
        block = cols.at[j]
        pts, sq, term = unpacked(block)
        y1, y2 = split(pts)
        bias = bias_lines((term - sq / epsilon) * LOG2E, 3).astype(jnp.bfloat16)
        y1 = y1.astype(jnp.bfloat16)
        right = jnp.concatenate([y1, y1, y2.astype(jnp.bfloat16), bias, jnp.zeros((48, BLK), jnp.bfloat16)], 0)
        most = jnp.maximum(most, sq)
        masses = masses + jnp.exp(block[128:136, :])
        total = jnp.zeros((8, BLK), jnp.float32)
        for i in range(nrow * BLK // step):
            rows = slice(i * step, (i + 1) * step)
            e = jnp.exp2(jnp.dot(xt[rows, :], right, preferred_element_type=jnp.float32))
            part = e[:, :128] + e[:, 128:]
            rowacc[rows, :] = part if j == 0 else rowacc[rows, :] + part
            total += jnp.sum(e.reshape(step // 8, 8, BLK), 0)
        colacc[:, at] = total

    s1, s2 = split(rowacc[...])
    parts = jnp.concatenate([s1, s2], 1).astype(jnp.bfloat16)
    rows = lax.dot_general(
        jnp.ones((16, 256), jnp.bfloat16), parts, (((1,), (1,)), ((), ())), preferred_element_type=jnp.float32
    )[:1]
    sums = jnp.sum(colacc[...], 0, keepdims=True)
    ill = outside(stats[...], floor_value, NORM) + outside(most, floor_value, NORM)
    for j in range(nrow):
        ill = ill + outside(rows[:, j * BLK : (j + 1) * BLK], LOW, HIGH)
    for j in range(ncol):
        ill = ill + outside(sums[:, j * BLK : (j + 1) * BLK], LOW, HIGH)
    fast = jnp.max(ill) < 0.5
    rlog[...] = jnp.log(rows)
    colacc[0:1, :] = jnp.log(sums)

    @pl.when(jnp.logical_not(fast))
    def _():
        colacc[0:1, :] = jnp.full((1, ncol * BLK), floor_value, jnp.float32)
        colacc[1:2, :] = jnp.zeros((1, ncol * BLK), jnp.float32)
        for k, block in enumerate(blocks):
            flat, _, term = unpacked(block)
            pts_t = flat.T
            sq_t = 0.5 * jnp.sum(pts_t * pts_t, 1, keepdims=True)
            term_t = jnp.broadcast_to(term, (128, BLK)).T[:, :1]
            rmax[...] = jnp.full(rmax.shape, floor_value, jnp.float32)
            rsum[...] = jnp.zeros_like(rsum)

            def exact(j, _):
                at = pl.ds(pl.multiple_of(j * BLK, BLK), BLK)
                pts, sq, col_term = unpacked(cols.at[j])
                cross = jnp.dot(
                    pts_t, pts, precision=lax.Precision.HIGHEST, preferred_element_type=jnp.float32
                )
                half = (sq_t + sq - cross) / epsilon
                scores = col_term - half
                old = rmax[...]
                new = jnp.maximum(old, jnp.max(scores, 1, keepdims=True))
                part = jnp.sum(jnp.exp(scores - new[:, :1]), 1, keepdims=True)
                rsum[...] = rsum[...] * jnp.exp(old - new) + part
                rmax[...] = new
                others = term_t - half
                old = colacc[0:1, at]
                new = jnp.maximum(old, jnp.max(others, 0, keepdims=True))
                part = jnp.sum(jnp.exp(others - new), 0, keepdims=True)
                colacc[1:2, at] = colacc[1:2, at] * jnp.exp(old - new) + part
                colacc[0:1, at] = new
                return 0

            lax.fori_loop(0, ncol, exact, 0)
            total = (rmax[...] + jnp.log(rsum[...])).T[:1]
            rlog[:, k * BLK : (k + 1) * BLK] = total + term

        def finish(j, _):
            at = pl.ds(pl.multiple_of(j * BLK, BLK), BLK)
            colacc[0:1, at] = colacc[0:1, at] + jnp.log(colacc[1:2, at]) + wide(cols.at[j], 128)
            return 0

        lax.fori_loop(0, ncol, finish, 0)

    target_mass = jnp.sum(masses[2:4, :], keepdims=True)
    source_mass = jnp.sum(masses[6:8, :], keepdims=True)
    mass = jnp.concatenate(
        [jnp.broadcast_to(source_mass, (1, 128)), jnp.broadcast_to(target_mass, (1, 128))], 1
    )
    for to, base in ((lines, 0), (cross, SIDE)):
        for k in range(SIDE):
            to[k : k + 1, :] = rlog[:, (base + k) * BLK : (base + k + 1) * BLK]
        to[4:5, :] = mass
    for j in range(ncol):
        out[j] = colacc[0:1, j * BLK : (j + 1) * BLK]
    at_plane = lax.axis_index("mem_1") * SIDE + lax.axis_index("mem_2")
    own[0:1, :] = wide(blocks[0], 128)
    own[1:2, :] = wide(blocks[0], 132)
    own[2:3, :] = wide(cols.at[at_plane], 128)
    own[3:4, :] = wide(cols.at[at_plane], 132)


def both_logs(a, b):
    peak = jnp.maximum(a, b)
    return peak + jnp.log(jnp.exp(a - peak) + jnp.exp(b - peak))


def merge_kernel(mine, other, *outs):
    logs = both_logs(mine[0:4, :], other[0:4, :])
    mass = mine[4:5, :] + other[4:5, :]
    for k, out in enumerate(outs):
        out[0:1, :] = logs[k : k + 1, :]
        out[1:2, :] = mass


def finish_kernel(got, own, *refs):
    lines, (source, target) = refs[:-2], refs[-2:]

    def total(logs):
        peak = jnp.max(logs, 0, keepdims=True)
        return peak + jnp.log(jnp.sum(jnp.exp(logs - peak), 0, keepdims=True))

    mass = jnp.log(sum(line[1:2, :] for line in lines))
    row_total = total(jnp.concatenate([line[0:1, :] for line in lines], 0)) - own[0:1, :] - wide_of(mass, 1)
    col_total = total(jnp.concatenate([got[j] for j in range(got.shape[0])], 0)) - own[2:3, :] - wide_of(mass, 0)
    source[...] = (0.5 * (own[1:2, :] - epsilon * row_total)).reshape(BLK)
    target[...] = (0.5 * (own[3:4, :] - epsilon * col_total)).reshape(BLK)


def wide_of(mass, half):
    line = mass[:, 128 * half : 128 * (half + 1)]
    return jnp.concatenate([line, line], 1)


def along(step):
    index = [(z % 2) * 2 + z // 2 for z in range(SIDE)]
    return [(index[z], index[(z + step) % SIDE]) for z in range(SIDE)]


def local(source_pts, target_pts, source_pot, target_pot, source_logw, target_logw):
    nrow, ncol = lax.axis_size(GROUP), lax.axis_size(PLANE)
    lines = [v.reshape(2, 128) for v in (source_pot, target_pot, source_logw, target_logw)]
    rows, copies = call(
        pack_kernel,
        (f32(TALL, 128), f32(ncol, TALL, 128)),
        6,
        scratch=[
            pltpu.VMEM((TALL, 128), jnp.float32),
            pltpu.VMEM((4, 2, 128), jnp.float32),
            pltpu.SemaphoreType.DMA((8,)),
            pltpu.SemaphoreType.DMA((ncol,)),
        ],
        specs=(VMEM, HBM),
    )(*(pltpu.with_memory_space_constraint(v, pltpu.HBM) for v in (source_pts, target_pts, *lines)))
    mine = [rows]
    for k in range(1, SIDE):
        mine.append(lax.ppermute(rows, LINE, along(-k)))
    others = lax.ppermute(jnp.stack(mine), CORE, [(0, 1), (1, 0)])
    cols = lax.all_to_all(copies, PLANE, 0, 0, tiled=True)
    size = nrow * ncol * BLK * BLK
    cost = pl.CostEstimate(flops=512 * size, bytes_accessed=4 * 2**20, transcendentals=size)
    xt, stats = call(
        rows_kernel,
        (jax.ShapeDtypeStruct((nrow * BLK, 256), jnp.bfloat16), f32(1, BLK)),
        5,
        cost=pl.CostEstimate(flops=10**6, bytes_accessed=10**6, transcendentals=0),
    )(*mine, others)
    scratch = [
        pltpu.VMEM((nrow * BLK, 128), jnp.float32),
        pltpu.VMEM((8, ncol * BLK), jnp.float32),
        pltpu.VMEM((BLK, 128), jnp.float32),
        pltpu.VMEM((BLK, 128), jnp.float32),
        pltpu.VMEM((1, nrow * BLK), jnp.float32),
    ]
    lines, cross, out, own = call(
        functools.partial(tile_kernel, nrow, ncol),
        (f32(LINES, BLK), f32(LINES, BLK), f32(ncol, 1, BLK), f32(8, BLK)),
        SIDE + 4,
        scratch=scratch,
        cost=cost,
    )(*mine, others, cols, xt, stats)
    crossed = lax.ppermute(cross, CORE, [(0, 1), (1, 0)])
    got = lax.all_to_all(out, PLANE, 0, 0, tiled=True)
    small = pl.CostEstimate(flops=10**5, bytes_accessed=10**5, transcendentals=0)
    parts = list(call(merge_kernel, (f32(SENT, BLK),) * SIDE, 2, cost=small)(lines, crossed))
    for k in range(1, SIDE):
        parts[k] = lax.ppermute(parts[k], LINE, along(k))
    return call(finish_kernel, (f32(BLK), f32(BLK)), 2 + SIDE)(got, own, *parts)


def solution(mesh):
    finer = Mesh(mesh.devices.reshape(2, 2, 2, 4, 4), GRP_MEM)
    return jax.shard_map(
        local,
        mesh=finer,
        in_specs=(P(None, GRP_MEM), P(None, GRP_MEM), P(GRP_MEM), P(GRP_MEM), P(GRP_MEM), P(GRP_MEM)),
        out_specs=(P(GRP_MEM), P(GRP_MEM)),
        check_vma=False,
    )
```

```python
import functools

import jax
import jax.numpy as jnp
from jax import lax
from jax.experimental import pallas as pl
from jax.experimental.pallas import tpu as pltpu
from jax.sharding import Mesh
from jax.sharding import PartitionSpec as P

GRP_MEM = ("grp_0", "grp_1", "mem_0", "mem_1", "mem_2")
GROUP = ("grp_0", "grp_1", "mem_0")
PLANE = ("mem_1", "mem_2")
LINE = ("grp_0", "mem_0")
CORE = "grp_1"
SIDE = 4
LINES = 8
SENT = 8

epsilon = 4.0
LOG2E = 1.4426950408889634
FEAT = 64
BLK = 256
TALL = 136
floor_value = -1e30
LOW = 2.0**-90
HIGH = 2.0**120
NORM = 90.5

VMEM = pl.BlockSpec(memory_space=pltpu.VMEM)


HBM = pl.BlockSpec(memory_space=pltpu.HBM)


def call(kernel, out, ins, scratch=(), cost=None, specs=None):
    return pl.pallas_call(
        kernel,
        out_shape=out,
        in_specs=[HBM if specs else VMEM] * ins,
        out_specs=specs or jax.tree.map(lambda _: VMEM, out),
        scratch_shapes=scratch,
        compiler_params=pltpu.CompilerParams(vmem_limit_bytes=40 * 2**20),
        cost_estimate=cost,
    )


def f32(*shape):
    return jax.ShapeDtypeStruct(shape, jnp.float32)


def pack_kernel(spts, tpts, spot, tpot, slogw, tlogw, rows, copies, cols, lines, sems, out_sems):
    loads = []
    for pts, block in ((tpts, cols), (spts, rows)):
        for half in range(2):
            loads.append((pts.at[:, 128 * half : 128 * (half + 1)], block.at[64 * half : 64 * (half + 1), :]))
    for k, ref in enumerate((slogw, spot, tlogw, tpot)):
        loads.append((ref, lines.at[k]))
    loads = [pltpu.make_async_copy(a, b, sems.at[k]) for k, (a, b) in enumerate(loads)]
    for load in loads:
        load.start()
    for k in range(4, 8):
        loads[k].wait()
    tails = []
    for logw, pot, other in ((lines[0], lines[1], lines[2]), (lines[2], lines[3], lines[0])):
        tails.append(jnp.concatenate((logw + pot / epsilon, logw, pot, other), 0))
    cols[128:136, :] = tails[1]
    loads[0].wait()
    loads[1].wait()
    stores = [pltpu.make_async_copy(cols, copies.at[k], out_sems.at[k]) for k in range(copies.shape[0])]
    for store in stores:
        store.start()
    rows[128:136, :] = tails[0]
    loads[2].wait()
    loads[3].wait()
    for store in stores:
        store.wait()


def wide(block, line):
    return jnp.concatenate([block[line : line + 1, :], block[line + 1 : line + 2, :]], 1)


def unpacked(block):
    pts = jnp.concatenate([block[0:64, :], block[64:128, :]], 1)
    return pts, 0.5 * jnp.sum(pts * pts, 0, keepdims=True), wide(block, 128)


def split(v):
    head = v.astype(jnp.bfloat16).astype(jnp.float32)
    return head, v - head


def bias_lines(bias, first):
    b1, rest = split(bias)
    b2, b3 = split(rest)
    line = lax.broadcasted_iota(jnp.int32, (16, BLK), 0)
    out = jnp.zeros((16, BLK), jnp.float32)
    for k, piece in enumerate((b1, b2, b3)):
        out = jnp.where(line == k + first, piece, out)
    return jnp.where((line >= 3 - first) & (line < 6 - first), 1.0, out)


def blocks_of(refs):
    out = []
    for ref in refs:
        out.extend([ref] if len(ref.shape) == 2 else [ref.at[k] for k in range(ref.shape[0])])
    return out


def rows_kernel(*refs):
    blocks = blocks_of(refs[:-2])
    xt, stats = refs[-2:]
    most = jnp.zeros((1, BLK), jnp.float32)
    for k, block in enumerate(blocks):
        pts, sq, term = unpacked(block)
        most = jnp.maximum(most, sq)
        x1, x2 = split(pts * (LOG2E / epsilon))
        bias = bias_lines((term - sq / epsilon) * LOG2E, 0)
        left = jnp.concatenate([x1, x2], 0)
        right = jnp.concatenate([x1, bias, jnp.zeros((48, BLK), jnp.float32)], 0)
        xt[k * BLK : (k + 1) * BLK, :128] = left.T.astype(jnp.bfloat16)
        xt[k * BLK : (k + 1) * BLK, 128:] = right.T.astype(jnp.bfloat16)
    stats[...] = most


def outside(v, low, high):
    return jnp.where((v > low) & (v < high), 0.0, 1.0)


def tile_kernel(nrow, ncol, *refs):
    blocks = blocks_of(refs[: SIDE + 1])
    cols, xt, stats, lines, cross, out, own, rowacc, colacc, rmax, rsum, rlog = refs[SIDE + 1 :]
    most = jnp.zeros((1, BLK), jnp.float32)
    masses = jnp.zeros((8, 128), jnp.float32)
    step = 2048

    for j in range(ncol):
        at = slice(j * BLK, (j + 1) * BLK)
        block = cols.at[j]
        pts, sq, term = unpacked(block)
        y1, y2 = split(pts)
        bias = bias_lines((term - sq / epsilon) * LOG2E, 3).astype(jnp.bfloat16)
        y1 = y1.astype(jnp.bfloat16)
        right = jnp.concatenate([y1, y1, y2.astype(jnp.bfloat16), bias, jnp.zeros((48, BLK), jnp.bfloat16)], 0)
        most = jnp.maximum(most, sq)
        masses = masses + jnp.exp(block[128:136, :])
        total = jnp.zeros((8, BLK), jnp.float32)
        for i in range(nrow * BLK // step):
            rows = slice(i * step, (i + 1) * step)
            e = jnp.exp2(jnp.dot(xt[rows, :], right, preferred_element_type=jnp.float32))
            part = e[:, :128] + e[:, 128:]
            rowacc[rows, :] = part if j == 0 else rowacc[rows, :] + part
            total += jnp.sum(e.reshape(step // 8, 8, BLK), 0)
        colacc[:, at] = total

    s1, s2 = split(rowacc[...])
    parts = jnp.concatenate([s1, s2], 1).astype(jnp.bfloat16)
    rows = lax.dot_general(
        jnp.ones((16, 256), jnp.bfloat16), parts, (((1,), (1,)), ((), ())), preferred_element_type=jnp.float32
    )[:1]
    sums = jnp.sum(colacc[...], 0, keepdims=True)
    ill = outside(stats[...], floor_value, NORM) + outside(most, floor_value, NORM)
    for j in range(nrow):
        ill = ill + outside(rows[:, j * BLK : (j + 1) * BLK], LOW, HIGH)
    for j in range(ncol):
        ill = ill + outside(sums[:, j * BLK : (j + 1) * BLK], LOW, HIGH)
    fast = jnp.max(ill) < 0.5
    rlog[...] = jnp.log(rows)
    colacc[0:1, :] = jnp.log(sums)

    @pl.when(jnp.logical_not(fast))
    def _():
        colacc[0:1, :] = jnp.full((1, ncol * BLK), floor_value, jnp.float32)
        colacc[1:2, :] = jnp.zeros((1, ncol * BLK), jnp.float32)
        for k, block in enumerate(blocks):
            flat, _, term = unpacked(block)
            pts_t = flat.T
            sq_t = 0.5 * jnp.sum(pts_t * pts_t, 1, keepdims=True)
            term_t = jnp.broadcast_to(term, (128, BLK)).T[:, :1]
            rmax[...] = jnp.full(rmax.shape, floor_value, jnp.float32)
            rsum[...] = jnp.zeros_like(rsum)

            def exact(j, _):
                at = pl.ds(pl.multiple_of(j * BLK, BLK), BLK)
                pts, sq, col_term = unpacked(cols.at[j])
                cross = jnp.dot(
                    pts_t, pts, precision=lax.Precision.HIGHEST, preferred_element_type=jnp.float32
                )
                half = (sq_t + sq - cross) / epsilon
                scores = col_term - half
                old = rmax[...]
                new = jnp.maximum(old, jnp.max(scores, 1, keepdims=True))
                part = jnp.sum(jnp.exp(scores - new[:, :1]), 1, keepdims=True)
                rsum[...] = rsum[...] * jnp.exp(old - new) + part
                rmax[...] = new
                others = term_t - half
                old = colacc[0:1, at]
                new = jnp.maximum(old, jnp.max(others, 0, keepdims=True))
                part = jnp.sum(jnp.exp(others - new), 0, keepdims=True)
                colacc[1:2, at] = colacc[1:2, at] * jnp.exp(old - new) + part
                colacc[0:1, at] = new
                return 0

            lax.fori_loop(0, ncol, exact, 0)
            total = (rmax[...] + jnp.log(rsum[...])).T[:1]
            rlog[:, k * BLK : (k + 1) * BLK] = total + term

        def finish(j, _):
            at = pl.ds(pl.multiple_of(j * BLK, BLK), BLK)
            colacc[0:1, at] = colacc[0:1, at] + jnp.log(colacc[1:2, at]) + wide(cols.at[j], 128)
            return 0

        lax.fori_loop(0, ncol, finish, 0)

    target_mass = jnp.sum(masses[2:4, :], keepdims=True)
    source_mass = jnp.sum(masses[6:8, :], keepdims=True)
    mass = jnp.concatenate(
        [jnp.broadcast_to(source_mass, (1, 128)), jnp.broadcast_to(target_mass, (1, 128))], 1
    )
    for to, base in ((lines, 0), (cross, SIDE)):
        for k in range(SIDE):
            to[k : k + 1, :] = rlog[:, (base + k) * BLK : (base + k + 1) * BLK]
        to[4:5, :] = mass
    for j in range(ncol):
        out[j] = colacc[0:1, j * BLK : (j + 1) * BLK]
    at_plane = lax.axis_index("mem_1") * SIDE + lax.axis_index("mem_2")
    own[0:1, :] = wide(blocks[0], 128)
    own[1:2, :] = wide(blocks[0], 132)
    own[2:3, :] = wide(cols.at[at_plane], 128)
    own[3:4, :] = wide(cols.at[at_plane], 132)


def both_logs(a, b):
    peak = jnp.maximum(a, b)
    return peak + jnp.log(jnp.exp(a - peak) + jnp.exp(b - peak))


def merge_kernel(mine, other, *outs):
    logs = both_logs(mine[0:4, :], other[0:4, :])
    mass = mine[4:5, :] + other[4:5, :]
    for k, out in enumerate(outs):
        out[0:1, :] = logs[k : k + 1, :]
        out[1:2, :] = mass


def finish_kernel(got, own, *refs):
    lines, (source, target) = refs[:-2], refs[-2:]

    def total(logs):
        peak = jnp.max(logs, 0, keepdims=True)
        return peak + jnp.log(jnp.sum(jnp.exp(logs - peak), 0, keepdims=True))

    mass = jnp.log(sum(line[1:2, :] for line in lines))
    row_total = total(jnp.concatenate([line[0:1, :] for line in lines], 0)) - own[0:1, :] - wide_of(mass, 1)
    col_total = total(jnp.concatenate([got[j] for j in range(got.shape[0])], 0)) - own[2:3, :] - wide_of(mass, 0)
    source[...] = (0.5 * (own[1:2, :] - epsilon * row_total)).reshape(BLK)
    target[...] = (0.5 * (own[3:4, :] - epsilon * col_total)).reshape(BLK)


def wide_of(mass, half):
    line = mass[:, 128 * half : 128 * (half + 1)]
    return jnp.concatenate([line, line], 1)


def along(step):
    index = [(z % 2) * 2 + z // 2 for z in range(SIDE)]
    return [(index[z], index[(z + step) % SIDE]) for z in range(SIDE)]


def local(source_pts, target_pts, source_pot, target_pot, source_logw, target_logw):
    nrow, ncol = lax.axis_size(GROUP), lax.axis_size(PLANE)
    lines = [v.reshape(2, 128) for v in (source_pot, target_pot, source_logw, target_logw)]
    rows, copies = call(
        pack_kernel,
        (f32(TALL, 128), f32(ncol, TALL, 128)),
        6,
        scratch=[
            pltpu.VMEM((TALL, 128), jnp.float32),
            pltpu.VMEM((4, 2, 128), jnp.float32),
            pltpu.SemaphoreType.DMA((8,)),
            pltpu.SemaphoreType.DMA((ncol,)),
        ],
        specs=(VMEM, HBM),
    )(*(pltpu.with_memory_space_constraint(v, pltpu.HBM) for v in (source_pts, target_pts, *lines)))
    mine = [rows]
    for k in range(1, SIDE):
        mine.append(lax.ppermute(rows, LINE, along(-k)))
    others = lax.ppermute(jnp.stack(mine), CORE, [(0, 1), (1, 0)])
    cols = lax.all_to_all(copies, PLANE, 0, 0, tiled=True)
    size = nrow * ncol * BLK * BLK
    cost = pl.CostEstimate(flops=512 * size, bytes_accessed=4 * 2**20, transcendentals=size)
    xt, stats = call(
        rows_kernel,
        (jax.ShapeDtypeStruct((nrow * BLK, 256), jnp.bfloat16), f32(1, BLK)),
        5,
        cost=pl.CostEstimate(flops=10**6, bytes_accessed=10**6, transcendentals=0),
    )(*mine, others)
    scratch = [
        pltpu.VMEM((nrow * BLK, 128), jnp.float32),
        pltpu.VMEM((8, ncol * BLK), jnp.float32),
        pltpu.VMEM((BLK, 128), jnp.float32),
        pltpu.VMEM((BLK, 128), jnp.float32),
        pltpu.VMEM((1, nrow * BLK), jnp.float32),
    ]
    lines, cross, out, own = call(
        functools.partial(tile_kernel, nrow, ncol),
        (f32(LINES, BLK), f32(LINES, BLK), f32(ncol, 1, BLK), f32(8, BLK)),
        SIDE + 4,
        scratch=scratch,
        cost=cost,
    )(*mine, others, cols, xt, stats)
    crossed = lax.ppermute(cross, CORE, [(0, 1), (1, 0)])
    got = lax.all_to_all(out, PLANE, 0, 0, tiled=True)
    small = pl.CostEstimate(flops=10**5, bytes_accessed=10**5, transcendentals=0)
    parts = list(call(merge_kernel, (f32(SENT, BLK),) * SIDE, 2, cost=small)(lines, crossed))
    for k in (2, 1, 3):
        parts[k] = lax.ppermute(parts[k], LINE, along(k))
    return call(finish_kernel, (f32(BLK), f32(BLK)), 2 + SIDE)(got, own, *parts)


def solution(mesh):
    finer = Mesh(mesh.devices.reshape(2, 2, 2, 4, 4), GRP_MEM)
    return jax.shard_map(
        local,
        mesh=finer,
        in_specs=(P(None, GRP_MEM), P(None, GRP_MEM), P(GRP_MEM), P(GRP_MEM), P(GRP_MEM), P(GRP_MEM)),
        out_specs=(P(GRP_MEM), P(GRP_MEM)),
        check_vma=False,
    )
```

```python
import functools

import jax
import jax.numpy as jnp
from jax import lax
from jax.experimental import pallas as pl
from jax.experimental.pallas import tpu as pltpu
from jax.sharding import Mesh
from jax.sharding import PartitionSpec as P

GRP_MEM = ("grp_0", "grp_1", "mem_0", "mem_1", "mem_2")
GROUP = ("grp_0", "grp_1", "mem_0")
PLANE = ("mem_1", "mem_2")
LINE = ("grp_0", "mem_0")
CORE = "grp_1"
SIDE = 4
LINES = 8
SENT = 8

epsilon = 4.0
LOG2E = 1.4426950408889634
FEAT = 64
BLK = 256
TALL = 136
floor_value = -1e30
LOW = 2.0**-90
HIGH = 2.0**120
NORM = 90.5

VMEM = pl.BlockSpec(memory_space=pltpu.VMEM)


HBM = pl.BlockSpec(memory_space=pltpu.HBM)


def call(kernel, out, ins, scratch=(), cost=None, specs=None):
    return pl.pallas_call(
        kernel,
        out_shape=out,
        in_specs=[HBM if specs else VMEM] * ins,
        out_specs=specs or jax.tree.map(lambda _: VMEM, out),
        scratch_shapes=scratch,
        compiler_params=pltpu.CompilerParams(vmem_limit_bytes=40 * 2**20),
        cost_estimate=cost,
    )


def f32(*shape):
    return jax.ShapeDtypeStruct(shape, jnp.float32)


def pack_kernel(spts, tpts, spot, tpot, slogw, tlogw, rows, copies, cols, lines, sems, out_sems):
    loads = []
    for pts, block in ((tpts, cols), (spts, rows)):
        for half in range(2):
            loads.append((pts.at[:, 128 * half : 128 * (half + 1)], block.at[64 * half : 64 * (half + 1), :]))
    for k, ref in enumerate((slogw, spot, tlogw, tpot)):
        loads.append((ref, lines.at[k]))
    loads = [pltpu.make_async_copy(a, b, sems.at[k]) for k, (a, b) in enumerate(loads)]
    for load in loads:
        load.start()
    for k in range(4, 8):
        loads[k].wait()
    tails = []
    for logw, pot, other in ((lines[0], lines[1], lines[2]), (lines[2], lines[3], lines[0])):
        tails.append(jnp.concatenate((logw + pot / epsilon, logw, pot, other), 0))
    cols[128:136, :] = tails[1]
    loads[0].wait()
    loads[1].wait()
    stores = [pltpu.make_async_copy(cols, copies.at[k], out_sems.at[k]) for k in range(copies.shape[0])]
    for store in stores:
        store.start()
    rows[128:136, :] = tails[0]
    loads[2].wait()
    loads[3].wait()
    for store in stores:
        store.wait()


def wide(block, line):
    return jnp.concatenate([block[line : line + 1, :], block[line + 1 : line + 2, :]], 1)


def unpacked(block):
    pts = jnp.concatenate([block[0:64, :], block[64:128, :]], 1)
    return pts, 0.5 * jnp.sum(pts * pts, 0, keepdims=True), wide(block, 128)


def split(v):
    head = v.astype(jnp.bfloat16).astype(jnp.float32)
    return head, v - head


def bias_lines(bias, first):
    b1, rest = split(bias)
    b2, b3 = split(rest)
    line = lax.broadcasted_iota(jnp.int32, (16, BLK), 0)
    out = jnp.zeros((16, BLK), jnp.float32)
    for k, piece in enumerate((b1, b2, b3)):
        out = jnp.where(line == k + first, piece, out)
    return jnp.where((line >= 3 - first) & (line < 6 - first), 1.0, out)


def blocks_of(refs):
    out = []
    for ref in refs:
        out.extend([ref] if len(ref.shape) == 2 else [ref.at[k] for k in range(ref.shape[0])])
    return out


def rows_kernel(*refs):
    blocks = blocks_of(refs[:-2])
    xt, stats = refs[-2:]
    most = jnp.zeros((1, BLK), jnp.float32)
    for k, block in enumerate(blocks):
        pts, sq, term = unpacked(block)
        most = jnp.maximum(most, sq)
        x1, x2 = split(pts * (LOG2E / epsilon))
        bias = bias_lines((term - sq / epsilon) * LOG2E, 0)
        left = jnp.concatenate([x1, x2], 0)
        right = jnp.concatenate([x1, bias, jnp.zeros((48, BLK), jnp.float32)], 0)
        xt[k * BLK : (k + 1) * BLK, :128] = left.T.astype(jnp.bfloat16)
        xt[k * BLK : (k + 1) * BLK, 128:] = right.T.astype(jnp.bfloat16)
    stats[...] = most


def outside(v, low, high):
    return jnp.where((v > low) & (v < high), 0.0, 1.0)


def tile_kernel(nrow, ncol, *refs):
    blocks = blocks_of(refs[: SIDE + 1])
    cols, xt, stats, lines, cross, out, own, rowacc, colacc, rmax, rsum, rlog = refs[SIDE + 1 :]
    most = jnp.zeros((1, BLK), jnp.float32)
    masses = jnp.zeros((8, 128), jnp.float32)
    step = 2048

    for j in range(ncol):
        at = slice(j * BLK, (j + 1) * BLK)
        block = cols.at[j]
        pts, sq, term = unpacked(block)
        y1, y2 = split(pts)
        bias = bias_lines((term - sq / epsilon) * LOG2E, 3).astype(jnp.bfloat16)
        y1 = y1.astype(jnp.bfloat16)
        right = jnp.concatenate([y1, y1, y2.astype(jnp.bfloat16), bias, jnp.zeros((48, BLK), jnp.bfloat16)], 0)
        most = jnp.maximum(most, sq)
        masses = masses + jnp.exp(block[128:136, :])
        total = jnp.zeros((8, BLK), jnp.float32)
        for i in range(nrow * BLK // step):
            rows = slice(i * step, (i + 1) * step)
            e = jnp.exp2(jnp.dot(xt[rows, :], right, preferred_element_type=jnp.float32))
            part = e[:, :128] + e[:, 128:]
            rowacc[rows, :] = part if j == 0 else rowacc[rows, :] + part
            total += jnp.sum(e.reshape(step // 8, 8, BLK), 0)
        colacc[:, at] = total

    s1, s2 = split(rowacc[...])
    parts = jnp.concatenate([s1, s2], 1).astype(jnp.bfloat16)
    rows = lax.dot_general(
        jnp.ones((16, 256), jnp.bfloat16), parts, (((1,), (1,)), ((), ())), preferred_element_type=jnp.float32
    )[:1]
    sums = jnp.sum(colacc[...], 0, keepdims=True)
    ill = outside(stats[...], floor_value, NORM) + outside(most, floor_value, NORM)
    for j in range(nrow):
        ill = ill + outside(rows[:, j * BLK : (j + 1) * BLK], LOW, HIGH)
    for j in range(ncol):
        ill = ill + outside(sums[:, j * BLK : (j + 1) * BLK], LOW, HIGH)
    fast = jnp.max(ill) < 0.5
    rlog[...] = jnp.log(rows)
    colacc[0:1, :] = jnp.log(sums)

    @pl.when(jnp.logical_not(fast))
    def _():
        colacc[0:1, :] = jnp.full((1, ncol * BLK), floor_value, jnp.float32)
        colacc[1:2, :] = jnp.zeros((1, ncol * BLK), jnp.float32)
        for k, block in enumerate(blocks):
            flat, _, term = unpacked(block)
            pts_t = flat.T
            sq_t = 0.5 * jnp.sum(pts_t * pts_t, 1, keepdims=True)
            term_t = jnp.broadcast_to(term, (128, BLK)).T[:, :1]
            rmax[...] = jnp.full(rmax.shape, floor_value, jnp.float32)
            rsum[...] = jnp.zeros_like(rsum)

            def exact(j, _):
                at = pl.ds(pl.multiple_of(j * BLK, BLK), BLK)
                pts, sq, col_term = unpacked(cols.at[j])
                cross = jnp.dot(
                    pts_t, pts, precision=lax.Precision.HIGHEST, preferred_element_type=jnp.float32
                )
                half = (sq_t + sq - cross) / epsilon
                scores = col_term - half
                old = rmax[...]
                new = jnp.maximum(old, jnp.max(scores, 1, keepdims=True))
                part = jnp.sum(jnp.exp(scores - new[:, :1]), 1, keepdims=True)
                rsum[...] = rsum[...] * jnp.exp(old - new) + part
                rmax[...] = new
                others = term_t - half
                old = colacc[0:1, at]
                new = jnp.maximum(old, jnp.max(others, 0, keepdims=True))
                part = jnp.sum(jnp.exp(others - new), 0, keepdims=True)
                colacc[1:2, at] = colacc[1:2, at] * jnp.exp(old - new) + part
                colacc[0:1, at] = new
                return 0

            lax.fori_loop(0, ncol, exact, 0)
            total = (rmax[...] + jnp.log(rsum[...])).T[:1]
            rlog[:, k * BLK : (k + 1) * BLK] = total + term

        def finish(j, _):
            at = pl.ds(pl.multiple_of(j * BLK, BLK), BLK)
            colacc[0:1, at] = colacc[0:1, at] + jnp.log(colacc[1:2, at]) + wide(cols.at[j], 128)
            return 0

        lax.fori_loop(0, ncol, finish, 0)

    target_mass = jnp.sum(masses[2:4, :], keepdims=True)
    source_mass = jnp.sum(masses[6:8, :], keepdims=True)
    mass = jnp.concatenate(
        [jnp.broadcast_to(source_mass, (1, 128)), jnp.broadcast_to(target_mass, (1, 128))], 1
    )
    for to, base in ((lines, 0), (cross, SIDE)):
        for k in range(SIDE):
            to[k : k + 1, :] = rlog[:, (base + k) * BLK : (base + k + 1) * BLK]
        to[4:5, :] = mass
    for j in range(ncol):
        out[j] = colacc[0:1, j * BLK : (j + 1) * BLK]
    at_plane = lax.axis_index("mem_1") * SIDE + lax.axis_index("mem_2")
    own[0:1, :] = wide(blocks[0], 128)
    own[1:2, :] = wide(blocks[0], 132)
    own[2:3, :] = wide(cols.at[at_plane], 128)
    own[3:4, :] = wide(cols.at[at_plane], 132)


def both_logs(a, b):
    peak = jnp.maximum(a, b)
    return peak + jnp.log(jnp.exp(a - peak) + jnp.exp(b - peak))


def merge_kernel(mine, other, *outs):
    logs = both_logs(mine[0:4, :], other[0:4, :])
    mass = mine[4:5, :] + other[4:5, :]
    for k, out in enumerate(outs):
        out[0:1, :] = logs[k : k + 1, :]
        out[1:2, :] = mass


def finish_kernel(got, own, *refs):
    lines, (source, target) = refs[:-2], refs[-2:]

    def total(logs):
        peak = jnp.max(logs, 0, keepdims=True)
        return peak + jnp.log(jnp.sum(jnp.exp(logs - peak), 0, keepdims=True))

    mass = jnp.log(sum(line[1:2, :] for line in lines))
    row_total = total(jnp.concatenate([line[0:1, :] for line in lines], 0)) - own[0:1, :] - wide_of(mass, 1)
    col_total = total(jnp.concatenate([got[j] for j in range(got.shape[0])], 0)) - own[2:3, :] - wide_of(mass, 0)
    source[...] = (0.5 * (own[1:2, :] - epsilon * row_total)).reshape(BLK)
    target[...] = (0.5 * (own[3:4, :] - epsilon * col_total)).reshape(BLK)


def wide_of(mass, half):
    line = mass[:, 128 * half : 128 * (half + 1)]
    return jnp.concatenate([line, line], 1)


def along(step):
    index = [(z % 2) * 2 + z // 2 for z in range(SIDE)]
    return [(index[z], index[(z + step) % SIDE]) for z in range(SIDE)]


def local(source_pts, target_pts, source_pot, target_pot, source_logw, target_logw):
    nrow, ncol = lax.axis_size(GROUP), lax.axis_size(PLANE)
    lines = [v.reshape(2, 128) for v in (source_pot, target_pot, source_logw, target_logw)]
    rows, copies = call(
        pack_kernel,
        (f32(TALL, 128), f32(ncol, TALL, 128)),
        6,
        scratch=[
            pltpu.VMEM((TALL, 128), jnp.float32),
            pltpu.VMEM((4, 2, 128), jnp.float32),
            pltpu.SemaphoreType.DMA((8,)),
            pltpu.SemaphoreType.DMA((ncol,)),
        ],
        specs=(VMEM, HBM),
    )(*(pltpu.with_memory_space_constraint(v, pltpu.HBM) for v in (source_pts, target_pts, *lines)))
    mine = [rows]
    for k in range(1, SIDE):
        mine.append(lax.ppermute(rows, LINE, along(-k)))
    others = lax.ppermute(jnp.stack(mine), CORE, [(0, 1), (1, 0)])
    cols = lax.all_to_all(copies, PLANE, 0, 0, tiled=True)
    size = nrow * ncol * BLK * BLK
    cost = pl.CostEstimate(flops=512 * size, bytes_accessed=4 * 2**20, transcendentals=size)
    xt, stats = call(
        rows_kernel,
        (jax.ShapeDtypeStruct((nrow * BLK, 256), jnp.bfloat16), f32(1, BLK)),
        5,
        cost=pl.CostEstimate(flops=10**6, bytes_accessed=10**6, transcendentals=0),
    )(*mine, others)
    scratch = [
        pltpu.VMEM((nrow * BLK, 128), jnp.float32),
        pltpu.VMEM((8, ncol * BLK), jnp.float32),
        pltpu.VMEM((BLK, 128), jnp.float32),
        pltpu.VMEM((BLK, 128), jnp.float32),
        pltpu.VMEM((1, nrow * BLK), jnp.float32),
    ]
    lines, cross, out, own = call(
        functools.partial(tile_kernel, nrow, ncol),
        (f32(LINES, BLK), f32(LINES, BLK), f32(ncol, 1, BLK), f32(8, BLK)),
        SIDE + 4,
        scratch=scratch,
        cost=cost,
    )(*mine, others, cols, xt, stats)
    crossed = lax.ppermute(cross, CORE, [(0, 1), (1, 0)])
    got = lax.all_to_all(out, PLANE, 0, 0, tiled=True)
    small = pl.CostEstimate(flops=10**5, bytes_accessed=10**5, transcendentals=0)
    parts = list(call(merge_kernel, (f32(SENT, BLK),) * SIDE, 2, cost=small)(lines, crossed))
    for k in (1, 3, 2):
        parts[k] = lax.ppermute(parts[k], LINE, along(k))
    return call(finish_kernel, (f32(BLK), f32(BLK)), 2 + SIDE)(got, own, *parts)


def solution(mesh):
    finer = Mesh(mesh.devices.reshape(2, 2, 2, 4, 4), GRP_MEM)
    return jax.shard_map(
        local,
        mesh=finer,
        in_specs=(P(None, GRP_MEM), P(None, GRP_MEM), P(GRP_MEM), P(GRP_MEM), P(GRP_MEM), P(GRP_MEM)),
        out_specs=(P(GRP_MEM), P(GRP_MEM)),
        check_vma=False,
    )
```
